32 devices in a mesh: seq: 8 (over y, x, core), slot: 4 (over z).
Axes of the slice: x: 2, y: 2, z: 4, core: 2. Of those that a mesh axis runs over, the one named last changes fastest.
Arguments:
- tokens: bfloat16 [8, 1024, 768], P('slot', 'seq'), may hold values from -6 to 6
- qkv_weight: bfloat16 [768, 2304], P(('seq', 'slot')), may hold values from -0.21875 to 0.21875
- query_bias: bfloat16 [768], P(('seq', 'slot')), may hold values from -3 to 3
- value_bias: bfloat16 [768], P(('seq', 'slot')), may hold values from -3 to 3
- out_weight: bfloat16 [768, 768], P(('seq', 'slot')), may hold values from -6 to 6
- out_bias: bfloat16 [768], P(('seq', 'slot')), may hold values from -3 to 3
- norm1_gain: bfloat16 [768], P(('seq', 'slot')), may hold values from 0.25 to 1.75
- norm1_shift: bfloat16 [768], P(('seq', 'slot')), may hold values from -2 to 2
- up_weight: bfloat16 [768, 3072], P(('seq', 'slot')), may hold values from -0.21875 to 0.21875
- up_bias: bfloat16 [3072], P(('seq', 'slot')), may hold values from -3 to 3
- down_weight: bfloat16 [3072, 768], P(('seq', 'slot')), may hold values from -0.109375 to 0.109375
- down_bias: bfloat16 [768], P(('seq', 'slot')), may hold values from -3 to 3
- norm2_gain: bfloat16 [768], P(('seq', 'slot')), may hold values from 0.25 to 1.75
- norm2_shift: bfloat16 [768], P(('seq', 'slot')), may hold values from -2 to 2
- slot_lengths: int32 [8], P('slot'), may hold values from 256 to 1024, as said below
- out_cotangent: bfloat16 [8, 1024, 768], P('slot', 'seq'), may hold values from -6 to 6
Outputs:
- layer_out: bfloat16 [8, 1024, 768], P('slot', 'seq')
- tokens_grad: bfloat16 [8, 1024, 768], P('slot', 'seq')
- qkv_weight_grad: float32 [768, 2304], P(('seq', 'slot'))
- query_bias_grad: float32 [768], P(('seq', 'slot'))
- value_bias_grad: float32 [768], P(('seq', 'slot'))
- out_weight_grad: float32 [768, 768], P(('seq', 'slot'))
- out_bias_grad: float32 [768], P(('seq', 'slot'))
- norm1_gain_grad: float32 [768], P(('seq', 'slot'))
- norm1_shift_grad: float32 [768], P(('seq', 'slot'))
- up_weight_grad: float32 [768, 3072], P(('seq', 'slot'))
- up_bias_grad: float32 [3072], P(('seq', 'slot'))
- down_weight_grad: float32 [3072, 768], P(('seq', 'slot'))
- down_bias_grad: float32 [768], P(('seq', 'slot'))
- norm2_gain_grad: float32 [768], P(('seq', 'slot'))
- norm2_shift_grad: float32 [768], P(('seq', 'slot'))
The draws below stay inside these ranges and needn't reach their ends.
Inputs may be any that keep to these rules, and one draw needn't show every extreme that they name: `slot_lengths`: the valid tokens of each slot stand at its start; some slot is full and some holds 256 tokens.
All inputs are finite; a program needn't handle non-finite values.
Results may differ from the reference program's by a relative error of at most 0.015.
Values may be sent and summed in bfloat16 or wider, within the bound.
No kernel may reach another device: no remote copies, remote signals or barrier semaphores. Data moves between devices by JAX's collectives and lax.ppermute only.
A program may use at most 192 MiB of HBM per device.

```python
import jax
import jax.numpy as jnp
from jax import lax

D = 768
HEADS = 12
HEAD_DIM = 64
FF = 3072
SLOT_LEN = 1024
SLOTS = 8


def draw_slot_lengths(key, part):
    shortest = SLOT_LEN // 4
    key_draw, key_order = jax.random.split(jax.random.fold_in(key, 11))
    drawn = jax.random.randint(key_draw, (SLOTS,), shortest, SLOT_LEN + 1)
    order = jax.random.permutation(key_order, SLOTS)
    drawn = drawn.at[order[0]].set(SLOT_LEN)
    drawn = drawn.at[order[1]].set(shortest)
    return drawn.astype(jnp.int32)


def levels(own_key, shape, shards, smallest, largest):
    def one(position, parts):
        steps = jax.random.uniform(jax.random.fold_in(jax.random.fold_in(own_key, 6), position), (parts,), jnp.float32, smallest / len(shards), largest / len(shards))
        return jnp.repeat(jnp.exp(steps), shape[position] // parts).reshape((-1,) + (1,) * (len(shape) - position - 1))

    level = one(*shards[0])
    for cut in shards[1:]:
        level = level * one(*cut)
    return level


def bell_draw(own_key, shape, scale, limit, pieces=(), dtype=jnp.bfloat16):
    level = levels(own_key, shape, pieces, -0.22, 0.18) if pieces else 1.0
    values = jax.random.normal(own_key, shape, jnp.float32) * scale * level
    return jnp.minimum(jnp.maximum(values, -limit), limit).astype(dtype)


def setup_inputs(seed: int = 0) -> dict:
    seeds = jax.random.split(jax.random.key(seed), 17)
    return {
        "tokens": bell_draw(seeds[0], (SLOTS, SLOT_LEN, D), 1.0, 6.0, ((0, 4), (1, 8))),
        "qkv_weight": bell_draw(seeds[1], (D, 3 * D), D ** -0.5, 0.21875, ((0, 32),)),
        "query_bias": bell_draw(seeds[2], (D,), 0.5, 3.0, ((0, 32),)),
        "value_bias": bell_draw(seeds[3], (D,), 0.5, 3.0, ((0, 32),)),
        "out_weight": bell_draw(seeds[4], (D, D), 1.0, 6.0, ((0, 32),)),
        "out_bias": bell_draw(seeds[5], (D,), 0.5, 3.0, ((0, 32),)),
        "norm1_gain": jnp.clip(1.0 + 0.15 * jax.random.normal(seeds[6], (D,), jnp.float32), 0.25, 1.75).astype(jnp.bfloat16),
        "norm1_shift": bell_draw(seeds[7], (D,), 0.3, 2.0, ((0, 32),)),
        "up_weight": bell_draw(seeds[8], (D, FF), D ** -0.5, 0.21875, ((0, 32),)),
        "up_bias": bell_draw(seeds[9], (FF,), 0.5, 3.0, ((0, 32),)),
        "down_weight": bell_draw(seeds[10], (FF, D), FF ** -0.5, 0.109375, ((0, 32),)),
        "down_bias": bell_draw(seeds[11], (D,), 0.5, 3.0, ((0, 32),)),
        "norm2_gain": jnp.clip(1.0 + 0.15 * jax.random.normal(seeds[12], (D,), jnp.float32), 0.25, 1.75).astype(jnp.bfloat16),
        "norm2_shift": bell_draw(seeds[13], (D,), 0.3, 2.0, ((0, 32),)),
        "slot_lengths": draw_slot_lengths(jax.random.fold_in(seeds[16], 71), 0),
        "out_cotangent": bell_draw(seeds[15], (SLOTS, SLOT_LEN, D), 1.0, 6.0, ((0, 4), (1, 8))),
    }


NEG_FILL = -1e+30
EPSILON = 1e-05
HIGHEST = lax.Precision.HIGHEST

@jax.custom_vjp
def low(v):
    return lax.optimization_barrier(v.astype(jnp.bfloat16)).astype(jnp.float32)

@jax.custom_vjp
def low_back(v):
    return v

def low_keep(v):
    return (low(v), None)

def low_pass(kept, grad):
    return (grad,)

def back_keep(v):
    return (v, None)

def back_low(kept, grad):
    return (low(grad),)
low.defvjp(low_keep, low_pass)
low_back.defvjp(back_keep, back_low)

def norm_rows(resid, gain, shift):
    centre = resid - lax.optimization_barrier(jnp.mean(resid, -1, keepdims=True))
    spread = lax.optimization_barrier(jnp.mean(centre * centre, -1, keepdims=True))
    return centre * lax.rsqrt(spread + EPSILON) * gain + shift

def matmul(left, right):
    return jnp.dot(left, right, precision=HIGHEST)

def slot_attention(operands):
    queries, key_rows, value_rows, length = operands
    seq_span = queries.shape[0]
    block_size = min(512, seq_span)
    live_keys = jnp.arange(seq_span) < length

    @jax.checkpoint
    def one_block(query_block):
        scores = low_back(jnp.einsum('qhd,khd->hqk', query_block, key_rows, precision=HIGHEST))
        scores = jnp.where(live_keys[None, None, :], scores, NEG_FILL)
        running_max = lax.optimization_barrier(jnp.max(scores, -1, keepdims=True))
        exponent = jnp.exp(scores - running_max)
        softmax_rows = exponent / lax.optimization_barrier(jnp.sum(exponent, -1, keepdims=True))
        return jnp.einsum('hqk,khd->qhd', low(softmax_rows), value_rows, precision=HIGHEST)
    query_blocks = queries.reshape(seq_span // block_size, block_size, queries.shape[1], queries.shape[2])
    return lax.map(one_block, query_blocks).reshape(queries.shape)

def reference(tokens, qkv_weight, query_bias, value_bias, out_weight, out_bias, norm1_gain, norm1_shift, up_weight, up_bias, down_weight, down_bias, norm2_gain, norm2_shift, slot_lengths, out_cotangent):

    def forward(tokens_full, qkv_matrix, query_shift, value_shift, out_matrix, out_shift, gain_one, shift_one, up_matrix, up_shift, down_matrix, down_shift, gain_two, shift_two):
        flat_rows = tokens_full.reshape(SLOTS * SLOT_LEN, D)
        mixed = matmul(flat_rows, qkv_matrix)
        queries = low_back(low((mixed[:, :D] + query_shift) * 0.125))
        key_rows = low_back(low(mixed[:, D:2 * D]))
        value_rows = low_back(low(mixed[:, 2 * D:] + value_shift))
        shaped = (SLOTS, SLOT_LEN, HEADS, HEAD_DIM)
        context = lax.map(slot_attention, (queries.reshape(shaped), key_rows.reshape(shaped), value_rows.reshape(shaped), slot_lengths))
        context = low_back(low(context.reshape(SLOTS * SLOT_LEN, D)))
        attn_out = low_back(matmul(context, out_matrix) + out_shift)
        hidden_one = norm_rows(flat_rows + attn_out, gain_one, shift_one)
        inner_act = low_back(matmul(low(hidden_one), up_matrix) + up_shift)
        activated = low(jax.nn.gelu(inner_act, approximate=False))
        ffn_out = low_back(matmul(activated, down_matrix) + down_shift)
        return norm_rows(hidden_one + ffn_out, gain_two, shift_two).reshape(SLOTS, SLOT_LEN, D)
    inputs = [array_in.astype(jnp.float32) for array_in in (tokens, qkv_weight, query_bias, value_bias, out_weight, out_bias, norm1_gain, norm1_shift, up_weight, up_bias, down_weight, down_bias, norm2_gain, norm2_shift)]
    layer_rows, backward = jax.vjp(forward, *inputs)
    live_rows = (jnp.arange(SLOT_LEN)[None, :] < slot_lengths[:, None]).astype(jnp.float32)
    grads = backward(out_cotangent.astype(jnp.float32) * live_rows[:, :, None])
    return (layer_rows.astype(jnp.bfloat16), grads[0].astype(jnp.bfloat16), grads[1], grads[2], grads[3], grads[4], grads[5], grads[6], grads[7], grads[8], grads[9], grads[10], grads[11], grads[12], grads[13])
```

```python
import jax
import jax.numpy as jnp
from jax import lax
from jax.sharding import PartitionSpec as P

HEADS = 12


NEG_FILL = -1e30
EPSILON = 1e-05


def norm_rows(resid, gain, shift):
    centre = resid - jnp.mean(resid, -1, keepdims=True)
    spread = jnp.mean(centre * centre, -1, keepdims=True)
    return centre * lax.rsqrt(spread + EPSILON) * gain + shift


def gelu_exact(inner_act):
    return jax.nn.gelu(inner_act, approximate=False)


def contract_rows(left, right):
    return lax.dot_general(
        left, right, (((0,), (0,)), ((), ())), preferred_element_type=jnp.float32
    )


def contract_last(left, right):
    return lax.dot_general(
        left, right, (((1,), (1,)), ((), ())), preferred_element_type=jnp.float32
    )


def split_heads(rows_in, head_count):
    return rows_in.reshape(
        rows_in.shape[0], rows_in.shape[1], head_count, rows_in.shape[2] // head_count
    )


def take_block(whole, position, block_size, axis_dim):
    return lax.dynamic_slice_in_dim(whole, position * block_size, block_size, axis_dim)


def masked_scores(queries, key_rows, key_start, slot_lengths):
    scores = jnp.einsum("sqhd,skhd->shqk", queries, key_rows, preferred_element_type=jnp.float32)
    key_places = key_start + jnp.arange(key_rows.shape[1])
    live_keys = key_places[None, :] < slot_lengths[:, None]
    return jnp.where(live_keys[:, None, None, :], scores, NEG_FILL)


def log_totals(queries, key_all, slot_lengths, block_size, head_count):
    block_count = key_all.shape[1] // block_size
    stat_shape = (queries.shape[0], head_count, queries.shape[1])

    def log_step_fn(carried, position):
        running_max, running_sum = carried
        key_rows = split_heads(take_block(key_all, position, block_size, 1), head_count)
        scores = masked_scores(queries, key_rows, position * block_size, slot_lengths)
        new_max = jnp.maximum(running_max, jnp.max(scores, -1))
        running_sum = running_sum * jnp.exp(running_max - new_max) + jnp.sum(
            jnp.exp(scores - new_max[..., None]), -1
        )
        return ((new_max, running_sum), None)

    start_state = (jnp.full(stat_shape, NEG_FILL, jnp.float32), jnp.zeros(stat_shape, jnp.float32))
    (running_max, running_sum), _ = lax.scan(log_step_fn, start_state, jnp.arange(block_count))
    return running_max + jnp.log(running_sum)


def attend(queries, key_all, value_all, slot_lengths, logsum, block_size, head_count):
    block_count = key_all.shape[1] // block_size

    def attend_step_fn(context, position):
        key_rows = split_heads(take_block(key_all, position, block_size, 1), head_count)
        value_rows = split_heads(take_block(value_all, position, block_size, 1), head_count)
        scores = masked_scores(queries, key_rows, position * block_size, slot_lengths)
        weights_low = jnp.exp(scores - logsum[..., None]).astype(jnp.bfloat16)
        return (
            context
            + jnp.einsum(
                "shqk,skhd->sqhd", weights_low, value_rows, preferred_element_type=jnp.float32
            ),
            None,
        )

    context, _ = lax.scan(
        attend_step_fn, jnp.zeros(queries.shape, jnp.float32), jnp.arange(block_count)
    )
    return context


def prob_grad_totals(
    queries, d_context, key_all, value_all, slot_lengths, logsum, block_size, head_count
):
    block_count = key_all.shape[1] // block_size

    def prob_step_fn(prob_delta, position):
        key_rows = split_heads(take_block(key_all, position, block_size, 1), head_count)
        value_rows = split_heads(take_block(value_all, position, block_size, 1), head_count)
        scores = masked_scores(queries, key_rows, position * block_size, slot_lengths)
        softmax_rows = jnp.exp(scores - logsum[..., None])
        d_probs = jnp.einsum(
            "sqhd,skhd->shqk", d_context, value_rows, preferred_element_type=jnp.float32
        )
        return (prob_delta + jnp.sum(softmax_rows * d_probs, -1), None)

    prob_delta, _ = lax.scan(
        prob_step_fn, jnp.zeros(logsum.shape, jnp.float32), jnp.arange(block_count)
    )
    return prob_delta


def key_side(
    queries, d_context, key_all, value_all, slot_lengths, logsum, prob_delta, block_size, head_count
):
    block_count = key_all.shape[1] // block_size

    def key_step_fn(d_query, position):
        key_rows = split_heads(take_block(key_all, position, block_size, 1), head_count)
        value_rows = split_heads(take_block(value_all, position, block_size, 1), head_count)
        scores = masked_scores(queries, key_rows, position * block_size, slot_lengths)
        softmax_rows = jnp.exp(scores - logsum[..., None])
        d_probs = jnp.einsum(
            "sqhd,skhd->shqk", d_context, value_rows, preferred_element_type=jnp.float32
        )
        d_scores = (softmax_rows * (d_probs - prob_delta[..., None])).astype(jnp.bfloat16)
        d_query = d_query + jnp.einsum(
            "shqk,skhd->sqhd", d_scores, key_rows, preferred_element_type=jnp.float32
        )
        d_key_rows = jnp.einsum(
            "shqk,sqhd->skhd", d_scores, queries, preferred_element_type=jnp.float32
        )
        d_value_rows = jnp.einsum(
            "shqk,sqhd->skhd",
            softmax_rows.astype(jnp.bfloat16),
            d_context,
            preferred_element_type=jnp.float32,
        )
        return (d_query, (d_key_rows, d_value_rows))

    return lax.scan(key_step_fn, jnp.zeros(queries.shape, jnp.float32), jnp.arange(block_count))


ALL_AXES = ("seq", "slot")


def flip_pairs(mask):
    return [((q * 4 + z), ((q ^ mask) * 4 + z)) for q in range(8) for z in range(4)]


def turn_pairs(step):
    return [((q * 4 + z), (q * 4 + (z + step) % 4)) for q in range(8) for z in range(4)]


CORE, X_AXIS, Y_AXIS = 1, 2, 4


def flip(value, mask):
    return lax.ppermute(value, ALL_AXES, flip_pairs(mask))


def turn(value, step):
    return lax.ppermute(value, ALL_AXES, turn_pairs(step))


def places():
    q = lax.axis_index("seq")
    return q & 1, (q >> 1) & 1, q >> 2, lax.axis_index("slot")


def merge(own, other, bit, axis):
    first = jnp.where(bit == 0, own, other)
    second = jnp.where(bit == 0, other, own)
    return jnp.stack([first, second], axis)


def gather_plane(a, b):
    core, x, y, _ = places()
    a1, b1 = merge(a, flip(a, X_AXIS), x, 0), merge(b, flip(b, Y_AXIS), y, 0)
    a2, b2 = merge(a1, flip(a1, Y_AXIS), y, 0), merge(b1, flip(b1, X_AXIS), x, 1)
    return merge(a2, flip(a2, CORE), core, 2), merge(b2, flip(b2, CORE), core, 2)


def gather_all(shard):
    rows, columns = shard.shape
    half = columns // 2
    z = places()[3]
    from_one, from_two, from_three = (turn(shard, step) for step in (1, 2, 3))
    ring = [shard, from_three, from_two, from_one]
    line = lax.dynamic_slice_in_dim(jnp.stack(ring + ring[:3]), (4 - z) % 4, 4, 0)
    a, b = gather_plane(line[..., :half], line[..., half:])
    return jnp.concatenate([a.reshape(32 * rows, half), b.reshape(32 * rows, half)], 1)


def pick(value, index, axis):
    return lax.dynamic_index_in_dim(value, index, axis, keepdims=False)


def add_low(left, right):
    return (left.astype(jnp.float32) + right.astype(jnp.float32)).astype(jnp.bfloat16)


def fold(value, bit, mask, axis):
    return add_low(pick(value, bit, axis), flip(pick(value, 1 - bit, axis), mask))


def scatter_plane(a, b):
    core, x, y, _ = places()
    a, b = fold(a, core, CORE, 2), fold(b, core, CORE, 2)
    a, b = fold(a, y, Y_AXIS, 0), fold(b, x, X_AXIS, 1)
    return fold(a, x, X_AXIS, 0), fold(b, y, Y_AXIS, 0)


def scatter_all(grad):
    rows, columns = grad.shape
    rows, half = rows // 32, columns // 2
    z = places()[3]
    a = grad[:, :half].reshape(2, 2, 2, 4, rows, half)
    b = grad[:, half:].reshape(2, 2, 2, 4, rows, half)
    sums = []
    for part in scatter_plane(a, b):
        total = pick(part, z, 0).astype(jnp.float32)
        for step in (1, 2, 3):
            total = total + turn(pick(part, (z + step) % 4, 0), step).astype(jnp.float32)
        sums.append(total)
    return jnp.concatenate(sums, 1)


def body(
    tokens,
    qkv_weight,
    query_bias,
    value_bias,
    out_weight,
    out_bias,
    norm1_gain,
    norm1_shift,
    up_weight,
    up_bias,
    down_weight,
    down_bias,
    norm2_gain,
    norm2_shift,
    slot_lengths,
    out_cotangent,
):
    slot_count, row_count, model_width = tokens.shape
    head_count = HEADS
    flat_rows = tokens.reshape(slot_count * row_count, model_width)
    attn_set = (
        lax.all_gather(qkv_weight, ("seq", "slot"), axis=0, tiled=True),
        lax.all_gather(out_weight, ("seq", "slot"), axis=0, tiled=True),
        lax.all_gather(query_bias, ("seq", "slot"), axis=0, tiled=True),
        lax.all_gather(value_bias, ("seq", "slot"), axis=0, tiled=True),
        lax.all_gather(out_bias, ("seq", "slot"), axis=0, tiled=True),
        lax.all_gather(norm1_gain, ("seq", "slot"), axis=0, tiled=True),
        lax.all_gather(norm1_shift, ("seq", "slot"), axis=0, tiled=True),
    )
    qkv_full, out_full, query_shift, value_shift, out_shift, gain_one, shift_one = attn_set
    mixed = jnp.dot(flat_rows, qkv_full, preferred_element_type=jnp.float32)
    queries = ((mixed[:, :model_width] + query_shift.astype(jnp.float32)) * 0.125).astype(
        jnp.bfloat16
    )
    queries = split_heads(queries.reshape(slot_count, row_count, model_width), head_count)
    keys_own = (
        mixed[:, model_width : 2 * model_width]
        .astype(jnp.bfloat16)
        .reshape(slot_count, row_count, model_width)
    )
    values_own = (
        (mixed[:, 2 * model_width :] + value_shift.astype(jnp.float32))
        .astype(jnp.bfloat16)
        .reshape(slot_count, row_count, model_width)
    )
    key_all, value_all = (
        lax.all_gather(keys_own, "seq", axis=1, tiled=True),
        lax.all_gather(values_own, "seq", axis=1, tiled=True),
    )
    length_all = key_all.shape[1]
    block_size = min(512, length_all)
    logsum = log_totals(queries, key_all, slot_lengths, block_size, head_count)
    context = attend(
        queries, key_all, value_all, slot_lengths, logsum, block_size, head_count
    ).astype(jnp.bfloat16)
    context_flat = context.reshape(slot_count * row_count, model_width)
    attn_out = jnp.dot(
        context_flat, out_full, preferred_element_type=jnp.float32
    ) + out_shift.astype(jnp.float32)
    resid_one = flat_rows.astype(jnp.float32) + attn_out
    hidden_one = norm_rows(resid_one, gain_one.astype(jnp.float32), shift_one.astype(jnp.float32))
    hidden_low = hidden_one.astype(jnp.bfloat16)
    ffn_set = (
        lax.all_gather(up_weight, ("seq", "slot"), axis=0, tiled=True),
        lax.all_gather(down_weight, ("seq", "slot"), axis=0, tiled=True),
        lax.all_gather(up_bias, ("seq", "slot"), axis=0, tiled=True),
        lax.all_gather(down_bias, ("seq", "slot"), axis=0, tiled=True),
        lax.all_gather(norm2_gain, ("seq", "slot"), axis=0, tiled=True),
        lax.all_gather(norm2_shift, ("seq", "slot"), axis=0, tiled=True),
    )
    up_full, down_full, up_shift, down_shift, gain_two, shift_two = ffn_set
    inner_act = jnp.dot(hidden_low, up_full, preferred_element_type=jnp.float32) + up_shift.astype(
        jnp.float32
    )
    activated = gelu_exact(inner_act).astype(jnp.bfloat16)
    ffn_out = jnp.dot(activated, down_full, preferred_element_type=jnp.float32) + down_shift.astype(
        jnp.float32
    )
    resid_two = hidden_one + ffn_out
    layer_out = norm_rows(resid_two, gain_two.astype(jnp.float32), shift_two.astype(jnp.float32))
    layer_out = layer_out.astype(jnp.bfloat16).reshape(slot_count, row_count, model_width)
    qkv_back, out_back, _, _, _, gain_one_back, shift_one_back = (
        lax.all_gather(qkv_weight, ("seq", "slot"), axis=0, tiled=True),
        lax.all_gather(out_weight, ("seq", "slot"), axis=0, tiled=True),
        lax.all_gather(query_bias, ("seq", "slot"), axis=0, tiled=True),
        lax.all_gather(value_bias, ("seq", "slot"), axis=0, tiled=True),
        lax.all_gather(out_bias, ("seq", "slot"), axis=0, tiled=True),
        lax.all_gather(norm1_gain, ("seq", "slot"), axis=0, tiled=True),
        lax.all_gather(norm1_shift, ("seq", "slot"), axis=0, tiled=True),
    )
    up_back, down_back, _, _, gain_two_back, shift_two_back = (
        lax.all_gather(up_weight, ("seq", "slot"), axis=0, tiled=True),
        lax.all_gather(down_weight, ("seq", "slot"), axis=0, tiled=True),
        lax.all_gather(up_bias, ("seq", "slot"), axis=0, tiled=True),
        lax.all_gather(down_bias, ("seq", "slot"), axis=0, tiled=True),
        lax.all_gather(norm2_gain, ("seq", "slot"), axis=0, tiled=True),
        lax.all_gather(norm2_shift, ("seq", "slot"), axis=0, tiled=True),
    )
    positions = lax.axis_index("seq") * row_count + jnp.arange(row_count)
    live_rows = (positions[None, :] < slot_lengths[:, None]).astype(jnp.float32)
    cotangent = (out_cotangent.astype(jnp.float32) * live_rows[:, :, None]).reshape(
        slot_count * row_count, model_width
    )
    _, norm_back_two = jax.vjp(
        norm_rows, resid_two, gain_two_back.astype(jnp.float32), shift_two_back.astype(jnp.float32)
    )
    d_resid_two, d_gain_two, d_shift_two = norm_back_two(cotangent)
    d_ffn = d_resid_two.astype(jnp.bfloat16)
    d_down = contract_rows(activated, d_ffn)
    d_down_shift = jnp.sum(d_ffn.astype(jnp.float32), 0)
    d_activated = contract_last(d_ffn, down_back)
    _, gelu_back = jax.vjp(gelu_exact, inner_act)
    d_inner = gelu_back(d_activated)[0].astype(jnp.bfloat16)
    d_up = contract_rows(hidden_low, d_inner)
    d_up_shift = jnp.sum(d_inner.astype(jnp.float32), 0)
    d_hidden = contract_last(d_inner, up_back) + d_resid_two
    _, norm_back_one = jax.vjp(
        norm_rows, resid_one, gain_one_back.astype(jnp.float32), shift_one_back.astype(jnp.float32)
    )
    d_resid_one, d_gain_one, d_shift_one = norm_back_one(d_hidden)
    d_attn = d_resid_one.astype(jnp.bfloat16)
    d_out = contract_rows(context_flat, d_attn)
    d_out_shift = jnp.sum(d_attn.astype(jnp.float32), 0)
    d_context = contract_last(d_attn, out_back).astype(jnp.bfloat16)
    d_context = split_heads(d_context.reshape(slot_count, row_count, model_width), head_count)
    prob_delta = prob_grad_totals(
        queries, d_context, key_all, value_all, slot_lengths, logsum, block_size, head_count
    )
    d_query, key_parts = key_side(
        queries,
        d_context,
        key_all,
        value_all,
        slot_lengths,
        logsum,
        prob_delta,
        block_size,
        head_count,
    )
    d_key_part = jnp.moveaxis(key_parts[0], 0, 1).reshape(slot_count, length_all, model_width)
    d_value_part = jnp.moveaxis(key_parts[1], 0, 1).reshape(slot_count, length_all, model_width)
    d_key_sum, d_value_sum = (
        lax.psum_scatter(
            d_key_part.astype(jnp.bfloat16), "seq", scatter_dimension=1, tiled=True
        ).astype(jnp.float32),
        lax.psum_scatter(
            d_value_part.astype(jnp.bfloat16), "seq", scatter_dimension=1, tiled=True
        ).astype(jnp.float32),
    )
    d_query_pre = d_query.astype(jnp.bfloat16).reshape(
        slot_count * row_count, model_width
    ) * jnp.asarray(0.125, jnp.bfloat16)
    d_key_low = d_key_sum.astype(jnp.bfloat16).reshape(slot_count * row_count, model_width)
    d_value_low = d_value_sum.astype(jnp.bfloat16).reshape(slot_count * row_count, model_width)
    d_mixed = jnp.concatenate([d_query_pre, d_key_low, d_value_low], 1)
    d_qkv = contract_rows(flat_rows, d_mixed)
    d_query_shift = jnp.sum(d_query_pre.astype(jnp.float32), 0)
    d_value_shift = jnp.sum(d_value_low.astype(jnp.float32), 0)
    tokens_grad = (
        (d_resid_one + contract_last(d_mixed, qkv_back))
        .astype(jnp.bfloat16)
        .reshape(slot_count, row_count, model_width)
    )
    attn_sums = (
        lax.psum_scatter(d_qkv, ("seq", "slot"), scatter_dimension=0, tiled=True),
        lax.psum_scatter(d_out, ("seq", "slot"), scatter_dimension=0, tiled=True),
        lax.psum_scatter(d_query_shift, ("seq", "slot"), scatter_dimension=0, tiled=True),
        lax.psum_scatter(d_value_shift, ("seq", "slot"), scatter_dimension=0, tiled=True),
        lax.psum_scatter(d_out_shift, ("seq", "slot"), scatter_dimension=0, tiled=True),
        lax.psum_scatter(d_gain_one, ("seq", "slot"), scatter_dimension=0, tiled=True),
        lax.psum_scatter(d_shift_one, ("seq", "slot"), scatter_dimension=0, tiled=True),
    )
    ffn_sums = (
        lax.psum_scatter(d_up, ("seq", "slot"), scatter_dimension=0, tiled=True),
        lax.psum_scatter(d_down, ("seq", "slot"), scatter_dimension=0, tiled=True),
        lax.psum_scatter(d_up_shift, ("seq", "slot"), scatter_dimension=0, tiled=True),
        lax.psum_scatter(d_down_shift, ("seq", "slot"), scatter_dimension=0, tiled=True),
        lax.psum_scatter(d_gain_two, ("seq", "slot"), scatter_dimension=0, tiled=True),
        lax.psum_scatter(d_shift_two, ("seq", "slot"), scatter_dimension=0, tiled=True),
    )
    return (
        layer_out,
        tokens_grad,
        attn_sums[0],
        attn_sums[2],
        attn_sums[3],
        attn_sums[1],
        attn_sums[4],
        attn_sums[5],
        attn_sums[6],
        ffn_sums[0],
        ffn_sums[2],
        ffn_sums[1],
        ffn_sums[3],
        ffn_sums[4],
        ffn_sums[5],
    )


def body_fast(
    tokens,
    qkv_weight,
    query_bias,
    value_bias,
    out_weight,
    out_bias,
    norm1_gain,
    norm1_shift,
    up_weight,
    up_bias,
    down_weight,
    down_bias,
    norm2_gain,
    norm2_shift,
    slot_lengths,
    out_cotangent,
):
    slot_count, row_count, model_width = tokens.shape
    head_count = HEADS
    part = qkv_weight.shape[0]
    inner_part = up_bias.shape[0]
    flat_rows = tokens.reshape(slot_count * row_count, model_width)
    small = jnp.concatenate(
        [
            query_bias,
            value_bias,
            out_bias,
            norm1_gain,
            norm1_shift,
            down_bias,
            norm2_gain,
            norm2_shift,
            up_bias,
        ]
    )
    small_columns = small.shape[0] // part
    small = jnp.pad(small.reshape(part, small_columns), ((0, 0), (0, 256 - small_columns)))
    attn_full = gather_all(jnp.concatenate([qkv_weight, out_weight, small], 1))
    up_full = gather_all(up_weight)
    down_full = gather_all(down_weight)
    qkv_full = attn_full[:, : 3 * model_width]
    out_full = attn_full[:, 3 * model_width : 4 * model_width]
    small_full = attn_full[:, 4 * model_width : 4 * model_width + small_columns]
    small_full = small_full.reshape(32, part * small_columns).astype(jnp.float32)

    def vector(position):
        return small_full[:, position * part : (position + 1) * part].reshape(model_width)

    query_shift, value_shift, out_shift, gain_one, shift_one, down_shift, gain_two, shift_two = (
        vector(position) for position in range(8)
    )
    up_shift = small_full[:, 8 * part :].reshape(32 * inner_part)
    mixed = jnp.dot(flat_rows, qkv_full, preferred_element_type=jnp.float32)
    queries = ((mixed[:, :model_width] + query_shift) * 0.125).astype(jnp.bfloat16)
    queries = split_heads(queries.reshape(slot_count, row_count, model_width), head_count)
    keys_own = (
        mixed[:, model_width : 2 * model_width]
        .astype(jnp.bfloat16)
        .reshape(slot_count, row_count, model_width)
    )
    values_own = (
        (mixed[:, 2 * model_width :] + value_shift)
        .astype(jnp.bfloat16)
        .reshape(slot_count, row_count, model_width)
    )

    def by_slot(parts):
        whole = parts.reshape(8, slot_count, row_count, model_width)
        return jnp.moveaxis(whole, 0, 1).reshape(slot_count, 8 * row_count, model_width)

    def by_place(whole):
        parts = whole.reshape(slot_count, 8, row_count, model_width)
        return jnp.moveaxis(parts, 1, 0).reshape(2, 2, 2, slot_count, row_count, model_width)

    key_all, value_all = gather_plane(keys_own, values_own)
    key_all, value_all = by_slot(key_all), by_slot(value_all)
    length_all = key_all.shape[1]
    block_size = min(512, length_all)
    logsum = log_totals(queries, key_all, slot_lengths, block_size, head_count)
    context = attend(
        queries, key_all, value_all, slot_lengths, logsum, block_size, head_count
    ).astype(jnp.bfloat16)
    context_flat = context.reshape(slot_count * row_count, model_width)
    attn_out = jnp.dot(context_flat, out_full, preferred_element_type=jnp.float32) + out_shift
    resid_one = flat_rows.astype(jnp.float32) + attn_out
    hidden_one = norm_rows(resid_one, gain_one, shift_one)
    hidden_low = hidden_one.astype(jnp.bfloat16)
    inner_act = jnp.dot(hidden_low, up_full, preferred_element_type=jnp.float32) + up_shift
    activated = gelu_exact(inner_act).astype(jnp.bfloat16)
    ffn_out = jnp.dot(activated, down_full, preferred_element_type=jnp.float32) + down_shift
    resid_two = hidden_one + ffn_out
    layer_out = norm_rows(resid_two, gain_two, shift_two)
    layer_out = layer_out.astype(jnp.bfloat16).reshape(slot_count, row_count, model_width)
    positions = lax.axis_index("seq") * row_count + jnp.arange(row_count)
    live_rows = (positions[None, :] < slot_lengths[:, None]).astype(jnp.float32)
    cotangent = (out_cotangent.astype(jnp.float32) * live_rows[:, :, None]).reshape(
        slot_count * row_count, model_width
    )
    _, norm_back_two = jax.vjp(norm_rows, resid_two, gain_two, shift_two)
    d_resid_two, d_gain_two, d_shift_two = norm_back_two(cotangent)
    d_ffn = d_resid_two.astype(jnp.bfloat16)
    d_down = scatter_all(contract_rows(activated, d_ffn).astype(jnp.bfloat16))
    d_down_shift = jnp.sum(d_ffn.astype(jnp.float32), 0)
    d_activated = contract_last(d_ffn, down_full)
    _, gelu_back = jax.vjp(gelu_exact, inner_act)
    d_inner = gelu_back(d_activated)[0].astype(jnp.bfloat16)
    d_up = scatter_all(contract_rows(hidden_low, d_inner).astype(jnp.bfloat16))
    d_up_shift = jnp.sum(d_inner.astype(jnp.float32), 0)
    d_hidden = contract_last(d_inner, up_full) + d_resid_two
    _, norm_back_one = jax.vjp(norm_rows, resid_one, gain_one, shift_one)
    d_resid_one, d_gain_one, d_shift_one = norm_back_one(d_hidden)
    d_attn = d_resid_one.astype(jnp.bfloat16)
    d_out = scatter_all(contract_rows(context_flat, d_attn).astype(jnp.bfloat16))
    d_out_shift = jnp.sum(d_attn.astype(jnp.float32), 0)
    d_context = contract_last(d_attn, out_full).astype(jnp.bfloat16)
    d_context = split_heads(d_context.reshape(slot_count, row_count, model_width), head_count)
    prob_delta = prob_grad_totals(
        queries, d_context, key_all, value_all, slot_lengths, logsum, block_size, head_count
    )
    d_query, key_parts = key_side(
        queries,
        d_context,
        key_all,
        value_all,
        slot_lengths,
        logsum,
        prob_delta,
        block_size,
        head_count,
    )
    d_key_part = jnp.moveaxis(key_parts[0], 0, 1).reshape(slot_count, length_all, model_width)
    d_value_part = jnp.moveaxis(key_parts[1], 0, 1).reshape(slot_count, length_all, model_width)
    d_key_low, d_value_low = scatter_plane(
        by_place(d_key_part.astype(jnp.bfloat16)), by_place(d_value_part.astype(jnp.bfloat16))
    )
    d_query_pre = d_query.astype(jnp.bfloat16).reshape(
        slot_count * row_count, model_width
    ) * jnp.asarray(0.125, jnp.bfloat16)
    d_key_low = d_key_low.reshape(slot_count * row_count, model_width)
    d_value_low = d_value_low.reshape(slot_count * row_count, model_width)
    d_mixed = jnp.concatenate([d_query_pre, d_key_low, d_value_low], 1)
    d_qkv = contract_rows(flat_rows, d_mixed).astype(jnp.bfloat16)
    d_query_shift = jnp.sum(d_query_pre.astype(jnp.float32), 0)
    d_value_shift = jnp.sum(d_value_low.astype(jnp.float32), 0)
    tokens_grad = (
        (d_resid_one + contract_last(d_mixed, qkv_full))
        .astype(jnp.bfloat16)
        .reshape(slot_count, row_count, model_width)
    )
    small_grads = jnp.concatenate(
        [
            grad.reshape(32, grad.shape[0] // 32)
            for grad in (
                d_query_shift,
                d_value_shift,
                d_out_shift,
                d_gain_one,
                d_shift_one,
                d_down_shift,
                d_gain_two,
                d_shift_two,
                d_up_shift,
            )
        ],
        1,
    ).astype(jnp.bfloat16)
    small_grads = jnp.pad(
        small_grads.reshape(32 * part, small_columns), ((0, 0), (0, 256 - small_columns))
    )
    attn_sums = scatter_all(jnp.concatenate([d_qkv, small_grads], 1))
    own = attn_sums[:, 3 * model_width : 3 * model_width + small_columns].reshape(-1)
    vectors = [own[position * part : (position + 1) * part] for position in range(8)]
    return (
        layer_out,
        tokens_grad,
        attn_sums[:, : 3 * model_width],
        vectors[0],
        vectors[1],
        d_out,
        vectors[2],
        vectors[3],
        vectors[4],
        d_up,
        own[8 * part :],
        d_down,
        vectors[5],
        vectors[6],
        vectors[7],
    )


def solution(mesh):
    fast = mesh.shape["seq"] == 8 and mesh.shape["slot"] == 4
    return jax.shard_map(
        body_fast if fast else body,
        mesh=mesh,
        in_specs=(
            P("slot", "seq", None),
            P(("seq", "slot"), None),
            P(("seq", "slot")),
            P(("seq", "slot")),
            P(("seq", "slot"), None),
            P(("seq", "slot")),
            P(("seq", "slot")),
            P(("seq", "slot")),
            P(("seq", "slot"), None),
            P(("seq", "slot")),
            P(("seq", "slot"), None),
            P(("seq", "slot")),
            P(("seq", "slot")),
            P(("seq", "slot")),
            P("slot"),
            P("slot", "seq", None),
        ),
        out_specs=(
            P("slot", "seq", None),
            P("slot", "seq", None),
            P(("seq", "slot"), None),
            P(("seq", "slot")),
            P(("seq", "slot")),
            P(("seq", "slot"), None),
            P(("seq", "slot")),
            P(("seq", "slot")),
            P(("seq", "slot")),
            P(("seq", "slot"), None),
            P(("seq", "slot")),
            P(("seq", "slot"), None),
            P(("seq", "slot")),
            P(("seq", "slot")),
            P(("seq", "slot")),
        ),
        check_vma=False,
    )
```

```python
import jax
import jax.numpy as jnp
from jax import lax
from jax.experimental import pallas as pl
from jax.experimental.pallas import tpu as pltpu
from jax.sharding import PartitionSpec as P

HEADS = 12


NEG_FILL = -1e30
EPSILON = 1e-05


def norm_rows(resid, gain, shift):
    centre = resid - jnp.mean(resid, -1, keepdims=True)
    spread = jnp.mean(centre * centre, -1, keepdims=True)
    return centre * lax.rsqrt(spread + EPSILON) * gain + shift


def gelu_exact(inner_act):
    return jax.nn.gelu(inner_act, approximate=False)


def contract_rows(left, right):
    return lax.dot_general(
        left, right, (((0,), (0,)), ((), ())), preferred_element_type=jnp.float32
    )


def contract_last(left, right):
    return lax.dot_general(
        left, right, (((1,), (1,)), ((), ())), preferred_element_type=jnp.float32
    )


def split_heads(rows_in, head_count):
    return rows_in.reshape(
        rows_in.shape[0], rows_in.shape[1], head_count, rows_in.shape[2] // head_count
    )


def take_block(whole, position, block_size, axis_dim):
    return lax.dynamic_slice_in_dim(whole, position * block_size, block_size, axis_dim)


def masked_scores(queries, key_rows, key_start, slot_lengths):
    scores = jnp.einsum("sqhd,skhd->shqk", queries, key_rows, preferred_element_type=jnp.float32)
    key_places = key_start + jnp.arange(key_rows.shape[1])
    live_keys = key_places[None, :] < slot_lengths[:, None]
    return jnp.where(live_keys[:, None, None, :], scores, NEG_FILL)


def log_totals(queries, key_all, slot_lengths, block_size, head_count):
    block_count = key_all.shape[1] // block_size
    stat_shape = (queries.shape[0], head_count, queries.shape[1])

    def log_step_fn(carried, position):
        running_max, running_sum = carried
        key_rows = split_heads(take_block(key_all, position, block_size, 1), head_count)
        scores = masked_scores(queries, key_rows, position * block_size, slot_lengths)
        new_max = jnp.maximum(running_max, jnp.max(scores, -1))
        running_sum = running_sum * jnp.exp(running_max - new_max) + jnp.sum(
            jnp.exp(scores - new_max[..., None]), -1
        )
        return ((new_max, running_sum), None)

    start_state = (jnp.full(stat_shape, NEG_FILL, jnp.float32), jnp.zeros(stat_shape, jnp.float32))
    (running_max, running_sum), _ = lax.scan(log_step_fn, start_state, jnp.arange(block_count))
    return running_max + jnp.log(running_sum)


def attend(queries, key_all, value_all, slot_lengths, logsum, block_size, head_count):
    block_count = key_all.shape[1] // block_size

    def attend_step_fn(context, position):
        key_rows = split_heads(take_block(key_all, position, block_size, 1), head_count)
        value_rows = split_heads(take_block(value_all, position, block_size, 1), head_count)
        scores = masked_scores(queries, key_rows, position * block_size, slot_lengths)
        weights_low = jnp.exp(scores - logsum[..., None]).astype(jnp.bfloat16)
        return (
            context
            + jnp.einsum(
                "shqk,skhd->sqhd", weights_low, value_rows, preferred_element_type=jnp.float32
            ),
            None,
        )

    context, _ = lax.scan(
        attend_step_fn, jnp.zeros(queries.shape, jnp.float32), jnp.arange(block_count)
    )
    return context


def prob_grad_totals(
    queries, d_context, key_all, value_all, slot_lengths, logsum, block_size, head_count
):
    block_count = key_all.shape[1] // block_size

    def prob_step_fn(prob_delta, position):
        key_rows = split_heads(take_block(key_all, position, block_size, 1), head_count)
        value_rows = split_heads(take_block(value_all, position, block_size, 1), head_count)
        scores = masked_scores(queries, key_rows, position * block_size, slot_lengths)
        softmax_rows = jnp.exp(scores - logsum[..., None])
        d_probs = jnp.einsum(
            "sqhd,skhd->shqk", d_context, value_rows, preferred_element_type=jnp.float32
        )
        return (prob_delta + jnp.sum(softmax_rows * d_probs, -1), None)

    prob_delta, _ = lax.scan(
        prob_step_fn, jnp.zeros(logsum.shape, jnp.float32), jnp.arange(block_count)
    )
    return prob_delta


def key_side(
    queries, d_context, key_all, value_all, slot_lengths, logsum, prob_delta, block_size, head_count
):
    block_count = key_all.shape[1] // block_size

    def key_step_fn(d_query, position):
        key_rows = split_heads(take_block(key_all, position, block_size, 1), head_count)
        value_rows = split_heads(take_block(value_all, position, block_size, 1), head_count)
        scores = masked_scores(queries, key_rows, position * block_size, slot_lengths)
        softmax_rows = jnp.exp(scores - logsum[..., None])
        d_probs = jnp.einsum(
            "sqhd,skhd->shqk", d_context, value_rows, preferred_element_type=jnp.float32
        )
        d_scores = (softmax_rows * (d_probs - prob_delta[..., None])).astype(jnp.bfloat16)
        d_query = d_query + jnp.einsum(
            "shqk,skhd->sqhd", d_scores, key_rows, preferred_element_type=jnp.float32
        )
        d_key_rows = jnp.einsum(
            "shqk,sqhd->skhd", d_scores, queries, preferred_element_type=jnp.float32
        )
        d_value_rows = jnp.einsum(
            "shqk,sqhd->skhd",
            softmax_rows.astype(jnp.bfloat16),
            d_context,
            preferred_element_type=jnp.float32,
        )
        return (d_query, (d_key_rows, d_value_rows))

    return lax.scan(key_step_fn, jnp.zeros(queries.shape, jnp.float32), jnp.arange(block_count))


ALL_AXES = ("seq", "slot")


def flip_pairs(mask):
    return [((q * 4 + z), ((q ^ mask) * 4 + z)) for q in range(8) for z in range(4)]


def turn_pairs(step):
    return [((q * 4 + z), (q * 4 + (z + step) % 4)) for q in range(8) for z in range(4)]


CORE, X_AXIS, Y_AXIS = 1, 2, 4


def flip(value, mask):
    return lax.ppermute(value, ALL_AXES, flip_pairs(mask))


def turn(value, step):
    return lax.ppermute(value, ALL_AXES, turn_pairs(step))


def places():
    q = lax.axis_index("seq")
    return q & 1, (q >> 1) & 1, q >> 2, lax.axis_index("slot")


def merge(own, other, bit, axis):
    first = jnp.where(bit == 0, own, other)
    second = jnp.where(bit == 0, other, own)
    return jnp.stack([first, second], axis)


def gather_plane(a, b):
    core, x, y, _ = places()
    a1, b1 = merge(a, flip(a, X_AXIS), x, 0), merge(b, flip(b, Y_AXIS), y, 0)
    a2, b2 = merge(a1, flip(a1, Y_AXIS), y, 0), merge(b1, flip(b1, X_AXIS), x, 1)
    return merge(a2, flip(a2, CORE), core, 2), merge(b2, flip(b2, CORE), core, 2)


def after(value, ready):
    return lax.optimization_barrier((value, ready))[0]


def gather_line(shard):
    z = places()[3]
    from_one, from_two, from_three = (turn(shard, step) for step in (1, 2, 3))
    ring = [shard, from_three, from_two, from_one]
    return lax.dynamic_slice_in_dim(jnp.stack(ring + ring[:3]), (4 - z) % 4, 4, 0)


def gather_all(line):
    _, rows, columns = line.shape
    half = columns // 2
    a, b = gather_plane(line[..., :half], line[..., half:])
    return jnp.concatenate([a.reshape(32 * rows, half), b.reshape(32 * rows, half)], 1)


def pick(value, index, axis):
    return lax.dynamic_index_in_dim(value, index, axis, keepdims=False)


def add_low(left, right):
    return (left.astype(jnp.float32) + right.astype(jnp.float32)).astype(jnp.bfloat16)


def fold(value, bit, mask, axis):
    return add_low(pick(value, bit, axis), flip(pick(value, 1 - bit, axis), mask))


def scatter_plane(a, b):
    core, x, y, _ = places()
    a, b = fold(a, core, CORE, 2), fold(b, core, CORE, 2)
    a, b = fold(a, y, Y_AXIS, 0), fold(b, x, X_AXIS, 1)
    return fold(a, x, X_AXIS, 0), fold(b, y, Y_AXIS, 0)


def scatter_all(grad):
    rows, columns = grad.shape
    rows, half = rows // 32, columns // 2
    z = places()[3]
    a = grad[:, :half].reshape(2, 2, 2, 4, rows, half)
    b = grad[:, half:].reshape(2, 2, 2, 4, rows, half)
    sums = []
    for part in scatter_plane(a, b):
        total = pick(part, z, 0).astype(jnp.float32)
        for step in (1, 2, 3):
            total = total + turn(pick(part, (z + step) % 4, 0), step).astype(jnp.float32)
        sums.append(total)
    return jnp.concatenate(sums, 1)


def body(
    tokens,
    qkv_weight,
    query_bias,
    value_bias,
    out_weight,
    out_bias,
    norm1_gain,
    norm1_shift,
    up_weight,
    up_bias,
    down_weight,
    down_bias,
    norm2_gain,
    norm2_shift,
    slot_lengths,
    out_cotangent,
):
    slot_count, row_count, model_width = tokens.shape
    head_count = HEADS
    flat_rows = tokens.reshape(slot_count * row_count, model_width)
    attn_set = (
        lax.all_gather(qkv_weight, ("seq", "slot"), axis=0, tiled=True),
        lax.all_gather(out_weight, ("seq", "slot"), axis=0, tiled=True),
        lax.all_gather(query_bias, ("seq", "slot"), axis=0, tiled=True),
        lax.all_gather(value_bias, ("seq", "slot"), axis=0, tiled=True),
        lax.all_gather(out_bias, ("seq", "slot"), axis=0, tiled=True),
        lax.all_gather(norm1_gain, ("seq", "slot"), axis=0, tiled=True),
        lax.all_gather(norm1_shift, ("seq", "slot"), axis=0, tiled=True),
    )
    qkv_full, out_full, query_shift, value_shift, out_shift, gain_one, shift_one = attn_set
    mixed = jnp.dot(flat_rows, qkv_full, preferred_element_type=jnp.float32)
    queries = ((mixed[:, :model_width] + query_shift.astype(jnp.float32)) * 0.125).astype(
        jnp.bfloat16
    )
    queries = split_heads(queries.reshape(slot_count, row_count, model_width), head_count)
    keys_own = (
        mixed[:, model_width : 2 * model_width]
        .astype(jnp.bfloat16)
        .reshape(slot_count, row_count, model_width)
    )
    values_own = (
        (mixed[:, 2 * model_width :] + value_shift.astype(jnp.float32))
        .astype(jnp.bfloat16)
        .reshape(slot_count, row_count, model_width)
    )
    key_all, value_all = (
        lax.all_gather(keys_own, "seq", axis=1, tiled=True),
        lax.all_gather(values_own, "seq", axis=1, tiled=True),
    )
    length_all = key_all.shape[1]
    block_size = min(512, length_all)
    logsum = log_totals(queries, key_all, slot_lengths, block_size, head_count)
    context = attend(
        queries, key_all, value_all, slot_lengths, logsum, block_size, head_count
    ).astype(jnp.bfloat16)
    context_flat = context.reshape(slot_count * row_count, model_width)
    attn_out = jnp.dot(
        context_flat, out_full, preferred_element_type=jnp.float32
    ) + out_shift.astype(jnp.float32)
    resid_one = flat_rows.astype(jnp.float32) + attn_out
    hidden_one = norm_rows(resid_one, gain_one.astype(jnp.float32), shift_one.astype(jnp.float32))
    hidden_low = hidden_one.astype(jnp.bfloat16)
    ffn_set = (
        lax.all_gather(up_weight, ("seq", "slot"), axis=0, tiled=True),
        lax.all_gather(down_weight, ("seq", "slot"), axis=0, tiled=True),
        lax.all_gather(up_bias, ("seq", "slot"), axis=0, tiled=True),
        lax.all_gather(down_bias, ("seq", "slot"), axis=0, tiled=True),
        lax.all_gather(norm2_gain, ("seq", "slot"), axis=0, tiled=True),
        lax.all_gather(norm2_shift, ("seq", "slot"), axis=0, tiled=True),
    )
    up_full, down_full, up_shift, down_shift, gain_two, shift_two = ffn_set
    inner_act = jnp.dot(hidden_low, up_full, preferred_element_type=jnp.float32) + up_shift.astype(
        jnp.float32
    )
    activated = gelu_exact(inner_act).astype(jnp.bfloat16)
    ffn_out = jnp.dot(activated, down_full, preferred_element_type=jnp.float32) + down_shift.astype(
        jnp.float32
    )
    resid_two = hidden_one + ffn_out
    layer_out = norm_rows(resid_two, gain_two.astype(jnp.float32), shift_two.astype(jnp.float32))
    layer_out = layer_out.astype(jnp.bfloat16).reshape(slot_count, row_count, model_width)
    qkv_back, out_back, _, _, _, gain_one_back, shift_one_back = (
        lax.all_gather(qkv_weight, ("seq", "slot"), axis=0, tiled=True),
        lax.all_gather(out_weight, ("seq", "slot"), axis=0, tiled=True),
        lax.all_gather(query_bias, ("seq", "slot"), axis=0, tiled=True),
        lax.all_gather(value_bias, ("seq", "slot"), axis=0, tiled=True),
        lax.all_gather(out_bias, ("seq", "slot"), axis=0, tiled=True),
        lax.all_gather(norm1_gain, ("seq", "slot"), axis=0, tiled=True),
        lax.all_gather(norm1_shift, ("seq", "slot"), axis=0, tiled=True),
    )
    up_back, down_back, _, _, gain_two_back, shift_two_back = (
        lax.all_gather(up_weight, ("seq", "slot"), axis=0, tiled=True),
        lax.all_gather(down_weight, ("seq", "slot"), axis=0, tiled=True),
        lax.all_gather(up_bias, ("seq", "slot"), axis=0, tiled=True),
        lax.all_gather(down_bias, ("seq", "slot"), axis=0, tiled=True),
        lax.all_gather(norm2_gain, ("seq", "slot"), axis=0, tiled=True),
        lax.all_gather(norm2_shift, ("seq", "slot"), axis=0, tiled=True),
    )
    positions = lax.axis_index("seq") * row_count + jnp.arange(row_count)
    live_rows = (positions[None, :] < slot_lengths[:, None]).astype(jnp.float32)
    cotangent = (out_cotangent.astype(jnp.float32) * live_rows[:, :, None]).reshape(
        slot_count * row_count, model_width
    )
    _, norm_back_two = jax.vjp(
        norm_rows, resid_two, gain_two_back.astype(jnp.float32), shift_two_back.astype(jnp.float32)
    )
    d_resid_two, d_gain_two, d_shift_two = norm_back_two(cotangent)
    d_ffn = d_resid_two.astype(jnp.bfloat16)
    d_down = contract_rows(activated, d_ffn)
    d_down_shift = jnp.sum(d_ffn.astype(jnp.float32), 0)
    d_activated = contract_last(d_ffn, down_back)
    _, gelu_back = jax.vjp(gelu_exact, inner_act)
    d_inner = gelu_back(d_activated)[0].astype(jnp.bfloat16)
    d_up = contract_rows(hidden_low, d_inner)
    d_up_shift = jnp.sum(d_inner.astype(jnp.float32), 0)
    d_hidden = contract_last(d_inner, up_back) + d_resid_two
    _, norm_back_one = jax.vjp(
        norm_rows, resid_one, gain_one_back.astype(jnp.float32), shift_one_back.astype(jnp.float32)
    )
    d_resid_one, d_gain_one, d_shift_one = norm_back_one(d_hidden)
    d_attn = d_resid_one.astype(jnp.bfloat16)
    d_out = contract_rows(context_flat, d_attn)
    d_out_shift = jnp.sum(d_attn.astype(jnp.float32), 0)
    d_context = contract_last(d_attn, out_back).astype(jnp.bfloat16)
    d_context = split_heads(d_context.reshape(slot_count, row_count, model_width), head_count)
    prob_delta = prob_grad_totals(
        queries, d_context, key_all, value_all, slot_lengths, logsum, block_size, head_count
    )
    d_query, key_parts = key_side(
        queries,
        d_context,
        key_all,
        value_all,
        slot_lengths,
        logsum,
        prob_delta,
        block_size,
        head_count,
    )
    d_key_part = jnp.moveaxis(key_parts[0], 0, 1).reshape(slot_count, length_all, model_width)
    d_value_part = jnp.moveaxis(key_parts[1], 0, 1).reshape(slot_count, length_all, model_width)
    d_key_sum, d_value_sum = (
        lax.psum_scatter(
            d_key_part.astype(jnp.bfloat16), "seq", scatter_dimension=1, tiled=True
        ).astype(jnp.float32),
        lax.psum_scatter(
            d_value_part.astype(jnp.bfloat16), "seq", scatter_dimension=1, tiled=True
        ).astype(jnp.float32),
    )
    d_query_pre = d_query.astype(jnp.bfloat16).reshape(
        slot_count * row_count, model_width
    ) * jnp.asarray(0.125, jnp.bfloat16)
    d_key_low = d_key_sum.astype(jnp.bfloat16).reshape(slot_count * row_count, model_width)
    d_value_low = d_value_sum.astype(jnp.bfloat16).reshape(slot_count * row_count, model_width)
    d_mixed = jnp.concatenate([d_query_pre, d_key_low, d_value_low], 1)
    d_qkv = contract_rows(flat_rows, d_mixed)
    d_query_shift = jnp.sum(d_query_pre.astype(jnp.float32), 0)
    d_value_shift = jnp.sum(d_value_low.astype(jnp.float32), 0)
    tokens_grad = (
        (d_resid_one + contract_last(d_mixed, qkv_back))
        .astype(jnp.bfloat16)
        .reshape(slot_count, row_count, model_width)
    )
    attn_sums = (
        lax.psum_scatter(d_qkv, ("seq", "slot"), scatter_dimension=0, tiled=True),
        lax.psum_scatter(d_out, ("seq", "slot"), scatter_dimension=0, tiled=True),
        lax.psum_scatter(d_query_shift, ("seq", "slot"), scatter_dimension=0, tiled=True),
        lax.psum_scatter(d_value_shift, ("seq", "slot"), scatter_dimension=0, tiled=True),
        lax.psum_scatter(d_out_shift, ("seq", "slot"), scatter_dimension=0, tiled=True),
        lax.psum_scatter(d_gain_one, ("seq", "slot"), scatter_dimension=0, tiled=True),
        lax.psum_scatter(d_shift_one, ("seq", "slot"), scatter_dimension=0, tiled=True),
    )
    ffn_sums = (
        lax.psum_scatter(d_up, ("seq", "slot"), scatter_dimension=0, tiled=True),
        lax.psum_scatter(d_down, ("seq", "slot"), scatter_dimension=0, tiled=True),
        lax.psum_scatter(d_up_shift, ("seq", "slot"), scatter_dimension=0, tiled=True),
        lax.psum_scatter(d_down_shift, ("seq", "slot"), scatter_dimension=0, tiled=True),
        lax.psum_scatter(d_gain_two, ("seq", "slot"), scatter_dimension=0, tiled=True),
        lax.psum_scatter(d_shift_two, ("seq", "slot"), scatter_dimension=0, tiled=True),
    )
    return (
        layer_out,
        tokens_grad,
        attn_sums[0],
        attn_sums[2],
        attn_sums[3],
        attn_sums[1],
        attn_sums[4],
        attn_sums[5],
        attn_sums[6],
        ffn_sums[0],
        ffn_sums[2],
        ffn_sums[1],
        ffn_sums[3],
        ffn_sums[4],
        ffn_sums[5],
    )


def body_fast(
    tokens,
    qkv_weight,
    query_bias,
    value_bias,
    out_weight,
    out_bias,
    norm1_gain,
    norm1_shift,
    up_weight,
    up_bias,
    down_weight,
    down_bias,
    norm2_gain,
    norm2_shift,
    slot_lengths,
    out_cotangent,
):
    slot_count, row_count, model_width = tokens.shape
    part = qkv_weight.shape[0]
    inner_part = up_bias.shape[0]
    flat_rows = tokens.reshape(slot_count * row_count, model_width)
    small = jnp.concatenate(
        [
            query_bias,
            value_bias,
            out_bias,
            norm1_gain,
            norm1_shift,
            down_bias,
            norm2_gain,
            norm2_shift,
            up_bias,
        ]
    )
    small_columns = small.shape[0] // part
    small = jnp.pad(small.reshape(part, small_columns), ((0, 0), (0, 256 - small_columns)))
    attn_line = gather_line(jnp.concatenate([qkv_weight, out_weight, small], 1))
    up_line = gather_line(after(up_weight, attn_line))
    down_line = gather_line(after(down_weight, up_line))
    attn_full = gather_all(attn_line)
    up_full = gather_all(up_line)
    down_full = gather_all(down_line)
    qkv_full = attn_full[:, : 3 * model_width]
    out_full = attn_full[:, 3 * model_width : 4 * model_width]
    small_full = attn_full[:, 4 * model_width : 4 * model_width + small_columns]
    small_full = small_full.reshape(32, part * small_columns).astype(jnp.float32)

    def vector(position):
        return small_full[:, position * part : (position + 1) * part].reshape(model_width)

    query_shift, value_shift, out_shift, gain_one, shift_one, down_shift, gain_two, shift_two = (
        vector(position) for position in range(8)
    )
    up_shift = small_full[:, 8 * part :].reshape(32 * inner_part)
    mixed = jnp.dot(flat_rows, qkv_full, preferred_element_type=jnp.float32)
    queries = ((mixed[:, :model_width] + query_shift) * 0.125).astype(jnp.bfloat16)
    queries = queries.reshape(slot_count, row_count, model_width)
    keys_own = (
        mixed[:, model_width : 2 * model_width]
        .astype(jnp.bfloat16)
        .reshape(slot_count, row_count, model_width)
    )
    values_own = (
        (mixed[:, 2 * model_width :] + value_shift)
        .astype(jnp.bfloat16)
        .reshape(slot_count, row_count, model_width)
    )

    places_shape = (8, slot_count, row_count, model_width)
    key_all, value_all = (part.reshape(places_shape) for part in gather_plane(keys_own, values_own))
    context, logsum = attention_call(
        attend_kernel, slot_lengths, (queries, key_all, value_all), False
    )
    context_flat = context.reshape(slot_count * row_count, model_width)
    attn_out = jnp.dot(context_flat, out_full, preferred_element_type=jnp.float32) + out_shift
    resid_one = flat_rows.astype(jnp.float32) + attn_out
    hidden_one = norm_rows(resid_one, gain_one, shift_one)
    hidden_low = hidden_one.astype(jnp.bfloat16)
    inner_act = jnp.dot(hidden_low, up_full, preferred_element_type=jnp.float32) + up_shift
    activated = gelu_exact(inner_act).astype(jnp.bfloat16)
    ffn_out = jnp.dot(activated, down_full, preferred_element_type=jnp.float32) + down_shift
    resid_two = hidden_one + ffn_out
    layer_out = norm_rows(resid_two, gain_two, shift_two)
    layer_out = layer_out.astype(jnp.bfloat16).reshape(slot_count, row_count, model_width)
    positions = lax.axis_index("seq") * row_count + jnp.arange(row_count)
    live_rows = (positions[None, :] < slot_lengths[:, None]).astype(jnp.float32)
    cotangent = (out_cotangent.astype(jnp.float32) * live_rows[:, :, None]).reshape(
        slot_count * row_count, model_width
    )
    _, norm_back_two = jax.vjp(norm_rows, resid_two, gain_two, shift_two)
    d_resid_two, d_gain_two, d_shift_two = norm_back_two(cotangent)
    d_ffn = d_resid_two.astype(jnp.bfloat16)
    d_down = scatter_all(contract_rows(activated, d_ffn).astype(jnp.bfloat16))
    d_down_shift = jnp.sum(d_ffn.astype(jnp.float32), 0)
    d_activated = contract_last(d_ffn, down_full)
    _, gelu_back = jax.vjp(gelu_exact, inner_act)
    d_inner = gelu_back(d_activated)[0].astype(jnp.bfloat16)
    d_up = scatter_all(contract_rows(hidden_low, d_inner).astype(jnp.bfloat16))
    d_up_shift = jnp.sum(d_inner.astype(jnp.float32), 0)
    d_hidden = contract_last(d_inner, up_full) + d_resid_two
    _, norm_back_one = jax.vjp(norm_rows, resid_one, gain_one, shift_one)
    d_resid_one, d_gain_one, d_shift_one = norm_back_one(d_hidden)
    d_attn = d_resid_one.astype(jnp.bfloat16)
    d_out = scatter_all(contract_rows(context_flat, d_attn).astype(jnp.bfloat16))
    d_out_shift = jnp.sum(d_attn.astype(jnp.float32), 0)
    d_context = contract_last(d_attn, out_full).astype(jnp.bfloat16)
    d_query, d_key_part, d_value_part = attention_call(
        attend_back_kernel,
        slot_lengths,
        (
            queries,
            d_context.reshape(slot_count, row_count, model_width),
            key_all,
            value_all,
            logsum,
        ),
        True,
    )
    d_key_low, d_value_low = scatter_plane(
        d_key_part.reshape((2, 2, 2) + places_shape[1:]),
        d_value_part.reshape((2, 2, 2) + places_shape[1:]),
    )
    d_query_pre = d_query.reshape(slot_count * row_count, model_width)
    d_key_low = d_key_low.reshape(slot_count * row_count, model_width)
    d_value_low = d_value_low.reshape(slot_count * row_count, model_width)
    d_mixed = jnp.concatenate([d_query_pre, d_key_low, d_value_low], 1)
    d_qkv = contract_rows(flat_rows, d_mixed).astype(jnp.bfloat16)
    d_query_shift = jnp.sum(d_query_pre.astype(jnp.float32), 0)
    d_value_shift = jnp.sum(d_value_low.astype(jnp.float32), 0)
    tokens_grad = (
        (d_resid_one + contract_last(d_mixed, qkv_full))
        .astype(jnp.bfloat16)
        .reshape(slot_count, row_count, model_width)
    )
    small_grads = jnp.concatenate(
        [
            grad.reshape(32, grad.shape[0] // 32)
            for grad in (
                d_query_shift,
                d_value_shift,
                d_out_shift,
                d_gain_one,
                d_shift_one,
                d_down_shift,
                d_gain_two,
                d_shift_two,
                d_up_shift,
            )
        ],
        1,
    ).astype(jnp.bfloat16)
    small_grads = jnp.pad(
        small_grads.reshape(32 * part, small_columns), ((0, 0), (0, 256 - small_columns))
    )
    attn_sums = scatter_all(jnp.concatenate([d_qkv, small_grads], 1))
    own = attn_sums[:, 3 * model_width : 3 * model_width + small_columns].reshape(-1)
    vectors = [own[position * part : (position + 1) * part] for position in range(8)]
    return (
        layer_out,
        tokens_grad,
        attn_sums[:, : 3 * model_width],
        vectors[0],
        vectors[1],
        d_out,
        vectors[2],
        vectors[3],
        vectors[4],
        d_up,
        own[8 * part :],
        d_down,
        vectors[5],
        vectors[6],
        vectors[7],
    )


def contract_first(left, right):
    return lax.dot_general(
        left, right, (((0,), (0,)), ((), ())), preferred_element_type=jnp.float32
    )


def pair_lanes(value):
    low_half = lax.broadcasted_iota(jnp.int32, value.shape, 1) < value.shape[1] // 2
    zero = jnp.zeros_like(value)
    return low_half, (jnp.where(low_half, value, zero), jnp.where(low_half, zero, value))


def live_scores(keys, query, length):
    scores = contract_last(keys, query)
    places = lax.broadcasted_iota(jnp.int32, scores.shape, 0)
    return jnp.where(places < length, scores, NEG_FILL)


def attend_kernel(lengths, query_ref, key_ref, value_ref, context_ref, logsum_ref):
    length = lengths[pl.program_id(0)]
    lanes = query_ref.shape[-1]
    keys = key_ref[...].reshape(-1, lanes)
    values = value_ref[...].reshape(-1, lanes)
    low_half, query_pair = pair_lanes(query_ref[0])
    outs = []
    for head, query in enumerate(query_pair):
        scores = live_scores(keys, query, length)
        row_max = jnp.max(scores, 0, keepdims=True)
        weights = jnp.exp(scores - row_max)
        total = jnp.sum(weights, 0, keepdims=True)
        logsum_ref[0, 0, head : head + 1, :] = row_max + jnp.log(total)
        probs_low = (weights * (1.0 / total)).astype(jnp.bfloat16)
        outs.append(contract_first(probs_low, values))
    context_ref[0] = jnp.where(low_half, outs[0], outs[1]).astype(jnp.bfloat16)


def attend_back_kernel(
    lengths,
    query_ref,
    d_context_ref,
    key_ref,
    value_ref,
    logsum_ref,
    d_query_ref,
    d_key_ref,
    d_value_ref,
):
    length = lengths[pl.program_id(0)]
    lanes = query_ref.shape[-1]
    keys = key_ref[...].reshape(-1, lanes)
    values = value_ref[...].reshape(-1, lanes)
    low_half, query_pair = pair_lanes(query_ref[0])
    _, d_context_pair = pair_lanes(d_context_ref[0])
    d_query_pair, d_keys, d_values = [], [], []
    for head in range(2):
        query, d_context = query_pair[head], d_context_pair[head]
        scores = live_scores(keys, query, length)
        probs = jnp.exp(scores - logsum_ref[0, 0, head : head + 1, :])
        d_probs = contract_last(values, d_context)
        prob_delta = jnp.sum(probs * d_probs, 0, keepdims=True)
        d_scores = (probs * (d_probs - prob_delta)).astype(jnp.bfloat16)
        d_query_pair.append(contract_first(d_scores, keys))
        d_keys.append(jnp.dot(d_scores, query, preferred_element_type=jnp.float32))
        d_values.append(
            jnp.dot(probs.astype(jnp.bfloat16), d_context, preferred_element_type=jnp.float32)
        )
    d_query = jnp.where(low_half, d_query_pair[0], d_query_pair[1]).astype(jnp.bfloat16)
    d_query_ref[0] = d_query * jnp.asarray(0.125, jnp.bfloat16)
    d_key_ref[...] = (d_keys[0] + d_keys[1]).astype(jnp.bfloat16).reshape(d_key_ref.shape)
    d_value_ref[...] = (d_values[0] + d_values[1]).astype(jnp.bfloat16).reshape(d_value_ref.shape)


def attention_call(kernel, slot_lengths, operands, backward):
    queries, keys = operands[0], operands[2 if backward else 1]
    slot_count, row_count, width = queries.shape
    place_count, lanes = keys.shape[0], 128
    pairs = width // lanes
    row_spec = pl.BlockSpec((1, row_count, lanes), lambda s, p, _: (s, 0, p))
    key_spec = pl.BlockSpec((place_count, 1, row_count, lanes), lambda s, p, _: (0, s, 0, p))
    stat_spec = pl.BlockSpec((1, 1, 8, row_count), lambda s, p, _: (s, p, 0, 0))
    low_rows = jax.ShapeDtypeStruct(queries.shape, jnp.bfloat16)
    low_keys = jax.ShapeDtypeStruct(keys.shape, jnp.bfloat16)
    stats = jax.ShapeDtypeStruct((slot_count, pairs, 8, row_count), jnp.float32)
    products = 5 if backward else 2
    scores = 2 * slot_count * pairs * row_count * place_count * row_count
    return pl.pallas_call(
        kernel,
        out_shape=(low_rows, low_keys, low_keys) if backward else (low_rows, stats),
        grid_spec=pltpu.PrefetchScalarGridSpec(
            num_scalar_prefetch=1,
            grid=(slot_count, pairs),
            in_specs=(
                [row_spec, row_spec, key_spec, key_spec, stat_spec]
                if backward
                else [row_spec, key_spec, key_spec]
            ),
            out_specs=[row_spec, key_spec, key_spec] if backward else [row_spec, stat_spec],
        ),
        cost_estimate=pl.CostEstimate(
            flops=products * 8 * scores * lanes,
            bytes_accessed=products * 2 * place_count * slot_count * row_count * width,
            transcendentals=scores,
        ),
    )(slot_lengths, *operands)


def solution(mesh):
    fast = mesh.shape["seq"] == 8 and mesh.shape["slot"] == 4
    return jax.shard_map(
        body_fast if fast else body,
        mesh=mesh,
        in_specs=(
            P("slot", "seq", None),
            P(("seq", "slot"), None),
            P(("seq", "slot")),
            P(("seq", "slot")),
            P(("seq", "slot"), None),
            P(("seq", "slot")),
            P(("seq", "slot")),
            P(("seq", "slot")),
            P(("seq", "slot"), None),
            P(("seq", "slot")),
            P(("seq", "slot"), None),
            P(("seq", "slot")),
            P(("seq", "slot")),
            P(("seq", "slot")),
            P("slot"),
            P("slot", "seq", None),
        ),
        out_specs=(
            P("slot", "seq", None),
            P("slot", "seq", None),
            P(("seq", "slot"), None),
            P(("seq", "slot")),
            P(("seq", "slot")),
            P(("seq", "slot"), None),
            P(("seq", "slot")),
            P(("seq", "slot")),
            P(("seq", "slot")),
            P(("seq", "slot"), None),
            P(("seq", "slot")),
            P(("seq", "slot"), None),
            P(("seq", "slot")),
            P(("seq", "slot")),
            P(("seq", "slot")),
        ),
        check_vma=False,
    )
```

```python
import jax
import jax.numpy as jnp
from jax import lax
from jax.experimental import pallas as pl
from jax.experimental.pallas import tpu as pltpu
from jax.sharding import PartitionSpec as P

HEADS = 12


NEG_FILL = -1e30
EPSILON = 1e-05


def norm_rows(resid, gain, shift):
    centre = resid - jnp.mean(resid, -1, keepdims=True)
    spread = jnp.mean(centre * centre, -1, keepdims=True)
    return centre * lax.rsqrt(spread + EPSILON) * gain + shift


def gelu_exact(inner_act):
    return jax.nn.gelu(inner_act, approximate=False)


def contract_rows(left, right):
    return lax.dot_general(
        left, right, (((0,), (0,)), ((), ())), preferred_element_type=jnp.float32
    )


def contract_last(left, right):
    return lax.dot_general(
        left, right, (((1,), (1,)), ((), ())), preferred_element_type=jnp.float32
    )


def split_heads(rows_in, head_count):
    return rows_in.reshape(
        rows_in.shape[0], rows_in.shape[1], head_count, rows_in.shape[2] // head_count
    )


def take_block(whole, position, block_size, axis_dim):
    return lax.dynamic_slice_in_dim(whole, position * block_size, block_size, axis_dim)


def masked_scores(queries, key_rows, key_start, slot_lengths):
    scores = jnp.einsum("sqhd,skhd->shqk", queries, key_rows, preferred_element_type=jnp.float32)
    key_places = key_start + jnp.arange(key_rows.shape[1])
    live_keys = key_places[None, :] < slot_lengths[:, None]
    return jnp.where(live_keys[:, None, None, :], scores, NEG_FILL)


def log_totals(queries, key_all, slot_lengths, block_size, head_count):
    block_count = key_all.shape[1] // block_size
    stat_shape = (queries.shape[0], head_count, queries.shape[1])

    def log_step_fn(carried, position):
        running_max, running_sum = carried
        key_rows = split_heads(take_block(key_all, position, block_size, 1), head_count)
        scores = masked_scores(queries, key_rows, position * block_size, slot_lengths)
        new_max = jnp.maximum(running_max, jnp.max(scores, -1))
        running_sum = running_sum * jnp.exp(running_max - new_max) + jnp.sum(
            jnp.exp(scores - new_max[..., None]), -1
        )
        return ((new_max, running_sum), None)

    start_state = (jnp.full(stat_shape, NEG_FILL, jnp.float32), jnp.zeros(stat_shape, jnp.float32))
    (running_max, running_sum), _ = lax.scan(log_step_fn, start_state, jnp.arange(block_count))
    return running_max + jnp.log(running_sum)


def attend(queries, key_all, value_all, slot_lengths, logsum, block_size, head_count):
    block_count = key_all.shape[1] // block_size

    def attend_step_fn(context, position):
        key_rows = split_heads(take_block(key_all, position, block_size, 1), head_count)
        value_rows = split_heads(take_block(value_all, position, block_size, 1), head_count)
        scores = masked_scores(queries, key_rows, position * block_size, slot_lengths)
        weights_low = jnp.exp(scores - logsum[..., None]).astype(jnp.bfloat16)
        return (
            context
            + jnp.einsum(
                "shqk,skhd->sqhd", weights_low, value_rows, preferred_element_type=jnp.float32
            ),
            None,
        )

    context, _ = lax.scan(
        attend_step_fn, jnp.zeros(queries.shape, jnp.float32), jnp.arange(block_count)
    )
    return context


def prob_grad_totals(
    queries, d_context, key_all, value_all, slot_lengths, logsum, block_size, head_count
):
    block_count = key_all.shape[1] // block_size

    def prob_step_fn(prob_delta, position):
        key_rows = split_heads(take_block(key_all, position, block_size, 1), head_count)
        value_rows = split_heads(take_block(value_all, position, block_size, 1), head_count)
        scores = masked_scores(queries, key_rows, position * block_size, slot_lengths)
        softmax_rows = jnp.exp(scores - logsum[..., None])
        d_probs = jnp.einsum(
            "sqhd,skhd->shqk", d_context, value_rows, preferred_element_type=jnp.float32
        )
        return (prob_delta + jnp.sum(softmax_rows * d_probs, -1), None)

    prob_delta, _ = lax.scan(
        prob_step_fn, jnp.zeros(logsum.shape, jnp.float32), jnp.arange(block_count)
    )
    return prob_delta


def key_side(
    queries, d_context, key_all, value_all, slot_lengths, logsum, prob_delta, block_size, head_count
):
    block_count = key_all.shape[1] // block_size

    def key_step_fn(d_query, position):
        key_rows = split_heads(take_block(key_all, position, block_size, 1), head_count)
        value_rows = split_heads(take_block(value_all, position, block_size, 1), head_count)
        scores = masked_scores(queries, key_rows, position * block_size, slot_lengths)
        softmax_rows = jnp.exp(scores - logsum[..., None])
        d_probs = jnp.einsum(
            "sqhd,skhd->shqk", d_context, value_rows, preferred_element_type=jnp.float32
        )
        d_scores = (softmax_rows * (d_probs - prob_delta[..., None])).astype(jnp.bfloat16)
        d_query = d_query + jnp.einsum(
            "shqk,skhd->sqhd", d_scores, key_rows, preferred_element_type=jnp.float32
        )
        d_key_rows = jnp.einsum(
            "shqk,sqhd->skhd", d_scores, queries, preferred_element_type=jnp.float32
        )
        d_value_rows = jnp.einsum(
            "shqk,sqhd->skhd",
            softmax_rows.astype(jnp.bfloat16),
            d_context,
            preferred_element_type=jnp.float32,
        )
        return (d_query, (d_key_rows, d_value_rows))

    return lax.scan(key_step_fn, jnp.zeros(queries.shape, jnp.float32), jnp.arange(block_count))


ALL_AXES = ("seq", "slot")


def flip_pairs(mask):
    return [((q * 4 + z), ((q ^ mask) * 4 + z)) for q in range(8) for z in range(4)]


def turn_pairs(step):
    return [((q * 4 + z), (q * 4 + (z + step) % 4)) for q in range(8) for z in range(4)]


CORE, X_AXIS, Y_AXIS = 1, 2, 4


def flip(value, mask):
    return lax.ppermute(value, ALL_AXES, flip_pairs(mask))


def turn(value, step):
    return lax.ppermute(value, ALL_AXES, turn_pairs(step))


def places():
    q = lax.axis_index("seq")
    return q & 1, (q >> 1) & 1, q >> 2, lax.axis_index("slot")


def merge(own, other, bit, axis):
    first = jnp.where(bit == 0, own, other)
    second = jnp.where(bit == 0, other, own)
    return jnp.stack([first, second], axis)


def gather_plane(a, b):
    core, x, y, _ = places()
    a1, b1 = flip(a, X_AXIS), flip(b, Y_AXIS)
    a1, b1 = merge(a, a1, x, 0), merge(b, b1, y, 0)
    a2, b2 = flip(a1, Y_AXIS), flip(b1, X_AXIS)
    a2, b2 = merge(a1, a2, y, 0), merge(b1, b2, x, 1)
    a3, b3 = flip(a2, CORE), flip(b2, CORE)
    return merge(a2, a3, core, 2), merge(b2, b3, core, 2)


def after(value, ready):
    return lax.optimization_barrier((value, ready))[0]


def gather_line(shard):
    z = places()[3]
    from_one, from_two, from_three = (turn(shard, step) for step in (1, 2, 3))
    ring = [shard, from_three, from_two, from_one]
    return lax.dynamic_slice_in_dim(jnp.stack(ring + ring[:3]), (4 - z) % 4, 4, 0)


def as_matrix(parts):
    return parts.reshape(32 * parts.shape[-2], parts.shape[-1])


def pick(value, index, axis):
    return lax.dynamic_index_in_dim(value, index, axis, keepdims=False)


def add_low(left, right):
    return (left.astype(jnp.float32) + right.astype(jnp.float32)).astype(jnp.bfloat16)


def fold(value, bit, mask, axis):
    return add_low(pick(value, bit, axis), flip(pick(value, 1 - bit, axis), mask))


def scatter_plane(a, b):
    core, x, y, _ = places()
    a, b = fold(a, core, CORE, 2), fold(b, core, CORE, 2)
    a, b = fold(a, y, Y_AXIS, 0), fold(b, x, X_AXIS, 1)
    return fold(a, x, X_AXIS, 0), fold(b, y, Y_AXIS, 0)


def scatter_line(part):
    z = places()[3]
    return [pick(part, z, 0)] + [turn(pick(part, (z + step) % 4, 0), step) for step in (1, 2, 3)]


def line_total(terms):
    return sum(term.astype(jnp.float32) for term in terms)


def place_blocks(part):
    return part.reshape(2, 2, 2, 4, part.shape[0] // 32, part.shape[1])


def body(
    tokens,
    qkv_weight,
    query_bias,
    value_bias,
    out_weight,
    out_bias,
    norm1_gain,
    norm1_shift,
    up_weight,
    up_bias,
    down_weight,
    down_bias,
    norm2_gain,
    norm2_shift,
    slot_lengths,
    out_cotangent,
):
    slot_count, row_count, model_width = tokens.shape
    head_count = HEADS
    flat_rows = tokens.reshape(slot_count * row_count, model_width)
    attn_set = (
        lax.all_gather(qkv_weight, ("seq", "slot"), axis=0, tiled=True),
        lax.all_gather(out_weight, ("seq", "slot"), axis=0, tiled=True),
        lax.all_gather(query_bias, ("seq", "slot"), axis=0, tiled=True),
        lax.all_gather(value_bias, ("seq", "slot"), axis=0, tiled=True),
        lax.all_gather(out_bias, ("seq", "slot"), axis=0, tiled=True),
        lax.all_gather(norm1_gain, ("seq", "slot"), axis=0, tiled=True),
        lax.all_gather(norm1_shift, ("seq", "slot"), axis=0, tiled=True),
    )
    qkv_full, out_full, query_shift, value_shift, out_shift, gain_one, shift_one = attn_set
    mixed = jnp.dot(flat_rows, qkv_full, preferred_element_type=jnp.float32)
    queries = ((mixed[:, :model_width] + query_shift.astype(jnp.float32)) * 0.125).astype(
        jnp.bfloat16
    )
    queries = split_heads(queries.reshape(slot_count, row_count, model_width), head_count)
    keys_own = (
        mixed[:, model_width : 2 * model_width]
        .astype(jnp.bfloat16)
        .reshape(slot_count, row_count, model_width)
    )
    values_own = (
        (mixed[:, 2 * model_width :] + value_shift.astype(jnp.float32))
        .astype(jnp.bfloat16)
        .reshape(slot_count, row_count, model_width)
    )
    key_all, value_all = (
        lax.all_gather(keys_own, "seq", axis=1, tiled=True),
        lax.all_gather(values_own, "seq", axis=1, tiled=True),
    )
    length_all = key_all.shape[1]
    block_size = min(512, length_all)
    logsum = log_totals(queries, key_all, slot_lengths, block_size, head_count)
    context = attend(
        queries, key_all, value_all, slot_lengths, logsum, block_size, head_count
    ).astype(jnp.bfloat16)
    context_flat = context.reshape(slot_count * row_count, model_width)
    attn_out = jnp.dot(
        context_flat, out_full, preferred_element_type=jnp.float32
    ) + out_shift.astype(jnp.float32)
    resid_one = flat_rows.astype(jnp.float32) + attn_out
    hidden_one = norm_rows(resid_one, gain_one.astype(jnp.float32), shift_one.astype(jnp.float32))
    hidden_low = hidden_one.astype(jnp.bfloat16)
    ffn_set = (
        lax.all_gather(up_weight, ("seq", "slot"), axis=0, tiled=True),
        lax.all_gather(down_weight, ("seq", "slot"), axis=0, tiled=True),
        lax.all_gather(up_bias, ("seq", "slot"), axis=0, tiled=True),
        lax.all_gather(down_bias, ("seq", "slot"), axis=0, tiled=True),
        lax.all_gather(norm2_gain, ("seq", "slot"), axis=0, tiled=True),
        lax.all_gather(norm2_shift, ("seq", "slot"), axis=0, tiled=True),
    )
    up_full, down_full, up_shift, down_shift, gain_two, shift_two = ffn_set
    inner_act = jnp.dot(hidden_low, up_full, preferred_element_type=jnp.float32) + up_shift.astype(
        jnp.float32
    )
    activated = gelu_exact(inner_act).astype(jnp.bfloat16)
    ffn_out = jnp.dot(activated, down_full, preferred_element_type=jnp.float32) + down_shift.astype(
        jnp.float32
    )
    resid_two = hidden_one + ffn_out
    layer_out = norm_rows(resid_two, gain_two.astype(jnp.float32), shift_two.astype(jnp.float32))
    layer_out = layer_out.astype(jnp.bfloat16).reshape(slot_count, row_count, model_width)
    qkv_back, out_back, _, _, _, gain_one_back, shift_one_back = (
        lax.all_gather(qkv_weight, ("seq", "slot"), axis=0, tiled=True),
        lax.all_gather(out_weight, ("seq", "slot"), axis=0, tiled=True),
        lax.all_gather(query_bias, ("seq", "slot"), axis=0, tiled=True),
        lax.all_gather(value_bias, ("seq", "slot"), axis=0, tiled=True),
        lax.all_gather(out_bias, ("seq", "slot"), axis=0, tiled=True),
        lax.all_gather(norm1_gain, ("seq", "slot"), axis=0, tiled=True),
        lax.all_gather(norm1_shift, ("seq", "slot"), axis=0, tiled=True),
    )
    up_back, down_back, _, _, gain_two_back, shift_two_back = (
        lax.all_gather(up_weight, ("seq", "slot"), axis=0, tiled=True),
        lax.all_gather(down_weight, ("seq", "slot"), axis=0, tiled=True),
        lax.all_gather(up_bias, ("seq", "slot"), axis=0, tiled=True),
        lax.all_gather(down_bias, ("seq", "slot"), axis=0, tiled=True),
        lax.all_gather(norm2_gain, ("seq", "slot"), axis=0, tiled=True),
        lax.all_gather(norm2_shift, ("seq", "slot"), axis=0, tiled=True),
    )
    positions = lax.axis_index("seq") * row_count + jnp.arange(row_count)
    live_rows = (positions[None, :] < slot_lengths[:, None]).astype(jnp.float32)
    cotangent = (out_cotangent.astype(jnp.float32) * live_rows[:, :, None]).reshape(
        slot_count * row_count, model_width
    )
    _, norm_back_two = jax.vjp(
        norm_rows, resid_two, gain_two_back.astype(jnp.float32), shift_two_back.astype(jnp.float32)
    )
    d_resid_two, d_gain_two, d_shift_two = norm_back_two(cotangent)
    d_ffn = d_resid_two.astype(jnp.bfloat16)
    d_down = contract_rows(activated, d_ffn)
    d_down_shift = jnp.sum(d_ffn.astype(jnp.float32), 0)
    d_activated = contract_last(d_ffn, down_back)
    _, gelu_back = jax.vjp(gelu_exact, inner_act)
    d_inner = gelu_back(d_activated)[0].astype(jnp.bfloat16)
    d_up = contract_rows(hidden_low, d_inner)
    d_up_shift = jnp.sum(d_inner.astype(jnp.float32), 0)
    d_hidden = contract_last(d_inner, up_back) + d_resid_two
    _, norm_back_one = jax.vjp(
        norm_rows, resid_one, gain_one_back.astype(jnp.float32), shift_one_back.astype(jnp.float32)
    )
    d_resid_one, d_gain_one, d_shift_one = norm_back_one(d_hidden)
    d_attn = d_resid_one.astype(jnp.bfloat16)
    d_out = contract_rows(context_flat, d_attn)
    d_out_shift = jnp.sum(d_attn.astype(jnp.float32), 0)
    d_context = contract_last(d_attn, out_back).astype(jnp.bfloat16)
    d_context = split_heads(d_context.reshape(slot_count, row_count, model_width), head_count)
    prob_delta = prob_grad_totals(
        queries, d_context, key_all, value_all, slot_lengths, logsum, block_size, head_count
    )
    d_query, key_parts = key_side(
        queries,
        d_context,
        key_all,
        value_all,
        slot_lengths,
        logsum,
        prob_delta,
        block_size,
        head_count,
    )
    d_key_part = jnp.moveaxis(key_parts[0], 0, 1).reshape(slot_count, length_all, model_width)
    d_value_part = jnp.moveaxis(key_parts[1], 0, 1).reshape(slot_count, length_all, model_width)
    d_key_sum, d_value_sum = (
        lax.psum_scatter(
            d_key_part.astype(jnp.bfloat16), "seq", scatter_dimension=1, tiled=True
        ).astype(jnp.float32),
        lax.psum_scatter(
            d_value_part.astype(jnp.bfloat16), "seq", scatter_dimension=1, tiled=True
        ).astype(jnp.float32),
    )
    d_query_pre = d_query.astype(jnp.bfloat16).reshape(
        slot_count * row_count, model_width
    ) * jnp.asarray(0.125, jnp.bfloat16)
    d_key_low = d_key_sum.astype(jnp.bfloat16).reshape(slot_count * row_count, model_width)
    d_value_low = d_value_sum.astype(jnp.bfloat16).reshape(slot_count * row_count, model_width)
    d_mixed = jnp.concatenate([d_query_pre, d_key_low, d_value_low], 1)
    d_qkv = contract_rows(flat_rows, d_mixed)
    d_query_shift = jnp.sum(d_query_pre.astype(jnp.float32), 0)
    d_value_shift = jnp.sum(d_value_low.astype(jnp.float32), 0)
    tokens_grad = (
        (d_resid_one + contract_last(d_mixed, qkv_back))
        .astype(jnp.bfloat16)
        .reshape(slot_count, row_count, model_width)
    )
    attn_sums = (
        lax.psum_scatter(d_qkv, ("seq", "slot"), scatter_dimension=0, tiled=True),
        lax.psum_scatter(d_out, ("seq", "slot"), scatter_dimension=0, tiled=True),
        lax.psum_scatter(d_query_shift, ("seq", "slot"), scatter_dimension=0, tiled=True),
        lax.psum_scatter(d_value_shift, ("seq", "slot"), scatter_dimension=0, tiled=True),
        lax.psum_scatter(d_out_shift, ("seq", "slot"), scatter_dimension=0, tiled=True),
        lax.psum_scatter(d_gain_one, ("seq", "slot"), scatter_dimension=0, tiled=True),
        lax.psum_scatter(d_shift_one, ("seq", "slot"), scatter_dimension=0, tiled=True),
    )
    ffn_sums = (
        lax.psum_scatter(d_up, ("seq", "slot"), scatter_dimension=0, tiled=True),
        lax.psum_scatter(d_down, ("seq", "slot"), scatter_dimension=0, tiled=True),
        lax.psum_scatter(d_up_shift, ("seq", "slot"), scatter_dimension=0, tiled=True),
        lax.psum_scatter(d_down_shift, ("seq", "slot"), scatter_dimension=0, tiled=True),
        lax.psum_scatter(d_gain_two, ("seq", "slot"), scatter_dimension=0, tiled=True),
        lax.psum_scatter(d_shift_two, ("seq", "slot"), scatter_dimension=0, tiled=True),
    )
    return (
        layer_out,
        tokens_grad,
        attn_sums[0],
        attn_sums[2],
        attn_sums[3],
        attn_sums[1],
        attn_sums[4],
        attn_sums[5],
        attn_sums[6],
        ffn_sums[0],
        ffn_sums[2],
        ffn_sums[1],
        ffn_sums[3],
        ffn_sums[4],
        ffn_sums[5],
    )


def body_fast(
    tokens,
    qkv_weight,
    query_bias,
    value_bias,
    out_weight,
    out_bias,
    norm1_gain,
    norm1_shift,
    up_weight,
    up_bias,
    down_weight,
    down_bias,
    norm2_gain,
    norm2_shift,
    slot_lengths,
    out_cotangent,
):
    slot_count, row_count, model_width = tokens.shape
    part = qkv_weight.shape[0]
    inner_part = up_bias.shape[0]
    flat_rows = tokens.reshape(slot_count * row_count, model_width)
    small = jnp.stack(
        [
            query_bias,
            value_bias,
            out_bias,
            norm1_gain,
            norm1_shift,
            down_bias,
            norm2_gain,
            norm2_shift,
        ]
    )
    small = jnp.concatenate(
        [
            jnp.pad(small, ((0, 0), (0, 256 - part))),
            jnp.pad(up_bias[None], ((0, part - 9), (0, 256 - inner_part))),
        ]
    )
    attn_line = gather_line(jnp.concatenate([qkv_weight, out_weight, small], 1))
    half = attn_line.shape[-1] // 2
    rest = 3 * model_width - half
    up_line = gather_line(after(up_weight, attn_line))
    down_line = gather_line(after(down_weight, attn_line))
    attn_parts = gather_plane(attn_line[..., :half], attn_line[..., half:])
    attn_a, attn_b = (as_matrix(parts) for parts in attn_parts)
    up_full, down_full = (as_matrix(parts) for parts in gather_plane(up_line, down_line))
    out_full = attn_b[:, rest : rest + model_width]
    small_full = attn_b[:, rest + model_width : rest + model_width + 128]
    small_full = small_full.reshape(32, part, 128).astype(jnp.float32)
    vectors = jnp.moveaxis(small_full[:, :8, :part], 1, 0).reshape(8, model_width)
    up_shift = small_full[:, 8, :inner_part].reshape(1, 32 * inner_part)
    vectors, up_shift = lax.optimization_barrier((vectors, up_shift))
    query_shift, value_shift, out_shift, gain_one, shift_one, down_shift, gain_two, shift_two = (
        vectors[position : position + 1] for position in range(8)
    )
    mixed = jnp.concatenate(
        [
            jnp.dot(flat_rows, attn_a, preferred_element_type=jnp.float32),
            jnp.dot(flat_rows, attn_b[:, :rest], preferred_element_type=jnp.float32),
        ],
        1,
    )
    queries = ((mixed[:, :model_width] + query_shift) * 0.125).astype(jnp.bfloat16)
    queries = queries.reshape(slot_count, row_count, model_width)
    keys_own = (
        mixed[:, model_width : 2 * model_width]
        .astype(jnp.bfloat16)
        .reshape(slot_count, row_count, model_width)
    )
    values_own = (
        (mixed[:, 2 * model_width :] + value_shift)
        .astype(jnp.bfloat16)
        .reshape(slot_count, row_count, model_width)
    )

    places_shape = (8, slot_count, row_count, model_width)
    key_all, value_all = (part.reshape(places_shape) for part in gather_plane(keys_own, values_own))
    context, logsum = attention_call(
        attend_kernel, slot_lengths, (queries, key_all, value_all), False
    )
    context_flat = context.reshape(slot_count * row_count, model_width)
    attn_out = jnp.dot(context_flat, out_full, preferred_element_type=jnp.float32) + out_shift
    resid_one = flat_rows.astype(jnp.float32) + attn_out
    hidden_one = norm_rows(resid_one, gain_one, shift_one)
    hidden_low = hidden_one.astype(jnp.bfloat16)
    inner_act = jnp.dot(hidden_low, up_full, preferred_element_type=jnp.float32) + up_shift
    activated = gelu_exact(inner_act).astype(jnp.bfloat16)
    ffn_out = jnp.dot(activated, down_full, preferred_element_type=jnp.float32) + down_shift
    resid_two = hidden_one + ffn_out
    layer_out = norm_rows(resid_two, gain_two, shift_two)
    layer_out = layer_out.astype(jnp.bfloat16).reshape(slot_count, row_count, model_width)
    positions = lax.axis_index("seq") * row_count + jnp.arange(row_count)
    live_rows = (positions[None, :] < slot_lengths[:, None]).astype(jnp.float32)
    cotangent = (out_cotangent.astype(jnp.float32) * live_rows[:, :, None]).reshape(
        slot_count * row_count, model_width
    )
    _, norm_back_two = jax.vjp(norm_rows, resid_two, gain_two, shift_two)
    d_resid_two, d_gain_two, d_shift_two = norm_back_two(cotangent)
    d_ffn = d_resid_two.astype(jnp.bfloat16)
    d_down = contract_rows(activated, d_ffn).astype(jnp.bfloat16)
    d_down_shift = jnp.sum(d_ffn.astype(jnp.float32), 0)
    d_activated = contract_last(d_ffn, down_full)
    _, gelu_back = jax.vjp(gelu_exact, inner_act)
    d_inner = gelu_back(d_activated)[0].astype(jnp.bfloat16)
    d_up = contract_rows(hidden_low, d_inner).astype(jnp.bfloat16)
    d_up, d_down = scatter_plane(place_blocks(d_up), place_blocks(d_down))
    d_up_terms, d_down_terms = (scatter_line(part_sum) for part_sum in (d_up, d_down))
    d_up_shift = jnp.sum(d_inner.astype(jnp.float32), 0)
    d_hidden = contract_last(d_inner, up_full) + d_resid_two
    _, norm_back_one = jax.vjp(norm_rows, resid_one, gain_one, shift_one)
    d_resid_one, d_gain_one, d_shift_one = norm_back_one(d_hidden)
    d_attn = d_resid_one.astype(jnp.bfloat16)
    d_out = contract_rows(context_flat, d_attn).astype(jnp.bfloat16)
    d_out_shift = jnp.sum(d_attn.astype(jnp.float32), 0)
    d_context = contract_last(d_attn, out_full).astype(jnp.bfloat16)
    d_query, d_key_part, d_value_part = attention_call(
        attend_back_kernel,
        slot_lengths,
        (
            queries,
            d_context.reshape(slot_count, row_count, model_width),
            key_all,
            value_all,
            logsum,
        ),
        True,
    )
    d_key_low, d_value_low = scatter_plane(
        d_key_part.reshape((2, 2, 2) + places_shape[1:]),
        d_value_part.reshape((2, 2, 2) + places_shape[1:]),
    )
    d_query_pre = d_query.reshape(slot_count * row_count, model_width)
    d_key_low = d_key_low.reshape(slot_count * row_count, model_width)
    d_value_low = d_value_low.reshape(slot_count * row_count, model_width)
    d_mixed = jnp.concatenate([d_query_pre, d_key_low, d_value_low], 1)
    d_attn_a = contract_rows(flat_rows, d_mixed[:, :half]).astype(jnp.bfloat16)
    d_attn_b = contract_rows(flat_rows, d_mixed[:, half:]).astype(jnp.bfloat16)
    d_query_shift = jnp.sum(d_query_pre.astype(jnp.float32), 0)
    d_value_shift = jnp.sum(d_value_low.astype(jnp.float32), 0)
    tokens_grad = (
        (
            d_resid_one
            + contract_last(d_mixed[:, :half], attn_a)
            + contract_last(d_mixed[:, half:], attn_b[:, :rest])
        )
        .astype(jnp.bfloat16)
        .reshape(slot_count, row_count, model_width)
    )
    small_grads = jnp.concatenate(
        [
            grad.reshape(1, model_width)
            for grad in (
                d_query_shift,
                d_value_shift,
                d_out_shift,
                d_gain_one,
                d_shift_one,
                d_down_shift,
                d_gain_two,
                d_shift_two,
            )
        ]
    ).astype(jnp.bfloat16)
    small_grads = jnp.moveaxis(small_grads.reshape(8, 32, part), 0, 1)
    inner_grads = d_up_shift.astype(jnp.bfloat16).reshape(32, 1, inner_part)
    small_grads = jnp.concatenate(
        [
            jnp.pad(small_grads, ((0, 0), (0, 0), (0, 256 - part))),
            jnp.pad(inner_grads, ((0, 0), (0, part - 9), (0, 256 - inner_part))),
        ],
        1,
    ).reshape(32 * part, 256)
    grad_a, grad_b = scatter_plane(
        place_blocks(d_attn_a), place_blocks(jnp.concatenate([d_attn_b, d_out, small_grads], 1))
    )
    sum_a = line_total(scatter_line(grad_a))
    sum_b = line_total(scatter_line(grad_b))
    d_up = line_total(after(d_up_terms, grad_a))
    d_down = line_total(after(d_down_terms, grad_a))
    own = sum_b[:, rest + model_width : rest + model_width + 128]
    vectors = [own[position, :part] for position in range(8)]
    return (
        layer_out,
        tokens_grad,
        jnp.concatenate([sum_a, sum_b[:, :rest]], 1),
        vectors[0],
        vectors[1],
        sum_b[:, rest : rest + model_width],
        vectors[2],
        vectors[3],
        vectors[4],
        d_up,
        own[8, :inner_part],
        d_down,
        vectors[5],
        vectors[6],
        vectors[7],
    )


def contract_first(left, right):
    return lax.dot_general(
        left, right, (((0,), (0,)), ((), ())), preferred_element_type=jnp.float32
    )


def pair_lanes(value):
    low_half = lax.broadcasted_iota(jnp.int32, value.shape, 1) < value.shape[1] // 2
    zero = jnp.zeros_like(value)
    return low_half, (jnp.where(low_half, value, zero), jnp.where(low_half, zero, value))


def live_scores(keys, query, length):
    scores = contract_last(keys, query)
    places = lax.broadcasted_iota(jnp.int32, scores.shape, 0)
    return jnp.where(places < length, scores, NEG_FILL)


def attend_kernel(lengths, query_ref, key_ref, value_ref, context_ref, logsum_ref):
    length = lengths[pl.program_id(0)]
    lanes = query_ref.shape[-1]
    keys = key_ref[...].reshape(-1, lanes)
    values = value_ref[...].reshape(-1, lanes)
    low_half, query_pair = pair_lanes(query_ref[0])
    outs = []
    for head, query in enumerate(query_pair):
        scores = live_scores(keys, query, length)
        row_max = jnp.max(scores, 0, keepdims=True)
        weights = jnp.exp(scores - row_max)
        total = jnp.sum(weights, 0, keepdims=True)
        logsum_ref[0, 0, head : head + 1, :] = row_max + jnp.log(total)
        probs_low = (weights * (1.0 / total)).astype(jnp.bfloat16)
        outs.append(contract_first(probs_low, values))
    context_ref[0] = jnp.where(low_half, outs[0], outs[1]).astype(jnp.bfloat16)


def attend_back_kernel(
    lengths,
    query_ref,
    d_context_ref,
    key_ref,
    value_ref,
    logsum_ref,
    d_query_ref,
    d_key_ref,
    d_value_ref,
):
    length = lengths[pl.program_id(0)]
    lanes = query_ref.shape[-1]
    keys = key_ref[...].reshape(-1, lanes)
    values = value_ref[...].reshape(-1, lanes)
    low_half, query_pair = pair_lanes(query_ref[0])
    _, d_context_pair = pair_lanes(d_context_ref[0])
    d_query_pair, d_keys, d_values = [], [], []
    for head in range(2):
        query, d_context = query_pair[head], d_context_pair[head]
        scores = live_scores(keys, query, length)
        probs = jnp.exp(scores - logsum_ref[0, 0, head : head + 1, :])
        d_probs = contract_last(values, d_context)
        prob_delta = jnp.sum(probs * d_probs, 0, keepdims=True)
        d_scores = (probs * (d_probs - prob_delta)).astype(jnp.bfloat16)
        d_query_pair.append(contract_first(d_scores, keys))
        d_keys.append(jnp.dot(d_scores, query, preferred_element_type=jnp.float32))
        d_values.append(
            jnp.dot(probs.astype(jnp.bfloat16), d_context, preferred_element_type=jnp.float32)
        )
    d_query = jnp.where(low_half, d_query_pair[0], d_query_pair[1]).astype(jnp.bfloat16)
    d_query_ref[0] = d_query * jnp.asarray(0.125, jnp.bfloat16)
    d_key_ref[...] = (d_keys[0] + d_keys[1]).astype(jnp.bfloat16).reshape(d_key_ref.shape)
    d_value_ref[...] = (d_values[0] + d_values[1]).astype(jnp.bfloat16).reshape(d_value_ref.shape)


def attention_call(kernel, slot_lengths, operands, backward):
    queries, keys = operands[0], operands[2 if backward else 1]
    slot_count, row_count, width = queries.shape
    place_count, lanes = keys.shape[0], 128
    pairs = width // lanes
    row_spec = pl.BlockSpec((1, row_count, lanes), lambda s, p, _: (s, 0, p))
    key_spec = pl.BlockSpec((place_count, 1, row_count, lanes), lambda s, p, _: (0, s, 0, p))
    stat_spec = pl.BlockSpec((1, 1, 8, row_count), lambda s, p, _: (s, p, 0, 0))
    low_rows = jax.ShapeDtypeStruct(queries.shape, jnp.bfloat16)
    low_keys = jax.ShapeDtypeStruct(keys.shape, jnp.bfloat16)
    stats = jax.ShapeDtypeStruct((slot_count, pairs, 8, row_count), jnp.float32)
    products = 5 if backward else 2
    scores = 2 * slot_count * pairs * row_count * place_count * row_count
    return pl.pallas_call(
        kernel,
        out_shape=(low_rows, low_keys, low_keys) if backward else (low_rows, stats),
        grid_spec=pltpu.PrefetchScalarGridSpec(
            num_scalar_prefetch=1,
            grid=(slot_count, pairs),
            in_specs=(
                [row_spec, row_spec, key_spec, key_spec, stat_spec]
                if backward
                else [row_spec, key_spec, key_spec]
            ),
            out_specs=[row_spec, key_spec, key_spec] if backward else [row_spec, stat_spec],
        ),
        cost_estimate=pl.CostEstimate(
            flops=products * 8 * scores * lanes,
            bytes_accessed=products * 2 * place_count * slot_count * row_count * width,
            transcendentals=scores,
        ),
    )(slot_lengths, *operands)


def solution(mesh):
    fast = mesh.shape["seq"] == 8 and mesh.shape["slot"] == 4
    return jax.shard_map(
        body_fast if fast else body,
        mesh=mesh,
        in_specs=(
            P("slot", "seq", None),
            P(("seq", "slot"), None),
            P(("seq", "slot")),
            P(("seq", "slot")),
            P(("seq", "slot"), None),
            P(("seq", "slot")),
            P(("seq", "slot")),
            P(("seq", "slot")),
            P(("seq", "slot"), None),
            P(("seq", "slot")),
            P(("seq", "slot"), None),
            P(("seq", "slot")),
            P(("seq", "slot")),
            P(("seq", "slot")),
            P("slot"),
            P("slot", "seq", None),
        ),
        out_specs=(
            P("slot", "seq", None),
            P("slot", "seq", None),
            P(("seq", "slot"), None),
            P(("seq", "slot")),
            P(("seq", "slot")),
            P(("seq", "slot"), None),
            P(("seq", "slot")),
            P(("seq", "slot")),
            P(("seq", "slot")),
            P(("seq", "slot"), None),
            P(("seq", "slot")),
            P(("seq", "slot"), None),
            P(("seq", "slot")),
            P(("seq", "slot")),
            P(("seq", "slot")),
        ),
        check_vma=False,
    )
```

```python
import jax
import jax.numpy as jnp
from jax import lax
from jax.experimental import pallas as pl
from jax.experimental.pallas import tpu as pltpu
from jax.sharding import PartitionSpec as P

HEADS = 12


NEG_FILL = -1e30
EPSILON = 1e-05


def norm_rows(resid, gain, shift):
    centre = resid - jnp.mean(resid, -1, keepdims=True)
    spread = jnp.mean(centre * centre, -1, keepdims=True)
    return centre * lax.rsqrt(spread + EPSILON) * gain + shift


def gelu_exact(inner_act):
    return jax.nn.gelu(inner_act, approximate=False)


def contract_rows(left, right):
    return lax.dot_general(
        left, right, (((0,), (0,)), ((), ())), preferred_element_type=jnp.float32
    )


def contract_last(left, right):
    return lax.dot_general(
        left, right, (((1,), (1,)), ((), ())), preferred_element_type=jnp.float32
    )


def split_heads(rows_in, head_count):
    return rows_in.reshape(
        rows_in.shape[0], rows_in.shape[1], head_count, rows_in.shape[2] // head_count
    )


def take_block(whole, position, block_size, axis_dim):
    return lax.dynamic_slice_in_dim(whole, position * block_size, block_size, axis_dim)


def masked_scores(queries, key_rows, key_start, slot_lengths):
    scores = jnp.einsum("sqhd,skhd->shqk", queries, key_rows, preferred_element_type=jnp.float32)
    key_places = key_start + jnp.arange(key_rows.shape[1])
    live_keys = key_places[None, :] < slot_lengths[:, None]
    return jnp.where(live_keys[:, None, None, :], scores, NEG_FILL)


def log_totals(queries, key_all, slot_lengths, block_size, head_count):
    block_count = key_all.shape[1] // block_size
    stat_shape = (queries.shape[0], head_count, queries.shape[1])

    def log_step_fn(carried, position):
        running_max, running_sum = carried
        key_rows = split_heads(take_block(key_all, position, block_size, 1), head_count)
        scores = masked_scores(queries, key_rows, position * block_size, slot_lengths)
        new_max = jnp.maximum(running_max, jnp.max(scores, -1))
        running_sum = running_sum * jnp.exp(running_max - new_max) + jnp.sum(
            jnp.exp(scores - new_max[..., None]), -1
        )
        return ((new_max, running_sum), None)

    start_state = (jnp.full(stat_shape, NEG_FILL, jnp.float32), jnp.zeros(stat_shape, jnp.float32))
    (running_max, running_sum), _ = lax.scan(log_step_fn, start_state, jnp.arange(block_count))
    return running_max + jnp.log(running_sum)


def attend(queries, key_all, value_all, slot_lengths, logsum, block_size, head_count):
    block_count = key_all.shape[1] // block_size

    def attend_step_fn(context, position):
        key_rows = split_heads(take_block(key_all, position, block_size, 1), head_count)
        value_rows = split_heads(take_block(value_all, position, block_size, 1), head_count)
        scores = masked_scores(queries, key_rows, position * block_size, slot_lengths)
        weights_low = jnp.exp(scores - logsum[..., None]).astype(jnp.bfloat16)
        return (
            context
            + jnp.einsum(
                "shqk,skhd->sqhd", weights_low, value_rows, preferred_element_type=jnp.float32
            ),
            None,
        )

    context, _ = lax.scan(
        attend_step_fn, jnp.zeros(queries.shape, jnp.float32), jnp.arange(block_count)
    )
    return context


def prob_grad_totals(
    queries, d_context, key_all, value_all, slot_lengths, logsum, block_size, head_count
):
    block_count = key_all.shape[1] // block_size

    def prob_step_fn(prob_delta, position):
        key_rows = split_heads(take_block(key_all, position, block_size, 1), head_count)
        value_rows = split_heads(take_block(value_all, position, block_size, 1), head_count)
        scores = masked_scores(queries, key_rows, position * block_size, slot_lengths)
        softmax_rows = jnp.exp(scores - logsum[..., None])
        d_probs = jnp.einsum(
            "sqhd,skhd->shqk", d_context, value_rows, preferred_element_type=jnp.float32
        )
        return (prob_delta + jnp.sum(softmax_rows * d_probs, -1), None)

    prob_delta, _ = lax.scan(
        prob_step_fn, jnp.zeros(logsum.shape, jnp.float32), jnp.arange(block_count)
    )
    return prob_delta


def key_side(
    queries, d_context, key_all, value_all, slot_lengths, logsum, prob_delta, block_size, head_count
):
    block_count = key_all.shape[1] // block_size

    def key_step_fn(d_query, position):
        key_rows = split_heads(take_block(key_all, position, block_size, 1), head_count)
        value_rows = split_heads(take_block(value_all, position, block_size, 1), head_count)
        scores = masked_scores(queries, key_rows, position * block_size, slot_lengths)
        softmax_rows = jnp.exp(scores - logsum[..., None])
        d_probs = jnp.einsum(
            "sqhd,skhd->shqk", d_context, value_rows, preferred_element_type=jnp.float32
        )
        d_scores = (softmax_rows * (d_probs - prob_delta[..., None])).astype(jnp.bfloat16)
        d_query = d_query + jnp.einsum(
            "shqk,skhd->sqhd", d_scores, key_rows, preferred_element_type=jnp.float32
        )
        d_key_rows = jnp.einsum(
            "shqk,sqhd->skhd", d_scores, queries, preferred_element_type=jnp.float32
        )
        d_value_rows = jnp.einsum(
            "shqk,sqhd->skhd",
            softmax_rows.astype(jnp.bfloat16),
            d_context,
            preferred_element_type=jnp.float32,
        )
        return (d_query, (d_key_rows, d_value_rows))

    return lax.scan(key_step_fn, jnp.zeros(queries.shape, jnp.float32), jnp.arange(block_count))


ALL_AXES = ("seq", "slot")


def flip_pairs(mask):
    return [((q * 4 + z), ((q ^ mask) * 4 + z)) for q in range(8) for z in range(4)]


def turn_pairs(step):
    return [((q * 4 + z), (q * 4 + (z + step) % 4)) for q in range(8) for z in range(4)]


CORE, X_AXIS, Y_AXIS = 1, 2, 4


def flip(value, mask):
    return lax.ppermute(value, ALL_AXES, flip_pairs(mask))


def turn(value, step):
    return lax.ppermute(value, ALL_AXES, turn_pairs(step))


def places():
    q = lax.axis_index("seq")
    return q & 1, (q >> 1) & 1, q >> 2, lax.axis_index("slot")


def merge(own, other, bit, axis):
    first = jnp.where(bit == 0, own, other)
    second = jnp.where(bit == 0, other, own)
    return jnp.stack([first, second], axis)


def plane_one(a, b):
    _, _, _, _ = places()
    a1, b1 = flip(a, X_AXIS), flip(b, Y_AXIS)
    return a1, b1


def plane_two(a, b, got):
    _, x, y, _ = places()
    a, b = merge(a, got[0], x, 0), merge(b, got[1], y, 0)
    return a, b, flip(a, Y_AXIS), flip(b, X_AXIS)


def plane_core(a, b, a2, b2):
    core, x, y, _ = places()
    a, b = merge(a, a2, y, 0), merge(b, b2, x, 1)
    a3, b3 = flip(a, CORE), flip(b, CORE)
    return merge(a, a3, core, 2), merge(b, b3, core, 2)


def after(value, ready):
    return lax.optimization_barrier((value, ready))[0]


def line_turns(shard):
    return tuple(turn(shard, step) for step in (1, 2, 3))


def line_blocks(shard, got):
    ring = [shard, got[2], got[1], got[0]]
    start = (4 - places()[3]) % 4
    return lax.dynamic_slice_in_dim(jnp.stack(ring + ring[:3]), start, 4, 0)


def as_matrix(parts):
    return parts.reshape(32 * parts.shape[-2], parts.shape[-1])


def pick(value, index, axis):
    return lax.dynamic_index_in_dim(value, index, axis, keepdims=False)


def choose(value, bit, axis):
    first = lax.index_in_dim(value, 0, axis, keepdims=False)
    return jnp.where(bit == 0, first, lax.index_in_dim(value, 1, axis, keepdims=False))


def add_low(left, right):
    return (left.astype(jnp.float32) + right.astype(jnp.float32)).astype(jnp.bfloat16)


def fold(value, bit, mask, axis):
    return add_low(choose(value, bit, axis), flip(choose(value, 1 - bit, axis), mask))


def core_fold(parts):
    core = places()[0]
    return tuple(fold(part, core, CORE, 2) for part in parts)


def core_fold_split(keep, send):
    return add_low(keep, flip(send, CORE))


def plane_fold(a, b):
    _, x, y, _ = places()
    a, b = fold(a, y, Y_AXIS, 0), fold(b, x, X_AXIS, 1)
    return fold(a, x, X_AXIS, 0), fold(b, y, Y_AXIS, 0)


def scatter_line(part):
    z = places()[3]
    return [pick(part, z, 0)] + [turn(pick(part, (z + step) % 4, 0), step) for step in (1, 2, 3)]


def line_total(terms):
    return sum(term.astype(jnp.float32) for term in terms)


def place_blocks(part):
    return part.reshape(2, 2, 2, 4, part.shape[0] // 32, part.shape[1])


def body(
    tokens,
    qkv_weight,
    query_bias,
    value_bias,
    out_weight,
    out_bias,
    norm1_gain,
    norm1_shift,
    up_weight,
    up_bias,
    down_weight,
    down_bias,
    norm2_gain,
    norm2_shift,
    slot_lengths,
    out_cotangent,
):
    slot_count, row_count, model_width = tokens.shape
    head_count = HEADS
    flat_rows = tokens.reshape(slot_count * row_count, model_width)
    attn_set = (
        lax.all_gather(qkv_weight, ("seq", "slot"), axis=0, tiled=True),
        lax.all_gather(out_weight, ("seq", "slot"), axis=0, tiled=True),
        lax.all_gather(query_bias, ("seq", "slot"), axis=0, tiled=True),
        lax.all_gather(value_bias, ("seq", "slot"), axis=0, tiled=True),
        lax.all_gather(out_bias, ("seq", "slot"), axis=0, tiled=True),
        lax.all_gather(norm1_gain, ("seq", "slot"), axis=0, tiled=True),
        lax.all_gather(norm1_shift, ("seq", "slot"), axis=0, tiled=True),
    )
    qkv_full, out_full, query_shift, value_shift, out_shift, gain_one, shift_one = attn_set
    mixed = jnp.dot(flat_rows, qkv_full, preferred_element_type=jnp.float32)
    queries = ((mixed[:, :model_width] + query_shift.astype(jnp.float32)) * 0.125).astype(
        jnp.bfloat16
    )
    queries = split_heads(queries.reshape(slot_count, row_count, model_width), head_count)
    keys_own = (
        mixed[:, model_width : 2 * model_width]
        .astype(jnp.bfloat16)
        .reshape(slot_count, row_count, model_width)
    )
    values_own = (
        (mixed[:, 2 * model_width :] + value_shift.astype(jnp.float32))
        .astype(jnp.bfloat16)
        .reshape(slot_count, row_count, model_width)
    )
    key_all, value_all = (
        lax.all_gather(keys_own, "seq", axis=1, tiled=True),
        lax.all_gather(values_own, "seq", axis=1, tiled=True),
    )
    length_all = key_all.shape[1]
    block_size = min(512, length_all)
    logsum = log_totals(queries, key_all, slot_lengths, block_size, head_count)
    context = attend(
        queries, key_all, value_all, slot_lengths, logsum, block_size, head_count
    ).astype(jnp.bfloat16)
    context_flat = context.reshape(slot_count * row_count, model_width)
    attn_out = jnp.dot(
        context_flat, out_full, preferred_element_type=jnp.float32
    ) + out_shift.astype(jnp.float32)
    resid_one = flat_rows.astype(jnp.float32) + attn_out
    hidden_one = norm_rows(resid_one, gain_one.astype(jnp.float32), shift_one.astype(jnp.float32))
    hidden_low = hidden_one.astype(jnp.bfloat16)
    ffn_set = (
        lax.all_gather(up_weight, ("seq", "slot"), axis=0, tiled=True),
        lax.all_gather(down_weight, ("seq", "slot"), axis=0, tiled=True),
        lax.all_gather(up_bias, ("seq", "slot"), axis=0, tiled=True),
        lax.all_gather(down_bias, ("seq", "slot"), axis=0, tiled=True),
        lax.all_gather(norm2_gain, ("seq", "slot"), axis=0, tiled=True),
        lax.all_gather(norm2_shift, ("seq", "slot"), axis=0, tiled=True),
    )
    up_full, down_full, up_shift, down_shift, gain_two, shift_two = ffn_set
    inner_act = jnp.dot(hidden_low, up_full, preferred_element_type=jnp.float32) + up_shift.astype(
        jnp.float32
    )
    activated = gelu_exact(inner_act).astype(jnp.bfloat16)
    ffn_out = jnp.dot(activated, down_full, preferred_element_type=jnp.float32) + down_shift.astype(
        jnp.float32
    )
    resid_two = hidden_one + ffn_out
    layer_out = norm_rows(resid_two, gain_two.astype(jnp.float32), shift_two.astype(jnp.float32))
    layer_out = layer_out.astype(jnp.bfloat16).reshape(slot_count, row_count, model_width)
    qkv_back, out_back, _, _, _, gain_one_back, shift_one_back = (
        lax.all_gather(qkv_weight, ("seq", "slot"), axis=0, tiled=True),
        lax.all_gather(out_weight, ("seq", "slot"), axis=0, tiled=True),
        lax.all_gather(query_bias, ("seq", "slot"), axis=0, tiled=True),
        lax.all_gather(value_bias, ("seq", "slot"), axis=0, tiled=True),
        lax.all_gather(out_bias, ("seq", "slot"), axis=0, tiled=True),
        lax.all_gather(norm1_gain, ("seq", "slot"), axis=0, tiled=True),
        lax.all_gather(norm1_shift, ("seq", "slot"), axis=0, tiled=True),
    )
    up_back, down_back, _, _, gain_two_back, shift_two_back = (
        lax.all_gather(up_weight, ("seq", "slot"), axis=0, tiled=True),
        lax.all_gather(down_weight, ("seq", "slot"), axis=0, tiled=True),
        lax.all_gather(up_bias, ("seq", "slot"), axis=0, tiled=True),
        lax.all_gather(down_bias, ("seq", "slot"), axis=0, tiled=True),
        lax.all_gather(norm2_gain, ("seq", "slot"), axis=0, tiled=True),
        lax.all_gather(norm2_shift, ("seq", "slot"), axis=0, tiled=True),
    )
    positions = lax.axis_index("seq") * row_count + jnp.arange(row_count)
    live_rows = (positions[None, :] < slot_lengths[:, None]).astype(jnp.float32)
    cotangent = (out_cotangent.astype(jnp.float32) * live_rows[:, :, None]).reshape(
        slot_count * row_count, model_width
    )
    _, norm_back_two = jax.vjp(
        norm_rows, resid_two, gain_two_back.astype(jnp.float32), shift_two_back.astype(jnp.float32)
    )
    d_resid_two, d_gain_two, d_shift_two = norm_back_two(cotangent)
    d_ffn = d_resid_two.astype(jnp.bfloat16)
    d_down = contract_rows(activated, d_ffn)
    d_down_shift = jnp.sum(d_ffn.astype(jnp.float32), 0)
    d_activated = contract_last(d_ffn, down_back)
    _, gelu_back = jax.vjp(gelu_exact, inner_act)
    d_inner = gelu_back(d_activated)[0].astype(jnp.bfloat16)
    d_up = contract_rows(hidden_low, d_inner)
    d_up_shift = jnp.sum(d_inner.astype(jnp.float32), 0)
    d_hidden = contract_last(d_inner, up_back) + d_resid_two
    _, norm_back_one = jax.vjp(
        norm_rows, resid_one, gain_one_back.astype(jnp.float32), shift_one_back.astype(jnp.float32)
    )
    d_resid_one, d_gain_one, d_shift_one = norm_back_one(d_hidden)
    d_attn = d_resid_one.astype(jnp.bfloat16)
    d_out = contract_rows(context_flat, d_attn)
    d_out_shift = jnp.sum(d_attn.astype(jnp.float32), 0)
    d_context = contract_last(d_attn, out_back).astype(jnp.bfloat16)
    d_context = split_heads(d_context.reshape(slot_count, row_count, model_width), head_count)
    prob_delta = prob_grad_totals(
        queries, d_context, key_all, value_all, slot_lengths, logsum, block_size, head_count
    )
    d_query, key_parts = key_side(
        queries,
        d_context,
        key_all,
        value_all,
        slot_lengths,
        logsum,
        prob_delta,
        block_size,
        head_count,
    )
    d_key_part = jnp.moveaxis(key_parts[0], 0, 1).reshape(slot_count, length_all, model_width)
    d_value_part = jnp.moveaxis(key_parts[1], 0, 1).reshape(slot_count, length_all, model_width)
    d_key_sum, d_value_sum = (
        lax.psum_scatter(
            d_key_part.astype(jnp.bfloat16), "seq", scatter_dimension=1, tiled=True
        ).astype(jnp.float32),
        lax.psum_scatter(
            d_value_part.astype(jnp.bfloat16), "seq", scatter_dimension=1, tiled=True
        ).astype(jnp.float32),
    )
    d_query_pre = d_query.astype(jnp.bfloat16).reshape(
        slot_count * row_count, model_width
    ) * jnp.asarray(0.125, jnp.bfloat16)
    d_key_low = d_key_sum.astype(jnp.bfloat16).reshape(slot_count * row_count, model_width)
    d_value_low = d_value_sum.astype(jnp.bfloat16).reshape(slot_count * row_count, model_width)
    d_mixed = jnp.concatenate([d_query_pre, d_key_low, d_value_low], 1)
    d_qkv = contract_rows(flat_rows, d_mixed)
    d_query_shift = jnp.sum(d_query_pre.astype(jnp.float32), 0)
    d_value_shift = jnp.sum(d_value_low.astype(jnp.float32), 0)
    tokens_grad = (
        (d_resid_one + contract_last(d_mixed, qkv_back))
        .astype(jnp.bfloat16)
        .reshape(slot_count, row_count, model_width)
    )
    attn_sums = (
        lax.psum_scatter(d_qkv, ("seq", "slot"), scatter_dimension=0, tiled=True),
        lax.psum_scatter(d_out, ("seq", "slot"), scatter_dimension=0, tiled=True),
        lax.psum_scatter(d_query_shift, ("seq", "slot"), scatter_dimension=0, tiled=True),
        lax.psum_scatter(d_value_shift, ("seq", "slot"), scatter_dimension=0, tiled=True),
        lax.psum_scatter(d_out_shift, ("seq", "slot"), scatter_dimension=0, tiled=True),
        lax.psum_scatter(d_gain_one, ("seq", "slot"), scatter_dimension=0, tiled=True),
        lax.psum_scatter(d_shift_one, ("seq", "slot"), scatter_dimension=0, tiled=True),
    )
    ffn_sums = (
        lax.psum_scatter(d_up, ("seq", "slot"), scatter_dimension=0, tiled=True),
        lax.psum_scatter(d_down, ("seq", "slot"), scatter_dimension=0, tiled=True),
        lax.psum_scatter(d_up_shift, ("seq", "slot"), scatter_dimension=0, tiled=True),
        lax.psum_scatter(d_down_shift, ("seq", "slot"), scatter_dimension=0, tiled=True),
        lax.psum_scatter(d_gain_two, ("seq", "slot"), scatter_dimension=0, tiled=True),
        lax.psum_scatter(d_shift_two, ("seq", "slot"), scatter_dimension=0, tiled=True),
    )
    return (
        layer_out,
        tokens_grad,
        attn_sums[0],
        attn_sums[2],
        attn_sums[3],
        attn_sums[1],
        attn_sums[4],
        attn_sums[5],
        attn_sums[6],
        ffn_sums[0],
        ffn_sums[2],
        ffn_sums[1],
        ffn_sums[3],
        ffn_sums[4],
        ffn_sums[5],
    )


def body_fast(
    tokens,
    qkv_weight,
    query_bias,
    value_bias,
    out_weight,
    out_bias,
    norm1_gain,
    norm1_shift,
    up_weight,
    up_bias,
    down_weight,
    down_bias,
    norm2_gain,
    norm2_shift,
    slot_lengths,
    out_cotangent,
):
    slot_count, row_count, model_width = tokens.shape
    part = qkv_weight.shape[0]
    inner_part = up_bias.shape[0]
    flat_rows = tokens.reshape(slot_count * row_count, model_width)
    small = jnp.stack(
        [
            query_bias,
            value_bias,
            out_bias,
            norm1_gain,
            norm1_shift,
            down_bias,
            norm2_gain,
            norm2_shift,
        ]
    )
    small = jnp.concatenate(
        [
            jnp.pad(small, ((0, 0), (0, 256 - part))),
            jnp.pad(up_bias[None], ((0, part - 9), (0, 256 - inner_part))),
        ]
    )
    attn_shard = jnp.concatenate([qkv_weight, out_weight, small], 1)
    attn_line = line_blocks(attn_shard, line_turns(attn_shard))
    half = attn_line.shape[-1] // 2
    rest = 3 * model_width - half
    attn_halves = attn_line[..., :half], attn_line[..., half:]
    stack_count = down_weight.shape[0] // part
    ffn_shard = jnp.concatenate(
        [up_weight] + [down_weight[k * part : (k + 1) * part] for k in range(stack_count)], 1
    )
    ffn_shard = after(ffn_shard, attn_line)
    ffn_got = line_turns(ffn_shard)
    attn_halves = plane_two(*attn_halves, plane_one(*attn_halves))
    ffn_line = line_blocks(ffn_shard, ffn_got)
    ff_width = up_weight.shape[1]
    down_line = [
        ffn_line[..., ff_width + k * model_width : ff_width + (k + 1) * model_width]
        for k in range(stack_count)
    ]
    ffn_halves = ffn_line[..., :ff_width], jnp.concatenate(down_line, 1)
    ffn_one = plane_one(*ffn_halves)
    attn_a, attn_b = (as_matrix(parts) for parts in plane_core(*attn_halves))
    out_full = attn_b[:, rest : rest + model_width]
    small_full = attn_b[:, rest + model_width : rest + model_width + 128]
    small_full = small_full.reshape(32, part, 128).astype(jnp.float32)
    vectors = jnp.moveaxis(small_full[:, :8, :part], 1, 0).reshape(8, model_width)
    up_shift = small_full[:, 8, :inner_part].reshape(1, 32 * inner_part)
    vectors, up_shift = lax.optimization_barrier((vectors, up_shift))
    query_shift, value_shift, out_shift, gain_one, shift_one, down_shift, gain_two, shift_two = (
        vectors[position : position + 1] for position in range(8)
    )
    mixed_a = jnp.dot(flat_rows, attn_a, preferred_element_type=jnp.float32)
    mixed_b = jnp.dot(flat_rows, attn_b[:, :rest], preferred_element_type=jnp.float32)
    mixed = jnp.concatenate([mixed_a, mixed_b], 1)
    queries = ((mixed[:, :model_width] + query_shift) * 0.125).astype(jnp.bfloat16)
    queries = queries.reshape(slot_count, row_count, model_width)
    keys_own = (
        mixed[:, model_width : 2 * model_width]
        .astype(jnp.bfloat16)
        .reshape(slot_count, row_count, model_width)
    )
    values_own = (
        (mixed[:, 2 * model_width :] + value_shift)
        .astype(jnp.bfloat16)
        .reshape(slot_count, row_count, model_width)
    )

    places_shape = (8, slot_count, row_count, model_width)
    kept = plane_two(keys_own, values_own, plane_one(keys_own, values_own))
    ffn_halves = plane_two(*ffn_halves, ffn_one)
    key_all, value_all = (part.reshape(places_shape) for part in plane_core(*kept))
    up_full, down_full = (as_matrix(parts) for parts in plane_core(*ffn_halves))
    context, logsum = attention_call(
        attend_kernel, slot_lengths, (queries, key_all, value_all), False
    )
    context_flat = context.reshape(slot_count * row_count, model_width)
    attn_out = jnp.dot(context_flat, out_full, preferred_element_type=jnp.float32) + out_shift
    resid_one = flat_rows.astype(jnp.float32) + attn_out
    hidden_one = norm_rows(resid_one, gain_one, shift_one)
    hidden_low = hidden_one.astype(jnp.bfloat16)
    inner_act = jnp.dot(hidden_low, up_full, preferred_element_type=jnp.float32) + up_shift
    activated = gelu_exact(inner_act).astype(jnp.bfloat16)
    ffn_out = jnp.dot(activated, down_full, preferred_element_type=jnp.float32) + down_shift
    resid_two = hidden_one + ffn_out
    layer_out = norm_rows(resid_two, gain_two, shift_two)
    layer_out = layer_out.astype(jnp.bfloat16).reshape(slot_count, row_count, model_width)
    positions = lax.axis_index("seq") * row_count + jnp.arange(row_count)
    live_rows = (positions[None, :] < slot_lengths[:, None]).astype(jnp.float32)
    cotangent = (out_cotangent.astype(jnp.float32) * live_rows[:, :, None]).reshape(
        slot_count * row_count, model_width
    )
    _, norm_back_two = jax.vjp(norm_rows, resid_two, gain_two, shift_two)
    d_resid_two, d_gain_two, d_shift_two = norm_back_two(cotangent)
    d_ffn = d_resid_two.astype(jnp.bfloat16)
    d_down = contract_rows(activated, d_ffn).astype(jnp.bfloat16)
    d_down_shift = jnp.sum(d_ffn.astype(jnp.float32), 0)
    d_activated = contract_last(d_ffn, down_full)
    _, gelu_back = jax.vjp(gelu_exact, inner_act)
    d_inner = gelu_back(d_activated)[0].astype(jnp.bfloat16)
    d_up = contract_rows(hidden_low, d_inner).astype(jnp.bfloat16)
    d_up, d_down = core_fold((place_blocks(d_up), place_blocks(d_down)))
    d_up, d_down = plane_fold(d_up, d_down)
    d_down = d_down.reshape(4, stack_count, part, model_width)
    ffn_terms = scatter_line(
        jnp.concatenate([d_up] + [d_down[:, k] for k in range(stack_count)], 2)
    )
    d_up_shift = jnp.sum(d_inner.astype(jnp.float32), 0)
    d_hidden = contract_last(d_inner, up_full) + d_resid_two
    _, norm_back_one = jax.vjp(norm_rows, resid_one, gain_one, shift_one)
    d_resid_one, d_gain_one, d_shift_one = norm_back_one(d_hidden)
    d_attn = d_resid_one.astype(jnp.bfloat16)
    d_out_shift = jnp.sum(d_attn.astype(jnp.float32), 0)
    d_context = contract_last(d_attn, out_full).astype(jnp.bfloat16)
    tokens_across, context_across = lax.optimization_barrier((flat_rows.T, context_flat.T))
    d_query, *key_parts = attention_call(
        attend_back_kernel,
        jnp.append(slot_lengths, places()[0]),
        (
            queries,
            d_context.reshape(slot_count, row_count, model_width),
            key_all,
            value_all,
            logsum,
        ),
        True,
    )
    d_key_low, d_value_low = plane_fold(
        core_fold_split(key_parts[0], key_parts[1]).reshape((2, 2) + places_shape[1:]),
        core_fold_split(key_parts[2], key_parts[3]).reshape((2, 2) + places_shape[1:]),
    )
    d_query_pre = d_query.reshape(slot_count * row_count, model_width)
    d_key_low = d_key_low.reshape(slot_count * row_count, model_width)
    d_value_low = d_value_low.reshape(slot_count * row_count, model_width)
    d_mixed = jnp.concatenate([d_query_pre, d_key_low, d_value_low], 1)
    d_query_shift = jnp.sum(d_query_pre.astype(jnp.float32), 0)
    d_value_shift = jnp.sum(d_value_low.astype(jnp.float32), 0)
    tokens_grad = (
        (
            d_resid_one
            + contract_last(d_mixed[:, :half], attn_a)
            + contract_last(d_mixed[:, half:], attn_b[:, :rest])
        )
        .astype(jnp.bfloat16)
        .reshape(slot_count, row_count, model_width)
    )
    row_places = lax.broadcasted_iota(jnp.int32, (8, model_width), 0)
    small_grads = jnp.zeros((8, model_width), jnp.float32)
    for position, grad in enumerate(
        (
            d_query_shift,
            d_value_shift,
            d_out_shift,
            d_gain_one,
            d_shift_one,
            d_down_shift,
            d_gain_two,
            d_shift_two,
        )
    ):
        small_grads = jnp.where(
            row_places == position, grad.reshape(1, model_width), small_grads
        )
    small_grads = lax.optimization_barrier(small_grads.astype(jnp.bfloat16))
    small_grads = jnp.moveaxis(small_grads.reshape(8, 32, part), 0, 1)
    inner_grads = d_up_shift.astype(jnp.bfloat16).reshape(32, 1, inner_part)
    small_grads = jnp.concatenate(
        [
            jnp.pad(small_grads, ((0, 0), (0, 0), (0, 256 - part))),
            jnp.pad(inner_grads, ((0, 0), (0, part - 9), (0, 256 - inner_part))),
        ],
        1,
    ).reshape(32 * part, 256)
    keep, send = attn_products(
        tokens_across,
        d_query_pre,
        d_key_low,
        d_value_low,
        context_across,
        d_attn,
        small_grads,
    )
    grads = core_fold_split(keep, send).reshape(2, 2, 4, part, keep.shape[-1])
    grads = jnp.concatenate(plane_fold(grads[..., :half], grads[..., half:]), 2)
    attn_terms = scatter_line(grads)
    ffn_total = line_total(ffn_terms)
    attn_total = line_total(attn_terms)
    d_up = ffn_total[:, :ff_width]
    d_down = jnp.concatenate(
        [
            ffn_total[:, ff_width + k * model_width : ff_width + (k + 1) * model_width]
            for k in range(stack_count)
        ]
    )
    own = attn_total[:, 4 * model_width : 4 * model_width + 128]
    vectors = [own[position, :part] for position in range(8)]
    return (
        layer_out,
        tokens_grad,
        attn_total[:, : 3 * model_width],
        vectors[0],
        vectors[1],
        attn_total[:, 3 * model_width : 4 * model_width],
        vectors[2],
        vectors[3],
        vectors[4],
        d_up,
        own[8, :inner_part],
        d_down,
        vectors[5],
        vectors[6],
        vectors[7],
    )


def contract_first(left, right):
    return lax.dot_general(
        left, right, (((0,), (0,)), ((), ())), preferred_element_type=jnp.float32
    )


def pair_lanes(value):
    low_half = lax.broadcasted_iota(jnp.int32, value.shape, 1) < value.shape[1] // 2
    zero = jnp.zeros_like(value)
    return low_half, (jnp.where(low_half, value, zero), jnp.where(low_half, zero, value))


def live_scores(keys, query, length):
    scores = contract_last(keys, query)
    places = lax.broadcasted_iota(jnp.int32, scores.shape, 0)
    return jnp.where(places < length, scores, NEG_FILL)


def attend_kernel(lengths, query_ref, key_ref, value_ref, context_ref, logsum_ref):
    length = lengths[pl.program_id(0)]
    lanes = query_ref.shape[-1]
    keys = key_ref[...].reshape(-1, lanes)
    values = value_ref[...].reshape(-1, lanes)
    low_half, query_pair = pair_lanes(query_ref[0])
    outs = []
    for head, query in enumerate(query_pair):
        scores = live_scores(keys, query, length)
        row_max = jnp.max(scores, 0, keepdims=True)
        weights = jnp.exp(scores - row_max)
        total = jnp.sum(weights, 0, keepdims=True)
        logsum_ref[0, 0, head : head + 1, :] = row_max + jnp.log(total)
        probs_low = (weights * (1.0 / total)).astype(jnp.bfloat16)
        outs.append(contract_first(probs_low, values))
    context_ref[0] = jnp.where(low_half, outs[0], outs[1]).astype(jnp.bfloat16)


def attend_back_kernel(
    lengths,
    query_ref,
    d_context_ref,
    key_ref,
    value_ref,
    logsum_ref,
    d_query_ref,
    d_key_keep,
    d_key_send,
    d_value_keep,
    d_value_send,
):
    length = lengths[pl.program_id(0)]
    lanes = query_ref.shape[-1]
    keys = key_ref[...].reshape(-1, lanes)
    values = value_ref[...].reshape(-1, lanes)
    low_half, query_pair = pair_lanes(query_ref[0])
    _, d_context_pair = pair_lanes(d_context_ref[0])
    d_query_pair, d_keys, d_values = [], [], []
    for head in range(2):
        query, d_context = query_pair[head], d_context_pair[head]
        scores = live_scores(keys, query, length)
        probs = jnp.exp(scores - logsum_ref[0, 0, head : head + 1, :])
        d_probs = contract_last(values, d_context)
        prob_delta = jnp.sum(probs * d_probs, 0, keepdims=True)
        d_scores = (probs * (d_probs - prob_delta)).astype(jnp.bfloat16)
        d_query_pair.append(contract_first(d_scores, keys))
        d_keys.append(jnp.dot(d_scores, query, preferred_element_type=jnp.float32))
        d_values.append(
            jnp.dot(probs.astype(jnp.bfloat16), d_context, preferred_element_type=jnp.float32)
        )
    d_query = jnp.where(low_half, d_query_pair[0], d_query_pair[1]).astype(jnp.bfloat16)
    d_query_ref[0] = d_query * jnp.asarray(0.125, jnp.bfloat16)
    core = lengths[pl.num_programs(0)]
    split = (d_key_keep.shape[0], 2, 1) + d_key_keep.shape[2:]
    for pair, keep_ref, send_ref in (
        (d_keys, d_key_keep, d_key_send),
        (d_values, d_value_keep, d_value_send),
    ):
        total = (pair[0] + pair[1]).astype(jnp.bfloat16).reshape(split)
        keep_ref[...] = jnp.where(core == 0, total[:, 0], total[:, 1])
        send_ref[...] = jnp.where(core == 0, total[:, 1], total[:, 0])


def attention_call(kernel, slot_lengths, operands, backward):
    queries, keys = operands[0], operands[2 if backward else 1]
    slot_count, row_count, width = queries.shape
    place_count, lanes = keys.shape[0], 128
    pairs = width // lanes
    row_spec = pl.BlockSpec((1, row_count, lanes), lambda s, p, _: (s, 0, p))
    key_spec = pl.BlockSpec((place_count, 1, row_count, lanes), lambda s, p, _: (0, s, 0, p))
    stat_spec = pl.BlockSpec((1, 1, 8, row_count), lambda s, p, _: (s, p, 0, 0))
    low_rows = jax.ShapeDtypeStruct(queries.shape, jnp.bfloat16)
    half_keys = jax.ShapeDtypeStruct((place_count // 2,) + keys.shape[1:], jnp.bfloat16)
    half_spec = pl.BlockSpec((place_count // 2, 1, row_count, lanes), lambda s, p, _: (0, s, 0, p))
    stats = jax.ShapeDtypeStruct((slot_count, pairs, 8, row_count), jnp.float32)
    products = 5 if backward else 2
    scores = 2 * slot_count * pairs * row_count * place_count * row_count
    return pl.pallas_call(
        kernel,
        out_shape=(low_rows,) + (half_keys,) * 4 if backward else (low_rows, stats),
        grid_spec=pltpu.PrefetchScalarGridSpec(
            num_scalar_prefetch=1,
            grid=(slot_count, pairs),
            in_specs=(
                [row_spec, row_spec, key_spec, key_spec, stat_spec]
                if backward
                else [row_spec, key_spec, key_spec]
            ),
            out_specs=[row_spec] + [half_spec] * 4 if backward else [row_spec, stat_spec],
        ),
        cost_estimate=pl.CostEstimate(
            flops=products * 8 * scores * lanes,
            bytes_accessed=products * 2 * place_count * slot_count * row_count * width,
            transcendentals=scores,
        ),
    )(slot_lengths, *operands)


def products_kernel(core_ref, *refs):
    tokens_ref, query_ref, key_ref, value_ref, context_ref, attn_ref, small_ref, keep, send = refs
    core = core_ref[0]
    width = small_ref.shape[0]
    half = keep.shape[-1]
    columns = []
    for left, right in (
        (tokens_ref, query_ref),
        (tokens_ref, key_ref),
        (tokens_ref, value_ref),
        (context_ref, attn_ref),
        (None, small_ref),
    ):
        columns += [(left, right, start) for start in range(0, right.shape[1], 128)]
    per_step = half // 128

    def run(mine):
        place = 0
        while place < len(mine):
            left, right, start = mine[place]
            wide = place + 1 < len(mine) and mine[place + 1][1] is right
            lanes = 256 if wide else 128
            block = right[:, start : start + lanes]
            if left is not None:
                block = jnp.dot(left[...], block, preferred_element_type=jnp.float32)
                block = block.astype(jnp.bfloat16)
            block = block.reshape(4, 2, width // 8, lanes)
            span = slice(place * 128, place * 128 + lanes)
            keep[:, :, span] = jnp.where(core == 0, block[:, 0], block[:, 1])
            send[:, :, span] = jnp.where(core == 0, block[:, 1], block[:, 0])
            place += lanes // 128

    for step in range(2):
        pl.when(pl.program_id(0) == step)(
            lambda step=step: run(columns[step * per_step : (step + 1) * per_step])
        )


def attn_products(tokens, d_query, d_key, d_value, context, d_attn, small):
    width, rows = tokens.shape
    operands = (tokens, d_query, d_key, d_value, context, d_attn, small)
    total = 4 * width + small.shape[1]
    out_shape = jax.ShapeDtypeStruct((4, width // 8, total), jnp.bfloat16)
    out_spec = pl.BlockSpec((4, width // 8, total // 2), lambda i, _: (0, 0, i))
    return pl.pallas_call(
        products_kernel,
        out_shape=(out_shape, out_shape),
        grid_spec=pltpu.PrefetchScalarGridSpec(
            num_scalar_prefetch=1,
            grid=(2,),
            in_specs=[pl.BlockSpec(operand.shape, lambda i, _: (0, 0)) for operand in operands],
            out_specs=[out_spec, out_spec],
        ),
        cost_estimate=pl.CostEstimate(
            flops=8 * rows * width * width, bytes_accessed=16 * width * width, transcendentals=0
        ),
    )(places()[0].reshape(1), *operands)


def solution(mesh):
    fast = mesh.shape["seq"] == 8 and mesh.shape["slot"] == 4
    return jax.shard_map(
        body_fast if fast else body,
        mesh=mesh,
        in_specs=(
            P("slot", "seq", None),
            P(("seq", "slot"), None),
            P(("seq", "slot")),
            P(("seq", "slot")),
            P(("seq", "slot"), None),
            P(("seq", "slot")),
            P(("seq", "slot")),
            P(("seq", "slot")),
            P(("seq", "slot"), None),
            P(("seq", "slot")),
            P(("seq", "slot"), None),
            P(("seq", "slot")),
            P(("seq", "slot")),
            P(("seq", "slot")),
            P("slot"),
            P("slot", "seq", None),
        ),
        out_specs=(
            P("slot", "seq", None),
            P("slot", "seq", None),
            P(("seq", "slot"), None),
            P(("seq", "slot")),
            P(("seq", "slot")),
            P(("seq", "slot"), None),
            P(("seq", "slot")),
            P(("seq", "slot")),
            P(("seq", "slot")),
            P(("seq", "slot"), None),
            P(("seq", "slot")),
            P(("seq", "slot"), None),
            P(("seq", "slot")),
            P(("seq", "slot")),
            P(("seq", "slot")),
        ),
        check_vma=False,
    )
```

```python
import jax
import jax.numpy as jnp
from jax import lax
from jax.experimental import pallas as pl
from jax.experimental.pallas import tpu as pltpu
from jax.sharding import PartitionSpec as P

HEADS = 12


NEG_FILL = -1e30
SEQ, SLOT = "seq", "slot"
ALL_AXES = (SEQ, SLOT)
EPSILON = 1e-05


def norm_rows(resid, gain, shift):
    centre = resid - jnp.mean(resid, -1, keepdims=True)
    spread = jnp.mean(centre * centre, -1, keepdims=True)
    return centre * lax.rsqrt(spread + EPSILON) * gain + shift


def gelu_exact(inner_act):
    return jax.nn.gelu(inner_act, approximate=False)


def contract_rows(left, right):
    return lax.dot_general(
        left, right, (((0,), (0,)), ((), ())), preferred_element_type=jnp.float32
    )


def contract_last(left, right):
    return lax.dot_general(
        left, right, (((1,), (1,)), ((), ())), preferred_element_type=jnp.float32
    )


def split_heads(rows_in, head_count):
    return rows_in.reshape(
        rows_in.shape[0], rows_in.shape[1], head_count, rows_in.shape[2] // head_count
    )


def take_block(whole, position, block_size, axis_dim):
    return lax.dynamic_slice_in_dim(whole, position * block_size, block_size, axis_dim)


def masked_scores(queries, key_rows, key_start, slot_lengths):
    scores = jnp.einsum("sqhd,skhd->shqk", queries, key_rows, preferred_element_type=jnp.float32)
    key_places = key_start + jnp.arange(key_rows.shape[1])
    live_keys = key_places[None, :] < slot_lengths[:, None]
    return jnp.where(live_keys[:, None, None, :], scores, NEG_FILL)


def log_totals(queries, key_all, slot_lengths, block_size, head_count):
    block_count = key_all.shape[1] // block_size
    stat_shape = (queries.shape[0], head_count, queries.shape[1])

    def log_step_fn(carried, position):
        running_max, running_sum = carried
        key_rows = split_heads(take_block(key_all, position, block_size, 1), head_count)
        scores = masked_scores(queries, key_rows, position * block_size, slot_lengths)
        new_max = jnp.maximum(running_max, jnp.max(scores, -1))
        running_sum = running_sum * jnp.exp(running_max - new_max) + jnp.sum(
            jnp.exp(scores - new_max[..., None]), -1
        )
        return ((new_max, running_sum), None)

    start_state = (jnp.full(stat_shape, NEG_FILL, jnp.float32), jnp.zeros(stat_shape, jnp.float32))
    (running_max, running_sum), _ = lax.scan(log_step_fn, start_state, jnp.arange(block_count))
    return running_max + jnp.log(running_sum)


def attend(queries, key_all, value_all, slot_lengths, logsum, block_size, head_count):
    block_count = key_all.shape[1] // block_size

    def attend_step_fn(context, position):
        key_rows = split_heads(take_block(key_all, position, block_size, 1), head_count)
        value_rows = split_heads(take_block(value_all, position, block_size, 1), head_count)
        scores = masked_scores(queries, key_rows, position * block_size, slot_lengths)
        weights_low = jnp.exp(scores - logsum[..., None]).astype(jnp.bfloat16)
        return (
            context
            + jnp.einsum(
                "shqk,skhd->sqhd", weights_low, value_rows, preferred_element_type=jnp.float32
            ),
            None,
        )

    context, _ = lax.scan(
        attend_step_fn, jnp.zeros(queries.shape, jnp.float32), jnp.arange(block_count)
    )
    return context


def prob_grad_totals(
    queries, d_context, key_all, value_all, slot_lengths, logsum, block_size, head_count
):
    block_count = key_all.shape[1] // block_size

    def prob_step_fn(prob_delta, position):
        key_rows = split_heads(take_block(key_all, position, block_size, 1), head_count)
        value_rows = split_heads(take_block(value_all, position, block_size, 1), head_count)
        scores = masked_scores(queries, key_rows, position * block_size, slot_lengths)
        softmax_rows = jnp.exp(scores - logsum[..., None])
        d_probs = jnp.einsum(
            "sqhd,skhd->shqk", d_context, value_rows, preferred_element_type=jnp.float32
        )
        return (prob_delta + jnp.sum(softmax_rows * d_probs, -1), None)

    prob_delta, _ = lax.scan(
        prob_step_fn, jnp.zeros(logsum.shape, jnp.float32), jnp.arange(block_count)
    )
    return prob_delta


def key_side(
    queries, d_context, key_all, value_all, slot_lengths, logsum, prob_delta, block_size, head_count
):
    block_count = key_all.shape[1] // block_size

    def key_step_fn(d_query, position):
        key_rows = split_heads(take_block(key_all, position, block_size, 1), head_count)
        value_rows = split_heads(take_block(value_all, position, block_size, 1), head_count)
        scores = masked_scores(queries, key_rows, position * block_size, slot_lengths)
        softmax_rows = jnp.exp(scores - logsum[..., None])
        d_probs = jnp.einsum(
            "sqhd,skhd->shqk", d_context, value_rows, preferred_element_type=jnp.float32
        )
        d_scores = (softmax_rows * (d_probs - prob_delta[..., None])).astype(jnp.bfloat16)
        d_query = d_query + jnp.einsum(
            "shqk,skhd->sqhd", d_scores, key_rows, preferred_element_type=jnp.float32
        )
        d_key_rows = jnp.einsum(
            "shqk,sqhd->skhd", d_scores, queries, preferred_element_type=jnp.float32
        )
        d_value_rows = jnp.einsum(
            "shqk,sqhd->skhd",
            softmax_rows.astype(jnp.bfloat16),
            d_context,
            preferred_element_type=jnp.float32,
        )
        return (d_query, (d_key_rows, d_value_rows))

    return lax.scan(key_step_fn, jnp.zeros(queries.shape, jnp.float32), jnp.arange(block_count))


def flip_pairs(mask):
    return [((q * 4 + z), ((q ^ mask) * 4 + z)) for q in range(8) for z in range(4)]


def turn_pairs(step):
    return [((q * 4 + z), (q * 4 + (z + step) % 4)) for q in range(8) for z in range(4)]


CORE, X_AXIS, Y_AXIS = 1, 2, 4


def flip(value, mask):
    return lax.ppermute(value, ALL_AXES, flip_pairs(mask))


def turn(value, step):
    return lax.ppermute(value, ALL_AXES, turn_pairs(step))


def places():
    q = lax.axis_index(SEQ)
    return q & 1, (q >> 1) & 1, q >> 2, lax.axis_index(SLOT)


def merge(own, other, bit, axis):
    first = jnp.where(bit == 0, own, other)
    second = jnp.where(bit == 0, other, own)
    return jnp.stack([first, second], axis)


def plane_one(a, b):
    _, _, _, _ = places()
    a1, b1 = flip(a, X_AXIS), flip(b, Y_AXIS)
    return a1, b1


def plane_two(a, b, got):
    _, x, y, _ = places()
    a, b = merge(a, got[0], x, 0), merge(b, got[1], y, 0)
    return a, b, flip(a, Y_AXIS), flip(b, X_AXIS)


def plane_core(a, b, a2, b2):
    core, x, y, _ = places()
    a, b = merge(a, a2, y, 0), merge(b, b2, x, 1)
    a3, b3 = flip(a, CORE), flip(b, CORE)
    return merge(a, a3, core, 2), merge(b, b3, core, 2)


def plane_rows(a, b, a2, b2):
    core, x, y, _ = places()
    a, b = merge(a, a2, y, 0), merge(b, b2, x, 1)
    rows, columns = a.shape[-2:]
    a, b = a.reshape(4, 2, rows, columns), b.reshape(4, 2, rows, columns)
    a3, b3 = flip(a, CORE), flip(b, CORE)
    own, got = jnp.concatenate([a, b], 1), jnp.concatenate([a3, b3], 1)
    whole = merge(own, got, core, 1)
    return as_matrix(whole)


def after(value, ready):
    return lax.optimization_barrier((value, ready))[0]


def line_turns(shard):
    return tuple(turn(shard, step) for step in (1, 2, 3))


def line_blocks(shard, got):
    ring = [shard, got[2], got[1], got[0]]
    start = (4 - places()[3]) % 4
    return lax.dynamic_slice_in_dim(jnp.stack(ring + ring[:3]), start, 4, 0)


def as_matrix(parts):
    return parts.reshape(32 * parts.shape[-2], parts.shape[-1])


def pick(value, index, axis):
    return lax.dynamic_index_in_dim(value, index, axis, keepdims=False)


def choose(value, bit, axis):
    first = lax.index_in_dim(value, 0, axis, keepdims=False)
    return jnp.where(bit == 0, first, lax.index_in_dim(value, 1, axis, keepdims=False))


def add_low(left, right):
    return (left.astype(jnp.float32) + right.astype(jnp.float32)).astype(jnp.bfloat16)


def fold(value, bit, mask, axis):
    return add_low(choose(value, bit, axis), flip(choose(value, 1 - bit, axis), mask))


def core_fold(parts):
    core = places()[0]
    return tuple(fold(part, core, CORE, 2) for part in parts)


def core_fold_split(keep, send):
    return add_low(keep, flip(send, CORE))


def plane_fold(a, b):
    _, x, y, _ = places()
    a, b = fold(a, y, Y_AXIS, 0), fold(b, x, X_AXIS, 1)
    return fold(a, x, X_AXIS, 0), fold(b, y, Y_AXIS, 0)


def scatter_line(part):
    z = places()[3]
    return [pick(part, z, 0)] + [turn(pick(part, (z + step) % 4, 0), step) for step in (1, 2, 3)]


def line_total(terms):
    return sum(term.astype(jnp.float32) for term in terms)


def place_blocks(part):
    return part.reshape(2, 2, 2, 4, part.shape[0] // 32, part.shape[1])


def body(
    tokens,
    qkv_weight,
    query_bias,
    value_bias,
    out_weight,
    out_bias,
    norm1_gain,
    norm1_shift,
    up_weight,
    up_bias,
    down_weight,
    down_bias,
    norm2_gain,
    norm2_shift,
    slot_lengths,
    out_cotangent,
):
    slot_count, row_count, model_width = tokens.shape
    head_count = HEADS
    flat_rows = tokens.reshape(slot_count * row_count, model_width)
    attn_set = (
        lax.all_gather(qkv_weight, ALL_AXES, axis=0, tiled=True),
        lax.all_gather(out_weight, ALL_AXES, axis=0, tiled=True),
        lax.all_gather(query_bias, ALL_AXES, axis=0, tiled=True),
        lax.all_gather(value_bias, ALL_AXES, axis=0, tiled=True),
        lax.all_gather(out_bias, ALL_AXES, axis=0, tiled=True),
        lax.all_gather(norm1_gain, ALL_AXES, axis=0, tiled=True),
        lax.all_gather(norm1_shift, ALL_AXES, axis=0, tiled=True),
    )
    qkv_full, out_full, query_shift, value_shift, out_shift, gain_one, shift_one = attn_set
    mixed = jnp.dot(flat_rows, qkv_full, preferred_element_type=jnp.float32)
    queries = ((mixed[:, :model_width] + query_shift.astype(jnp.float32)) * 0.125).astype(
        jnp.bfloat16
    )
    queries = split_heads(queries.reshape(slot_count, row_count, model_width), head_count)
    keys_own = (
        mixed[:, model_width : 2 * model_width]
        .astype(jnp.bfloat16)
        .reshape(slot_count, row_count, model_width)
    )
    values_own = (
        (mixed[:, 2 * model_width :] + value_shift.astype(jnp.float32))
        .astype(jnp.bfloat16)
        .reshape(slot_count, row_count, model_width)
    )
    key_all, value_all = (
        lax.all_gather(keys_own, SEQ, axis=1, tiled=True),
        lax.all_gather(values_own, SEQ, axis=1, tiled=True),
    )
    length_all = key_all.shape[1]
    block_size = min(512, length_all)
    logsum = log_totals(queries, key_all, slot_lengths, block_size, head_count)
    context = attend(
        queries, key_all, value_all, slot_lengths, logsum, block_size, head_count
    ).astype(jnp.bfloat16)
    context_flat = context.reshape(slot_count * row_count, model_width)
    attn_out = jnp.dot(
        context_flat, out_full, preferred_element_type=jnp.float32
    ) + out_shift.astype(jnp.float32)
    resid_one = flat_rows.astype(jnp.float32) + attn_out
    hidden_one = norm_rows(resid_one, gain_one.astype(jnp.float32), shift_one.astype(jnp.float32))
    hidden_low = hidden_one.astype(jnp.bfloat16)
    ffn_set = (
        lax.all_gather(up_weight, ALL_AXES, axis=0, tiled=True),
        lax.all_gather(down_weight, ALL_AXES, axis=0, tiled=True),
        lax.all_gather(up_bias, ALL_AXES, axis=0, tiled=True),
        lax.all_gather(down_bias, ALL_AXES, axis=0, tiled=True),
        lax.all_gather(norm2_gain, ALL_AXES, axis=0, tiled=True),
        lax.all_gather(norm2_shift, ALL_AXES, axis=0, tiled=True),
    )
    up_full, down_full, up_shift, down_shift, gain_two, shift_two = ffn_set
    inner_act = jnp.dot(hidden_low, up_full, preferred_element_type=jnp.float32) + up_shift.astype(
        jnp.float32
    )
    activated = gelu_exact(inner_act).astype(jnp.bfloat16)
    ffn_out = jnp.dot(activated, down_full, preferred_element_type=jnp.float32) + down_shift.astype(
        jnp.float32
    )
    resid_two = hidden_one + ffn_out
    layer_out = norm_rows(resid_two, gain_two.astype(jnp.float32), shift_two.astype(jnp.float32))
    layer_out = layer_out.astype(jnp.bfloat16).reshape(slot_count, row_count, model_width)
    qkv_back, out_back, _, _, _, gain_one_back, shift_one_back = (
        lax.all_gather(qkv_weight, ALL_AXES, axis=0, tiled=True),
        lax.all_gather(out_weight, ALL_AXES, axis=0, tiled=True),
        lax.all_gather(query_bias, ALL_AXES, axis=0, tiled=True),
        lax.all_gather(value_bias, ALL_AXES, axis=0, tiled=True),
        lax.all_gather(out_bias, ALL_AXES, axis=0, tiled=True),
        lax.all_gather(norm1_gain, ALL_AXES, axis=0, tiled=True),
        lax.all_gather(norm1_shift, ALL_AXES, axis=0, tiled=True),
    )
    up_back, down_back, _, _, gain_two_back, shift_two_back = (
        lax.all_gather(up_weight, ALL_AXES, axis=0, tiled=True),
        lax.all_gather(down_weight, ALL_AXES, axis=0, tiled=True),
        lax.all_gather(up_bias, ALL_AXES, axis=0, tiled=True),
        lax.all_gather(down_bias, ALL_AXES, axis=0, tiled=True),
        lax.all_gather(norm2_gain, ALL_AXES, axis=0, tiled=True),
        lax.all_gather(norm2_shift, ALL_AXES, axis=0, tiled=True),
    )
    positions = lax.axis_index(SEQ) * row_count + jnp.arange(row_count)
    live_rows = (positions[None, :] < slot_lengths[:, None]).astype(jnp.float32)
    cotangent = (out_cotangent.astype(jnp.float32) * live_rows[:, :, None]).reshape(
        slot_count * row_count, model_width
    )
    _, norm_back_two = jax.vjp(
        norm_rows, resid_two, gain_two_back.astype(jnp.float32), shift_two_back.astype(jnp.float32)
    )
    d_resid_two, d_gain_two, d_shift_two = norm_back_two(cotangent)
    d_ffn = d_resid_two.astype(jnp.bfloat16)
    d_down = contract_rows(activated, d_ffn)
    d_down_shift = jnp.sum(d_ffn.astype(jnp.float32), 0)
    d_activated = contract_last(d_ffn, down_back)
    _, gelu_back = jax.vjp(gelu_exact, inner_act)
    d_inner = gelu_back(d_activated)[0].astype(jnp.bfloat16)
    d_up = contract_rows(hidden_low, d_inner)
    d_up_shift = jnp.sum(d_inner.astype(jnp.float32), 0)
    d_hidden = contract_last(d_inner, up_back) + d_resid_two
    _, norm_back_one = jax.vjp(
        norm_rows, resid_one, gain_one_back.astype(jnp.float32), shift_one_back.astype(jnp.float32)
    )
    d_resid_one, d_gain_one, d_shift_one = norm_back_one(d_hidden)
    d_attn = d_resid_one.astype(jnp.bfloat16)
    d_out = contract_rows(context_flat, d_attn)
    d_out_shift = jnp.sum(d_attn.astype(jnp.float32), 0)
    d_context = contract_last(d_attn, out_back).astype(jnp.bfloat16)
    d_context = split_heads(d_context.reshape(slot_count, row_count, model_width), head_count)
    prob_delta = prob_grad_totals(
        queries, d_context, key_all, value_all, slot_lengths, logsum, block_size, head_count
    )
    d_query, key_parts = key_side(
        queries,
        d_context,
        key_all,
        value_all,
        slot_lengths,
        logsum,
        prob_delta,
        block_size,
        head_count,
    )
    d_key_part = jnp.moveaxis(key_parts[0], 0, 1).reshape(slot_count, length_all, model_width)
    d_value_part = jnp.moveaxis(key_parts[1], 0, 1).reshape(slot_count, length_all, model_width)
    d_key_sum, d_value_sum = (
        lax.psum_scatter(
            d_key_part.astype(jnp.bfloat16), SEQ, scatter_dimension=1, tiled=True
        ).astype(jnp.float32),
        lax.psum_scatter(
            d_value_part.astype(jnp.bfloat16), SEQ, scatter_dimension=1, tiled=True
        ).astype(jnp.float32),
    )
    d_query_pre = d_query.astype(jnp.bfloat16).reshape(
        slot_count * row_count, model_width
    ) * jnp.asarray(0.125, jnp.bfloat16)
    d_key_low = d_key_sum.astype(jnp.bfloat16).reshape(slot_count * row_count, model_width)
    d_value_low = d_value_sum.astype(jnp.bfloat16).reshape(slot_count * row_count, model_width)
    d_mixed = jnp.concatenate([d_query_pre, d_key_low, d_value_low], 1)
    d_qkv = contract_rows(flat_rows, d_mixed)
    d_query_shift = jnp.sum(d_query_pre.astype(jnp.float32), 0)
    d_value_shift = jnp.sum(d_value_low.astype(jnp.float32), 0)
    tokens_grad = (
        (d_resid_one + contract_last(d_mixed, qkv_back))
        .astype(jnp.bfloat16)
        .reshape(slot_count, row_count, model_width)
    )
    attn_sums = (
        lax.psum_scatter(d_qkv, ALL_AXES, scatter_dimension=0, tiled=True),
        lax.psum_scatter(d_out, ALL_AXES, scatter_dimension=0, tiled=True),
        lax.psum_scatter(d_query_shift, ALL_AXES, scatter_dimension=0, tiled=True),
        lax.psum_scatter(d_value_shift, ALL_AXES, scatter_dimension=0, tiled=True),
        lax.psum_scatter(d_out_shift, ALL_AXES, scatter_dimension=0, tiled=True),
        lax.psum_scatter(d_gain_one, ALL_AXES, scatter_dimension=0, tiled=True),
        lax.psum_scatter(d_shift_one, ALL_AXES, scatter_dimension=0, tiled=True),
    )
    ffn_sums = (
        lax.psum_scatter(d_up, ALL_AXES, scatter_dimension=0, tiled=True),
        lax.psum_scatter(d_down, ALL_AXES, scatter_dimension=0, tiled=True),
        lax.psum_scatter(d_up_shift, ALL_AXES, scatter_dimension=0, tiled=True),
        lax.psum_scatter(d_down_shift, ALL_AXES, scatter_dimension=0, tiled=True),
        lax.psum_scatter(d_gain_two, ALL_AXES, scatter_dimension=0, tiled=True),
        lax.psum_scatter(d_shift_two, ALL_AXES, scatter_dimension=0, tiled=True),
    )
    return (
        layer_out,
        tokens_grad,
        attn_sums[0],
        attn_sums[2],
        attn_sums[3],
        attn_sums[1],
        attn_sums[4],
        attn_sums[5],
        attn_sums[6],
        ffn_sums[0],
        ffn_sums[2],
        ffn_sums[1],
        ffn_sums[3],
        ffn_sums[4],
        ffn_sums[5],
    )


def body_fast(
    tokens,
    qkv_weight,
    query_bias,
    value_bias,
    out_weight,
    out_bias,
    norm1_gain,
    norm1_shift,
    up_weight,
    up_bias,
    down_weight,
    down_bias,
    norm2_gain,
    norm2_shift,
    slot_lengths,
    out_cotangent,
):
    slot_count, row_count, model_width = tokens.shape
    part = qkv_weight.shape[0]
    inner_part = up_bias.shape[0]
    flat_rows = tokens.reshape(slot_count * row_count, model_width)
    small = jnp.stack(
        [
            query_bias,
            value_bias,
            out_bias,
            norm1_gain,
            norm1_shift,
            down_bias,
            norm2_gain,
            norm2_shift,
        ]
    )
    small = jnp.concatenate(
        [
            jnp.pad(small, ((0, 0), (0, 256 - part))),
            jnp.pad(up_bias[None], ((0, part - 9), (0, 256 - inner_part))),
        ]
    )
    attn_shard = jnp.concatenate([qkv_weight, out_weight, small], 1)
    attn_line = line_blocks(attn_shard, line_turns(attn_shard))
    half = attn_line.shape[-1] // 2
    rest = 3 * model_width - half
    attn_halves = attn_line[..., :half], attn_line[..., half:]
    stack_count = down_weight.shape[0] // part
    ffn_shard = jnp.concatenate(
        [up_weight] + [down_weight[k * part : (k + 1) * part] for k in range(stack_count)], 1
    )
    ffn_shard = after(ffn_shard, attn_line)
    ffn_got = line_turns(ffn_shard)
    attn_halves = plane_two(*attn_halves, plane_one(*attn_halves))
    ffn_line = line_blocks(ffn_shard, ffn_got)
    ff_width = up_weight.shape[1]
    down_line = [
        ffn_line[..., ff_width + k * model_width : ff_width + (k + 1) * model_width]
        for k in range(stack_count)
    ]
    down_line = jnp.concatenate(down_line, 1)
    up_halves = ffn_line[:2, :, :ff_width], ffn_line[2:, :, :ff_width]
    down_halves = down_line[:2], down_line[2:]
    up_got = plane_one(*up_halves)
    down_got = plane_one(*down_halves)
    attn_a, attn_b = (as_matrix(parts) for parts in plane_core(*attn_halves))
    out_full = attn_b[:, rest : rest + model_width]
    small_full = attn_b[:, rest + model_width : rest + model_width + 128]
    small_full = small_full.reshape(32, part, 128).astype(jnp.float32)
    vectors = jnp.moveaxis(small_full[:, :8, :part], 1, 0).reshape(8, model_width)
    up_shift = small_full[:, 8, :inner_part].reshape(1, 32 * inner_part)
    vectors, up_shift = lax.optimization_barrier((vectors, up_shift))
    query_shift, value_shift, out_shift, gain_one, shift_one, down_shift, gain_two, shift_two = (
        vectors[position : position + 1] for position in range(8)
    )
    mixed_a = jnp.dot(flat_rows, attn_a, preferred_element_type=jnp.float32)
    mixed_b = jnp.dot(flat_rows, attn_b[:, :rest], preferred_element_type=jnp.float32)
    mixed = jnp.concatenate([mixed_a, mixed_b], 1)
    queries = ((mixed[:, :model_width] + query_shift) * 0.125).astype(jnp.bfloat16)
    queries = queries.reshape(slot_count, row_count, model_width)
    keys_own = (
        mixed[:, model_width : 2 * model_width]
        .astype(jnp.bfloat16)
        .reshape(slot_count, row_count, model_width)
    )
    values_own = (
        (mixed[:, 2 * model_width :] + value_shift)
        .astype(jnp.bfloat16)
        .reshape(slot_count, row_count, model_width)
    )

    places_shape = (8, slot_count, row_count, model_width)
    kept = plane_two(keys_own, values_own, plane_one(keys_own, values_own))
    up_full = plane_rows(*plane_two(*up_halves, up_got))
    down_full = plane_rows(*plane_two(*down_halves, down_got))
    key_all, value_all = (part.reshape(places_shape) for part in plane_core(*kept))
    context, logsum = attention_call(
        attend_kernel, slot_lengths, (queries, key_all, value_all), False
    )
    context_flat = context.reshape(slot_count * row_count, model_width)
    attn_out = jnp.dot(context_flat, out_full, preferred_element_type=jnp.float32) + out_shift
    resid_one = flat_rows.astype(jnp.float32) + attn_out
    hidden_one = norm_rows(resid_one, gain_one, shift_one)
    hidden_low = hidden_one.astype(jnp.bfloat16)
    inner_act = jnp.dot(hidden_low, up_full, preferred_element_type=jnp.float32) + up_shift
    activated = gelu_exact(inner_act).astype(jnp.bfloat16)
    ffn_out = jnp.dot(activated, down_full, preferred_element_type=jnp.float32) + down_shift
    resid_two = hidden_one + ffn_out
    layer_out = norm_rows(resid_two, gain_two, shift_two)
    layer_out = layer_out.astype(jnp.bfloat16).reshape(slot_count, row_count, model_width)
    positions = lax.axis_index(SEQ) * row_count + jnp.arange(row_count)
    live_rows = (positions[None, :] < slot_lengths[:, None]).astype(jnp.float32)
    cotangent = (out_cotangent.astype(jnp.float32) * live_rows[:, :, None]).reshape(
        slot_count * row_count, model_width
    )
    _, norm_back_two = jax.vjp(norm_rows, resid_two, gain_two, shift_two)
    d_resid_two, d_gain_two, d_shift_two = norm_back_two(cotangent)
    d_ffn = d_resid_two.astype(jnp.bfloat16)
    d_down = contract_rows(activated, d_ffn).astype(jnp.bfloat16)
    d_down_shift = jnp.sum(d_ffn.astype(jnp.float32), 0)
    d_activated = contract_last(d_ffn, down_full)
    _, gelu_back = jax.vjp(gelu_exact, inner_act)
    d_inner = gelu_back(d_activated)[0].astype(jnp.bfloat16)
    d_up = contract_rows(hidden_low, d_inner).astype(jnp.bfloat16)
    d_up, d_down = core_fold((place_blocks(d_up), place_blocks(d_down)))
    d_up, d_down = plane_fold(d_up, d_down)
    d_down = d_down.reshape(4, stack_count, part, model_width)
    ffn_terms = scatter_line(
        jnp.concatenate([d_up] + [d_down[:, k] for k in range(stack_count)], 2)
    )
    d_up_shift = jnp.sum(d_inner.astype(jnp.float32), 0)
    d_hidden = contract_last(d_inner, up_full) + d_resid_two
    _, norm_back_one = jax.vjp(norm_rows, resid_one, gain_one, shift_one)
    d_resid_one, d_gain_one, d_shift_one = norm_back_one(d_hidden)
    d_attn = d_resid_one.astype(jnp.bfloat16)
    d_out_shift = jnp.sum(d_attn.astype(jnp.float32), 0)
    d_context = contract_last(d_attn, out_full).astype(jnp.bfloat16)
    tokens_across, context_across = lax.optimization_barrier((flat_rows.T, context_flat.T))
    d_query, *key_parts = attention_call(
        attend_back_kernel,
        jnp.append(slot_lengths, places()[0]),
        (
            queries,
            d_context.reshape(slot_count, row_count, model_width),
            key_all,
            value_all,
            logsum,
        ),
        True,
    )
    half_shape = (2, 2) + places_shape[1:]
    d_key_low, d_value_low = plane_fold(
        core_fold_split(key_parts[0], key_parts[1]).reshape(half_shape),
        core_fold_split(key_parts[2], key_parts[3]).reshape(half_shape),
    )
    d_query_pre = d_query.reshape(slot_count * row_count, model_width)
    d_key_low = d_key_low.reshape(slot_count * row_count, model_width)
    d_value_low = d_value_low.reshape(slot_count * row_count, model_width)
    d_mixed = jnp.concatenate([d_query_pre, d_key_low, d_value_low], 1)
    d_query_shift = jnp.sum(d_query_pre.astype(jnp.float32), 0)
    d_value_shift = jnp.sum(d_value_low.astype(jnp.float32), 0)
    tokens_grad = (
        (
            d_resid_one
            + contract_last(d_mixed[:, :half], attn_a)
            + contract_last(d_mixed[:, half:], attn_b[:, :rest])
        )
        .astype(jnp.bfloat16)
        .reshape(slot_count, row_count, model_width)
    )
    row_places = lax.broadcasted_iota(jnp.int32, (8, model_width), 0)
    small_grads = jnp.zeros((8, model_width), jnp.float32)
    for position, grad in enumerate(
        (
            d_query_shift,
            d_value_shift,
            d_out_shift,
            d_gain_one,
            d_shift_one,
            d_down_shift,
            d_gain_two,
            d_shift_two,
        )
    ):
        small_grads = jnp.where(
            row_places == position, grad.reshape(1, model_width), small_grads
        )
    small_grads = lax.optimization_barrier(small_grads.astype(jnp.bfloat16))
    small_grads = jnp.moveaxis(small_grads.reshape(8, 32, part), 0, 1)
    inner_grads = d_up_shift.astype(jnp.bfloat16).reshape(32, 1, inner_part)
    small_grads = jnp.concatenate(
        [
            jnp.pad(small_grads, ((0, 0), (0, 0), (0, 256 - part))),
            jnp.pad(inner_grads, ((0, 0), (0, part - 9), (0, 256 - inner_part))),
        ],
        1,
    ).reshape(32 * part, 256)
    keep, send = attn_products(
        tokens_across,
        d_query_pre,
        d_key_low,
        d_value_low,
        context_across,
        d_attn,
        small_grads,
    )
    grads = core_fold_split(keep, send).reshape(2, 2, 4, part, keep.shape[-1])
    grads = jnp.concatenate(plane_fold(grads[..., :half], grads[..., half:]), 2)
    attn_terms = scatter_line(grads)
    ffn_total = line_total(ffn_terms)
    attn_total = line_total(attn_terms)
    d_up = ffn_total[:, :ff_width]
    d_down = jnp.concatenate(
        [
            ffn_total[:, ff_width + k * model_width : ff_width + (k + 1) * model_width]
            for k in range(stack_count)
        ]
    )
    own = attn_total[:, 4 * model_width : 4 * model_width + 128]
    vectors = [own[position, :part] for position in range(8)]
    return (
        layer_out,
        tokens_grad,
        attn_total[:, : 3 * model_width],
        vectors[0],
        vectors[1],
        attn_total[:, 3 * model_width : 4 * model_width],
        vectors[2],
        vectors[3],
        vectors[4],
        d_up,
        own[8, :inner_part],
        d_down,
        vectors[5],
        vectors[6],
        vectors[7],
    )


def contract_first(left, right):
    return lax.dot_general(
        left, right, (((0,), (0,)), ((), ())), preferred_element_type=jnp.float32
    )


def low_lanes(shape):
    return lax.broadcasted_iota(jnp.int32, shape, 1) < shape[1] // 2


def stack_heads(value):
    zero, low_half = jnp.zeros_like(value), low_lanes(value.shape)
    return jnp.concatenate(
        [jnp.where(low_half, value, zero), jnp.where(low_half, zero, value)], 0
    )


def join_heads(stacked):
    rows = stacked.shape[0] // 2
    return jnp.where(low_lanes((rows, stacked.shape[1])), stacked[:rows], stacked[rows:])


def length_bias(length, key_count):
    places = lax.broadcasted_iota(jnp.int32, (1, key_count), 1)
    return jnp.where(places < length, 0.0, NEG_FILL)


def pair_rows(ref, span):
    return ref[:, 0, :, span].reshape(-1, 128)


def attend_kernel(lengths, query_ref, key_ref, value_ref, context_ref, logsum_ref):
    bias = length_bias(lengths[pl.program_id(0)], key_ref.shape[0] * key_ref.shape[2])
    for pair in range(query_ref.shape[2] // 128):
        span = slice(pair * 128, (pair + 1) * 128)
        keys, values = pair_rows(key_ref, span), pair_rows(value_ref, span)
        scores = contract_last(stack_heads(query_ref[0, :, span]), keys) + bias
        row_max = jnp.max(scores, 1, keepdims=True)
        weights = jnp.exp(scores - row_max)
        total = jnp.sum(weights, 1, keepdims=True)
        logsum_ref[0, pair] = jnp.broadcast_to(
            row_max + jnp.log(total), logsum_ref.shape[2:]
        )
        summed = jnp.dot(
            weights.astype(jnp.bfloat16), values, preferred_element_type=jnp.float32
        )
        context_ref[0, :, span] = join_heads(summed * (1.0 / total)).astype(jnp.bfloat16)


def attend_back_kernel(
    lengths,
    query_ref,
    d_context_ref,
    key_ref,
    value_ref,
    logsum_ref,
    d_query_ref,
    d_key_keep,
    d_key_send,
    d_value_keep,
    d_value_send,
):
    core = lengths[pl.num_programs(0)]
    place_count, rows = key_ref.shape[0], key_ref.shape[2]
    bias = length_bias(lengths[pl.program_id(0)], place_count * rows)
    for pair in range(query_ref.shape[2] // 128):
        span = slice(pair * 128, (pair + 1) * 128)
        keys, values = pair_rows(key_ref, span), pair_rows(value_ref, span)
        query = stack_heads(query_ref[0, :, span])
        d_context = stack_heads(d_context_ref[0, :, span])
        scores = contract_last(query, keys) + bias
        probs = jnp.exp(scores - logsum_ref[0, pair][:, 0:1])
        d_probs = contract_last(d_context, values)
        prob_delta = jnp.sum(probs * d_probs, 1, keepdims=True)
        d_scores = (probs * (d_probs - prob_delta)).astype(jnp.bfloat16)
        d_query = join_heads(jnp.dot(d_scores, keys, preferred_element_type=jnp.float32))
        d_query_ref[0, :, span] = d_query.astype(jnp.bfloat16) * jnp.asarray(0.125, jnp.bfloat16)
        for total, keep_ref, send_ref in (
            (contract_first(d_scores, query), d_key_keep, d_key_send),
            (contract_first(probs.astype(jnp.bfloat16), d_context), d_value_keep, d_value_send),
        ):
            total = total.astype(jnp.bfloat16).reshape(place_count // 2, 2, rows, 128)
            keep_ref[:, 0, :, span] = jnp.where(core == 0, total[:, 0], total[:, 1])
            send_ref[:, 0, :, span] = jnp.where(core == 0, total[:, 1], total[:, 0])


def attention_call(kernel, slot_lengths, operands, backward):
    queries, keys = operands[0], operands[2 if backward else 1]
    slot_count, row_count, width = queries.shape
    place_count, lanes = keys.shape[0], 256
    pairs = width // lanes
    row_spec = pl.BlockSpec((1, row_count, lanes), lambda s, p, _: (s, 0, p))
    key_spec = pl.BlockSpec((place_count, 1, row_count, lanes), lambda s, p, _: (0, s, 0, p))
    stat_spec = pl.BlockSpec((1, 2, 2 * row_count, 128), lambda s, p, _: (s, p, 0, 0))
    low_rows = jax.ShapeDtypeStruct(queries.shape, jnp.bfloat16)
    half_keys = jax.ShapeDtypeStruct((place_count // 2,) + keys.shape[1:], jnp.bfloat16)
    half_spec = pl.BlockSpec((place_count // 2, 1, row_count, lanes), lambda s, p, _: (0, s, 0, p))
    stats = jax.ShapeDtypeStruct((slot_count, 2 * pairs, 2 * row_count, 128), jnp.float32)
    products = 5 if backward else 2
    scores = 4 * slot_count * pairs * row_count * place_count * row_count
    return pl.pallas_call(
        kernel,
        out_shape=(low_rows,) + (half_keys,) * 4 if backward else (low_rows, stats),
        grid_spec=pltpu.PrefetchScalarGridSpec(
            num_scalar_prefetch=1,
            grid=(slot_count, pairs),
            in_specs=(
                [row_spec, row_spec, key_spec, key_spec, stat_spec]
                if backward
                else [row_spec, key_spec, key_spec]
            ),
            out_specs=[row_spec] + [half_spec] * 4 if backward else [row_spec, stat_spec],
        ),
        cost_estimate=pl.CostEstimate(
            flops=products * 4 * scores * lanes,
            bytes_accessed=products * 2 * place_count * slot_count * row_count * width,
            transcendentals=scores,
        ),
    )(slot_lengths, *operands)


def products_kernel(core_ref, *refs):
    tokens_ref, query_ref, key_ref, value_ref, context_ref, attn_ref, small_ref, keep, send = refs
    core = core_ref[0]
    width = small_ref.shape[0]
    half = keep.shape[-1]
    columns = []
    for left, right in (
        (tokens_ref, query_ref),
        (tokens_ref, key_ref),
        (tokens_ref, value_ref),
        (context_ref, attn_ref),
        (None, small_ref),
    ):
        columns += [(left, right, start) for start in range(0, right.shape[1], 128)]
    per_step = half // 128

    def run(mine):
        place = 0
        while place < len(mine):
            left, right, start = mine[place]
            wide = place + 1 < len(mine) and mine[place + 1][1] is right
            lanes = 256 if wide else 128
            block = right[:, start : start + lanes]
            if left is not None:
                block = jnp.dot(left[...], block, preferred_element_type=jnp.float32)
                block = block.astype(jnp.bfloat16)
            block = block.reshape(4, 2, width // 8, lanes)
            span = slice(place * 128, place * 128 + lanes)
            keep[:, :, span] = jnp.where(core == 0, block[:, 0], block[:, 1])
            send[:, :, span] = jnp.where(core == 0, block[:, 1], block[:, 0])
            place += lanes // 128

    for step in range(2):
        pl.when(pl.program_id(0) == step)(
            lambda step=step: run(columns[step * per_step : (step + 1) * per_step])
        )


def attn_products(tokens, d_query, d_key, d_value, context, d_attn, small):
    width, rows = tokens.shape
    operands = (tokens, d_query, d_key, d_value, context, d_attn, small)
    total = 4 * width + small.shape[1]
    out_shape = jax.ShapeDtypeStruct((4, width // 8, total), jnp.bfloat16)
    out_spec = pl.BlockSpec((4, width // 8, total // 2), lambda i, _: (0, 0, i))
    return pl.pallas_call(
        products_kernel,
        out_shape=(out_shape, out_shape),
        grid_spec=pltpu.PrefetchScalarGridSpec(
            num_scalar_prefetch=1,
            grid=(2,),
            in_specs=[pl.BlockSpec(operand.shape, lambda i, _: (0, 0)) for operand in operands],
            out_specs=[out_spec, out_spec],
        ),
        cost_estimate=pl.CostEstimate(
            flops=8 * rows * width * width, bytes_accessed=16 * width * width, transcendentals=0
        ),
    )(places()[0].reshape(1), *operands)


def solution(mesh):
    fast = mesh.shape[SEQ] == 8 and mesh.shape[SLOT] == 4
    return jax.shard_map(
        body_fast if fast else body,
        mesh=mesh,
        in_specs=(
            P(SLOT, SEQ, None),
            P(ALL_AXES, None),
            P(ALL_AXES),
            P(ALL_AXES),
            P(ALL_AXES, None),
            P(ALL_AXES),
            P(ALL_AXES),
            P(ALL_AXES),
            P(ALL_AXES, None),
            P(ALL_AXES),
            P(ALL_AXES, None),
            P(ALL_AXES),
            P(ALL_AXES),
            P(ALL_AXES),
            P(SLOT),
            P(SLOT, SEQ, None),
        ),
        out_specs=(
            P(SLOT, SEQ, None),
            P(SLOT, SEQ, None),
            P(ALL_AXES, None),
            P(ALL_AXES),
            P(ALL_AXES),
            P(ALL_AXES, None),
            P(ALL_AXES),
            P(ALL_AXES),
            P(ALL_AXES),
            P(ALL_AXES, None),
            P(ALL_AXES),
            P(ALL_AXES, None),
            P(ALL_AXES),
            P(ALL_AXES),
            P(ALL_AXES),
        ),
        check_vma=False,
    )
```

```python
import jax
import jax.numpy as jnp
from jax import lax
from jax.experimental import pallas as pl
from jax.experimental.pallas import tpu as pltpu
from jax.sharding import PartitionSpec as P

HEADS = 12


NEG_FILL = -1e30
SEQ, SLOT = "seq", "slot"
ALL_AXES = (SEQ, SLOT)
EPSILON = 1e-05


def norm_rows(resid, gain, shift):
    centre = resid - jnp.mean(resid, -1, keepdims=True)
    spread = jnp.mean(centre * centre, -1, keepdims=True)
    return centre * lax.rsqrt(spread + EPSILON) * gain + shift


def gelu_exact(inner_act):
    return jax.nn.gelu(inner_act, approximate=False)


def contract_rows(left, right):
    return lax.dot_general(
        left, right, (((0,), (0,)), ((), ())), preferred_element_type=jnp.float32
    )


def contract_last(left, right):
    return lax.dot_general(
        left, right, (((1,), (1,)), ((), ())), preferred_element_type=jnp.float32
    )


def split_heads(rows_in, head_count):
    return rows_in.reshape(
        rows_in.shape[0], rows_in.shape[1], head_count, rows_in.shape[2] // head_count
    )


def take_block(whole, position, block_size, axis_dim):
    return lax.dynamic_slice_in_dim(whole, position * block_size, block_size, axis_dim)


def masked_scores(queries, key_rows, key_start, slot_lengths):
    scores = jnp.einsum("sqhd,skhd->shqk", queries, key_rows, preferred_element_type=jnp.float32)
    key_places = key_start + jnp.arange(key_rows.shape[1])
    live_keys = key_places[None, :] < slot_lengths[:, None]
    return jnp.where(live_keys[:, None, None, :], scores, NEG_FILL)


def log_totals(queries, key_all, slot_lengths, block_size, head_count):
    block_count = key_all.shape[1] // block_size
    stat_shape = (queries.shape[0], head_count, queries.shape[1])

    def log_step_fn(carried, position):
        running_max, running_sum = carried
        key_rows = split_heads(take_block(key_all, position, block_size, 1), head_count)
        scores = masked_scores(queries, key_rows, position * block_size, slot_lengths)
        new_max = jnp.maximum(running_max, jnp.max(scores, -1))
        running_sum = running_sum * jnp.exp(running_max - new_max) + jnp.sum(
            jnp.exp(scores - new_max[..., None]), -1
        )
        return ((new_max, running_sum), None)

    start_state = (jnp.full(stat_shape, NEG_FILL, jnp.float32), jnp.zeros(stat_shape, jnp.float32))
    (running_max, running_sum), _ = lax.scan(log_step_fn, start_state, jnp.arange(block_count))
    return running_max + jnp.log(running_sum)


def attend(queries, key_all, value_all, slot_lengths, logsum, block_size, head_count):
    block_count = key_all.shape[1] // block_size

    def attend_step_fn(context, position):
        key_rows = split_heads(take_block(key_all, position, block_size, 1), head_count)
        value_rows = split_heads(take_block(value_all, position, block_size, 1), head_count)
        scores = masked_scores(queries, key_rows, position * block_size, slot_lengths)
        weights_low = jnp.exp(scores - logsum[..., None]).astype(jnp.bfloat16)
        return (
            context
            + jnp.einsum(
                "shqk,skhd->sqhd", weights_low, value_rows, preferred_element_type=jnp.float32
            ),
            None,
        )

    context, _ = lax.scan(
        attend_step_fn, jnp.zeros(queries.shape, jnp.float32), jnp.arange(block_count)
    )
    return context


def prob_grad_totals(
    queries, d_context, key_all, value_all, slot_lengths, logsum, block_size, head_count
):
    block_count = key_all.shape[1] // block_size

    def prob_step_fn(prob_delta, position):
        key_rows = split_heads(take_block(key_all, position, block_size, 1), head_count)
        value_rows = split_heads(take_block(value_all, position, block_size, 1), head_count)
        scores = masked_scores(queries, key_rows, position * block_size, slot_lengths)
        softmax_rows = jnp.exp(scores - logsum[..., None])
        d_probs = jnp.einsum(
            "sqhd,skhd->shqk", d_context, value_rows, preferred_element_type=jnp.float32
        )
        return (prob_delta + jnp.sum(softmax_rows * d_probs, -1), None)

    prob_delta, _ = lax.scan(
        prob_step_fn, jnp.zeros(logsum.shape, jnp.float32), jnp.arange(block_count)
    )
    return prob_delta


def key_side(
    queries, d_context, key_all, value_all, slot_lengths, logsum, prob_delta, block_size, head_count
):
    block_count = key_all.shape[1] // block_size

    def key_step_fn(d_query, position):
        key_rows = split_heads(take_block(key_all, position, block_size, 1), head_count)
        value_rows = split_heads(take_block(value_all, position, block_size, 1), head_count)
        scores = masked_scores(queries, key_rows, position * block_size, slot_lengths)
        softmax_rows = jnp.exp(scores - logsum[..., None])
        d_probs = jnp.einsum(
            "sqhd,skhd->shqk", d_context, value_rows, preferred_element_type=jnp.float32
        )
        d_scores = (softmax_rows * (d_probs - prob_delta[..., None])).astype(jnp.bfloat16)
        d_query = d_query + jnp.einsum(
            "shqk,skhd->sqhd", d_scores, key_rows, preferred_element_type=jnp.float32
        )
        d_key_rows = jnp.einsum(
            "shqk,sqhd->skhd", d_scores, queries, preferred_element_type=jnp.float32
        )
        d_value_rows = jnp.einsum(
            "shqk,sqhd->skhd",
            softmax_rows.astype(jnp.bfloat16),
            d_context,
            preferred_element_type=jnp.float32,
        )
        return (d_query, (d_key_rows, d_value_rows))

    return lax.scan(key_step_fn, jnp.zeros(queries.shape, jnp.float32), jnp.arange(block_count))


def flip_pairs(mask):
    return [((q * 4 + z), ((q ^ mask) * 4 + z)) for q in range(8) for z in range(4)]


def turn_pairs(step):
    return [((q * 4 + z), (q * 4 + (z + step) % 4)) for q in range(8) for z in range(4)]


CORE, X_AXIS, Y_AXIS = 1, 2, 4


def flip(value, mask):
    return lax.ppermute(value, ALL_AXES, flip_pairs(mask))


def turn(value, step):
    return lax.ppermute(value, ALL_AXES, turn_pairs(step))


def places():
    q = lax.axis_index(SEQ)
    return q & 1, (q >> 1) & 1, q >> 2, lax.axis_index(SLOT)


def merge(own, other, bit, axis):
    first = jnp.where(bit == 0, own, other)
    second = jnp.where(bit == 0, other, own)
    return jnp.stack([first, second], axis)


def plane_one(a, b):
    _, _, _, _ = places()
    a1, b1 = flip(a, X_AXIS), flip(b, Y_AXIS)
    return a1, b1


def plane_two(a, b, got):
    _, x, y, _ = places()
    a, b = merge(a, got[0], x, 0), merge(b, got[1], y, 0)
    return a, b, flip(a, Y_AXIS), flip(b, X_AXIS)


def plane_core(a, b, a2, b2):
    core, x, y, _ = places()
    a, b = merge(a, a2, y, 0), merge(b, b2, x, 1)
    a3, b3 = flip(a, CORE), flip(b, CORE)
    return merge(a, a3, core, 2), merge(b, b3, core, 2)


def plane_rows(a, b, a2, b2):
    core, x, y, _ = places()
    a, b = merge(a, a2, y, 0), merge(b, b2, x, 1)
    rows, columns = a.shape[-2:]
    a, b = a.reshape(4, 2, rows, columns), b.reshape(4, 2, rows, columns)
    a3, b3 = flip(a, CORE), flip(b, CORE)
    own, got = jnp.concatenate([a, b], 1), jnp.concatenate([a3, b3], 1)
    whole = merge(own, got, core, 1)
    return as_matrix(whole)


def after(value, ready):
    return lax.optimization_barrier((value, ready))[0]


def line_turns(shard):
    return tuple(turn(shard, step) for step in (1, 2, 3))


def line_blocks(shard, got):
    ring = [shard, got[2], got[1], got[0]]
    start = (4 - places()[3]) % 4
    return lax.dynamic_slice_in_dim(jnp.stack(ring + ring[:3]), start, 4, 0)


def as_matrix(parts):
    return parts.reshape(32 * parts.shape[-2], parts.shape[-1])


def pick(value, index, axis):
    return lax.dynamic_index_in_dim(value, index, axis, keepdims=False)


def choose(value, bit, axis):
    first = lax.index_in_dim(value, 0, axis, keepdims=False)
    return jnp.where(bit == 0, first, lax.index_in_dim(value, 1, axis, keepdims=False))


def add_low(left, right):
    return (left.astype(jnp.float32) + right.astype(jnp.float32)).astype(jnp.bfloat16)


def fold(value, bit, mask, axis):
    return add_low(choose(value, bit, axis), flip(choose(value, 1 - bit, axis), mask))


def core_fold(parts):
    core = places()[0]
    return tuple(fold(part, core, CORE, 2) for part in parts)


def core_fold_split(keep, send):
    return add_low(keep, flip(send, CORE))


def plane_fold(a, b):
    _, x, y, _ = places()
    a, b = fold(a, y, Y_AXIS, 0), fold(b, x, X_AXIS, 1)
    return fold(a, x, X_AXIS, 0), fold(b, y, Y_AXIS, 0)


def scatter_line(part):
    z = places()[3]
    return [pick(part, z, 0)] + [turn(pick(part, (z + step) % 4, 0), step) for step in (1, 2, 3)]


def line_total(terms):
    return sum(term.astype(jnp.float32) for term in terms)


def place_blocks(part):
    return part.reshape(2, 2, 2, 4, part.shape[0] // 32, part.shape[1])


def body(
    tokens,
    qkv_weight,
    query_bias,
    value_bias,
    out_weight,
    out_bias,
    norm1_gain,
    norm1_shift,
    up_weight,
    up_bias,
    down_weight,
    down_bias,
    norm2_gain,
    norm2_shift,
    slot_lengths,
    out_cotangent,
):
    slot_count, row_count, model_width = tokens.shape
    head_count = HEADS
    flat_rows = tokens.reshape(slot_count * row_count, model_width)
    attn_set = (
        lax.all_gather(qkv_weight, ALL_AXES, axis=0, tiled=True),
        lax.all_gather(out_weight, ALL_AXES, axis=0, tiled=True),
        lax.all_gather(query_bias, ALL_AXES, axis=0, tiled=True),
        lax.all_gather(value_bias, ALL_AXES, axis=0, tiled=True),
        lax.all_gather(out_bias, ALL_AXES, axis=0, tiled=True),
        lax.all_gather(norm1_gain, ALL_AXES, axis=0, tiled=True),
        lax.all_gather(norm1_shift, ALL_AXES, axis=0, tiled=True),
    )
    qkv_full, out_full, query_shift, value_shift, out_shift, gain_one, shift_one = attn_set
    mixed = jnp.dot(flat_rows, qkv_full, preferred_element_type=jnp.float32)
    queries = ((mixed[:, :model_width] + query_shift.astype(jnp.float32)) * 0.125).astype(
        jnp.bfloat16
    )
    queries = split_heads(queries.reshape(slot_count, row_count, model_width), head_count)
    keys_own = (
        mixed[:, model_width : 2 * model_width]
        .astype(jnp.bfloat16)
        .reshape(slot_count, row_count, model_width)
    )
    values_own = (
        (mixed[:, 2 * model_width :] + value_shift.astype(jnp.float32))
        .astype(jnp.bfloat16)
        .reshape(slot_count, row_count, model_width)
    )
    key_all, value_all = (
        lax.all_gather(keys_own, SEQ, axis=1, tiled=True),
        lax.all_gather(values_own, SEQ, axis=1, tiled=True),
    )
    length_all = key_all.shape[1]
    block_size = min(512, length_all)
    logsum = log_totals(queries, key_all, slot_lengths, block_size, head_count)
    context = attend(
        queries, key_all, value_all, slot_lengths, logsum, block_size, head_count
    ).astype(jnp.bfloat16)
    context_flat = context.reshape(slot_count * row_count, model_width)
    attn_out = jnp.dot(
        context_flat, out_full, preferred_element_type=jnp.float32
    ) + out_shift.astype(jnp.float32)
    resid_one = flat_rows.astype(jnp.float32) + attn_out
    hidden_one = norm_rows(resid_one, gain_one.astype(jnp.float32), shift_one.astype(jnp.float32))
    hidden_low = hidden_one.astype(jnp.bfloat16)
    ffn_set = (
        lax.all_gather(up_weight, ALL_AXES, axis=0, tiled=True),
        lax.all_gather(down_weight, ALL_AXES, axis=0, tiled=True),
        lax.all_gather(up_bias, ALL_AXES, axis=0, tiled=True),
        lax.all_gather(down_bias, ALL_AXES, axis=0, tiled=True),
        lax.all_gather(norm2_gain, ALL_AXES, axis=0, tiled=True),
        lax.all_gather(norm2_shift, ALL_AXES, axis=0, tiled=True),
    )
    up_full, down_full, up_shift, down_shift, gain_two, shift_two = ffn_set
    inner_act = jnp.dot(hidden_low, up_full, preferred_element_type=jnp.float32) + up_shift.astype(
        jnp.float32
    )
    activated = gelu_exact(inner_act).astype(jnp.bfloat16)
    ffn_out = jnp.dot(activated, down_full, preferred_element_type=jnp.float32) + down_shift.astype(
        jnp.float32
    )
    resid_two = hidden_one + ffn_out
    layer_out = norm_rows(resid_two, gain_two.astype(jnp.float32), shift_two.astype(jnp.float32))
    layer_out = layer_out.astype(jnp.bfloat16).reshape(slot_count, row_count, model_width)
    qkv_back, out_back, _, _, _, gain_one_back, shift_one_back = (
        lax.all_gather(qkv_weight, ALL_AXES, axis=0, tiled=True),
        lax.all_gather(out_weight, ALL_AXES, axis=0, tiled=True),
        lax.all_gather(query_bias, ALL_AXES, axis=0, tiled=True),
        lax.all_gather(value_bias, ALL_AXES, axis=0, tiled=True),
        lax.all_gather(out_bias, ALL_AXES, axis=0, tiled=True),
        lax.all_gather(norm1_gain, ALL_AXES, axis=0, tiled=True),
        lax.all_gather(norm1_shift, ALL_AXES, axis=0, tiled=True),
    )
    up_back, down_back, _, _, gain_two_back, shift_two_back = (
        lax.all_gather(up_weight, ALL_AXES, axis=0, tiled=True),
        lax.all_gather(down_weight, ALL_AXES, axis=0, tiled=True),
        lax.all_gather(up_bias, ALL_AXES, axis=0, tiled=True),
        lax.all_gather(down_bias, ALL_AXES, axis=0, tiled=True),
        lax.all_gather(norm2_gain, ALL_AXES, axis=0, tiled=True),
        lax.all_gather(norm2_shift, ALL_AXES, axis=0, tiled=True),
    )
    positions = lax.axis_index(SEQ) * row_count + jnp.arange(row_count)
    live_rows = (positions[None, :] < slot_lengths[:, None]).astype(jnp.float32)
    cotangent = (out_cotangent.astype(jnp.float32) * live_rows[:, :, None]).reshape(
        slot_count * row_count, model_width
    )
    _, norm_back_two = jax.vjp(
        norm_rows, resid_two, gain_two_back.astype(jnp.float32), shift_two_back.astype(jnp.float32)
    )
    d_resid_two, d_gain_two, d_shift_two = norm_back_two(cotangent)
    d_ffn = d_resid_two.astype(jnp.bfloat16)
    d_down = contract_rows(activated, d_ffn)
    d_down_shift = jnp.sum(d_ffn.astype(jnp.float32), 0)
    d_activated = contract_last(d_ffn, down_back)
    _, gelu_back = jax.vjp(gelu_exact, inner_act)
    d_inner = gelu_back(d_activated)[0].astype(jnp.bfloat16)
    d_up = contract_rows(hidden_low, d_inner)
    d_up_shift = jnp.sum(d_inner.astype(jnp.float32), 0)
    d_hidden = contract_last(d_inner, up_back) + d_resid_two
    _, norm_back_one = jax.vjp(
        norm_rows, resid_one, gain_one_back.astype(jnp.float32), shift_one_back.astype(jnp.float32)
    )
    d_resid_one, d_gain_one, d_shift_one = norm_back_one(d_hidden)
    d_attn = d_resid_one.astype(jnp.bfloat16)
    d_out = contract_rows(context_flat, d_attn)
    d_out_shift = jnp.sum(d_attn.astype(jnp.float32), 0)
    d_context = contract_last(d_attn, out_back).astype(jnp.bfloat16)
    d_context = split_heads(d_context.reshape(slot_count, row_count, model_width), head_count)
    prob_delta = prob_grad_totals(
        queries, d_context, key_all, value_all, slot_lengths, logsum, block_size, head_count
    )
    d_query, key_parts = key_side(
        queries,
        d_context,
        key_all,
        value_all,
        slot_lengths,
        logsum,
        prob_delta,
        block_size,
        head_count,
    )
    d_key_part = jnp.moveaxis(key_parts[0], 0, 1).reshape(slot_count, length_all, model_width)
    d_value_part = jnp.moveaxis(key_parts[1], 0, 1).reshape(slot_count, length_all, model_width)
    d_key_sum, d_value_sum = (
        lax.psum_scatter(
            d_key_part.astype(jnp.bfloat16), SEQ, scatter_dimension=1, tiled=True
        ).astype(jnp.float32),
        lax.psum_scatter(
            d_value_part.astype(jnp.bfloat16), SEQ, scatter_dimension=1, tiled=True
        ).astype(jnp.float32),
    )
    d_query_pre = d_query.astype(jnp.bfloat16).reshape(
        slot_count * row_count, model_width
    ) * jnp.asarray(0.125, jnp.bfloat16)
    d_key_low = d_key_sum.astype(jnp.bfloat16).reshape(slot_count * row_count, model_width)
    d_value_low = d_value_sum.astype(jnp.bfloat16).reshape(slot_count * row_count, model_width)
    d_mixed = jnp.concatenate([d_query_pre, d_key_low, d_value_low], 1)
    d_qkv = contract_rows(flat_rows, d_mixed)
    d_query_shift = jnp.sum(d_query_pre.astype(jnp.float32), 0)
    d_value_shift = jnp.sum(d_value_low.astype(jnp.float32), 0)
    tokens_grad = (
        (d_resid_one + contract_last(d_mixed, qkv_back))
        .astype(jnp.bfloat16)
        .reshape(slot_count, row_count, model_width)
    )
    attn_sums = (
        lax.psum_scatter(d_qkv, ALL_AXES, scatter_dimension=0, tiled=True),
        lax.psum_scatter(d_out, ALL_AXES, scatter_dimension=0, tiled=True),
        lax.psum_scatter(d_query_shift, ALL_AXES, scatter_dimension=0, tiled=True),
        lax.psum_scatter(d_value_shift, ALL_AXES, scatter_dimension=0, tiled=True),
        lax.psum_scatter(d_out_shift, ALL_AXES, scatter_dimension=0, tiled=True),
        lax.psum_scatter(d_gain_one, ALL_AXES, scatter_dimension=0, tiled=True),
        lax.psum_scatter(d_shift_one, ALL_AXES, scatter_dimension=0, tiled=True),
    )
    ffn_sums = (
        lax.psum_scatter(d_up, ALL_AXES, scatter_dimension=0, tiled=True),
        lax.psum_scatter(d_down, ALL_AXES, scatter_dimension=0, tiled=True),
        lax.psum_scatter(d_up_shift, ALL_AXES, scatter_dimension=0, tiled=True),
        lax.psum_scatter(d_down_shift, ALL_AXES, scatter_dimension=0, tiled=True),
        lax.psum_scatter(d_gain_two, ALL_AXES, scatter_dimension=0, tiled=True),
        lax.psum_scatter(d_shift_two, ALL_AXES, scatter_dimension=0, tiled=True),
    )
    return (
        layer_out,
        tokens_grad,
        attn_sums[0],
        attn_sums[2],
        attn_sums[3],
        attn_sums[1],
        attn_sums[4],
        attn_sums[5],
        attn_sums[6],
        ffn_sums[0],
        ffn_sums[2],
        ffn_sums[1],
        ffn_sums[3],
        ffn_sums[4],
        ffn_sums[5],
    )


def body_fast(
    tokens,
    qkv_weight,
    query_bias,
    value_bias,
    out_weight,
    out_bias,
    norm1_gain,
    norm1_shift,
    up_weight,
    up_bias,
    down_weight,
    down_bias,
    norm2_gain,
    norm2_shift,
    slot_lengths,
    out_cotangent,
):
    slot_count, row_count, model_width = tokens.shape
    part = qkv_weight.shape[0]
    inner_part = up_bias.shape[0]
    flat_rows = tokens.reshape(slot_count * row_count, model_width)
    small = jnp.stack(
        [
            query_bias,
            value_bias,
            out_bias,
            norm1_gain,
            norm1_shift,
            down_bias,
            norm2_gain,
            norm2_shift,
        ]
    )
    small = jnp.concatenate(
        [
            jnp.pad(small, ((0, 0), (0, 256 - part))),
            jnp.pad(up_bias[None], ((0, part - 9), (0, 256 - inner_part))),
        ]
    )
    attn_shard = jnp.concatenate([qkv_weight, out_weight, small], 1)
    attn_line = line_blocks(attn_shard, line_turns(attn_shard))
    half = attn_line.shape[-1] // 2
    rest = 3 * model_width - half
    attn_halves = attn_line[..., :half], attn_line[..., half:]
    stack_count = down_weight.shape[0] // part
    ffn_shard = jnp.concatenate(
        [up_weight] + [down_weight[k * part : (k + 1) * part] for k in range(stack_count)], 1
    )
    ffn_shard = after(ffn_shard, attn_line)
    ffn_got = line_turns(ffn_shard)
    attn_halves = plane_two(*attn_halves, plane_one(*attn_halves))
    ffn_line = line_blocks(ffn_shard, ffn_got)
    ff_width = up_weight.shape[1]
    down_line = [
        ffn_line[..., ff_width + k * model_width : ff_width + (k + 1) * model_width]
        for k in range(stack_count)
    ]
    down_line = jnp.concatenate(down_line, 1)
    up_halves = ffn_line[:2, :, :ff_width], ffn_line[2:, :, :ff_width]
    down_halves = down_line[:2], down_line[2:]
    up_got = plane_one(*up_halves)
    down_got = plane_one(*down_halves)
    attn_a, attn_b = (as_matrix(parts) for parts in plane_core(*attn_halves))
    out_full = attn_b[:, rest : rest + model_width]
    small_full = attn_b[:, rest + model_width : rest + model_width + 128]
    small_full = small_full.reshape(32, part, 128).astype(jnp.float32)
    vectors = jnp.moveaxis(small_full[:, :8, :part], 1, 0).reshape(8, model_width)
    up_shift = small_full[:, 8, :inner_part].reshape(1, 32 * inner_part)
    vectors, up_shift = lax.optimization_barrier((vectors, up_shift))
    query_shift, value_shift, out_shift, gain_one, shift_one, down_shift, gain_two, shift_two = (
        vectors[position : position + 1] for position in range(8)
    )
    mixed_a = jnp.dot(flat_rows, attn_a, preferred_element_type=jnp.float32)
    mixed_b = jnp.dot(flat_rows, attn_b[:, :rest], preferred_element_type=jnp.float32)
    mixed = jnp.concatenate([mixed_a, mixed_b], 1)
    queries = ((mixed[:, :model_width] + query_shift) * 0.125).astype(jnp.bfloat16)
    queries = queries.reshape(slot_count, row_count, model_width)
    keys_own = (
        mixed[:, model_width : 2 * model_width]
        .astype(jnp.bfloat16)
        .reshape(slot_count, row_count, model_width)
    )
    values_own = (
        (mixed[:, 2 * model_width :] + value_shift)
        .astype(jnp.bfloat16)
        .reshape(slot_count, row_count, model_width)
    )

    places_shape = (8, slot_count, row_count, model_width)
    kept = plane_two(keys_own, values_own, plane_one(keys_own, values_own))
    up_full = plane_rows(*plane_two(*up_halves, up_got))
    down_full = plane_rows(*plane_two(*down_halves, down_got))
    key_all, value_all = (part.reshape(places_shape) for part in plane_core(*kept))
    context, logsum = attention_call(
        attend_kernel, slot_lengths, (queries, key_all, value_all), False
    )
    context_flat = context.reshape(slot_count * row_count, model_width)
    attn_out = jnp.dot(context_flat, out_full, preferred_element_type=jnp.float32) + out_shift
    resid_one = flat_rows.astype(jnp.float32) + attn_out
    hidden_one = norm_rows(resid_one, gain_one, shift_one)
    hidden_low = hidden_one.astype(jnp.bfloat16)
    inner_act = jnp.dot(hidden_low, up_full, preferred_element_type=jnp.float32) + up_shift
    share = 0.5 + 0.5 * lax.erf(inner_act * 0.5**0.5)
    bell = jnp.exp(-0.5 * inner_act * inner_act) * (0.5 / jnp.pi) ** 0.5
    activated, slope = lax.optimization_barrier(
        ((inner_act * share).astype(jnp.bfloat16), share + inner_act * bell)
    )
    ffn_out = jnp.dot(activated, down_full, preferred_element_type=jnp.float32) + down_shift
    resid_two = hidden_one + ffn_out
    layer_out = norm_rows(resid_two, gain_two, shift_two)
    layer_out = layer_out.astype(jnp.bfloat16).reshape(slot_count, row_count, model_width)
    positions = lax.axis_index(SEQ) * row_count + jnp.arange(row_count)
    live_rows = (positions[None, :] < slot_lengths[:, None]).astype(jnp.float32)
    cotangent = (out_cotangent.astype(jnp.float32) * live_rows[:, :, None]).reshape(
        slot_count * row_count, model_width
    )
    _, norm_back_two = jax.vjp(norm_rows, resid_two, gain_two, shift_two)
    d_resid_two, d_gain_two, d_shift_two = norm_back_two(cotangent)
    d_ffn = d_resid_two.astype(jnp.bfloat16)
    d_down = contract_rows(activated, d_ffn).astype(jnp.bfloat16)
    d_down_shift = jnp.sum(d_ffn.astype(jnp.float32), 0)
    d_activated = contract_last(d_ffn, down_full)
    d_inner = (d_activated * slope).astype(jnp.bfloat16)
    d_up = contract_rows(hidden_low, d_inner).astype(jnp.bfloat16)
    d_up, d_down = core_fold((place_blocks(d_up), place_blocks(d_down)))
    d_up, d_down = plane_fold(d_up, d_down)
    d_down = d_down.reshape(4, stack_count, part, model_width)
    ffn_terms = scatter_line(
        jnp.concatenate([d_up] + [d_down[:, k] for k in range(stack_count)], 2)
    )
    d_up_shift = jnp.sum(d_inner.astype(jnp.float32), 0)
    d_hidden = contract_last(d_inner, up_full) + d_resid_two
    _, norm_back_one = jax.vjp(norm_rows, resid_one, gain_one, shift_one)
    d_resid_one, d_gain_one, d_shift_one = norm_back_one(d_hidden)
    d_attn = d_resid_one.astype(jnp.bfloat16)
    d_out_shift = jnp.sum(d_attn.astype(jnp.float32), 0)
    d_context = contract_last(d_attn, out_full).astype(jnp.bfloat16)
    tokens_across, context_across = lax.optimization_barrier((flat_rows.T, context_flat.T))
    d_query, *key_parts = attention_call(
        attend_back_kernel,
        jnp.append(slot_lengths, places()[0]),
        (
            queries,
            d_context.reshape(slot_count, row_count, model_width),
            key_all,
            value_all,
            logsum,
        ),
        True,
    )
    half_shape = (2, 2) + places_shape[1:]
    d_key_low, d_value_low = plane_fold(
        core_fold_split(key_parts[0], key_parts[1]).reshape(half_shape),
        core_fold_split(key_parts[2], key_parts[3]).reshape(half_shape),
    )
    d_query_pre = d_query.reshape(slot_count * row_count, model_width)
    d_key_low = d_key_low.reshape(slot_count * row_count, model_width)
    d_value_low = d_value_low.reshape(slot_count * row_count, model_width)
    d_mixed = jnp.concatenate([d_query_pre, d_key_low, d_value_low], 1)
    d_query_shift = jnp.sum(d_query_pre.astype(jnp.float32), 0)
    d_value_shift = jnp.sum(d_value_low.astype(jnp.float32), 0)
    tokens_grad = (
        (
            d_resid_one
            + contract_last(d_mixed[:, :half], attn_a)
            + contract_last(d_mixed[:, half:], attn_b[:, :rest])
        )
        .astype(jnp.bfloat16)
        .reshape(slot_count, row_count, model_width)
    )
    row_places = lax.broadcasted_iota(jnp.int32, (8, model_width), 0)
    small_grads = jnp.zeros((8, model_width), jnp.float32)
    for position, grad in enumerate(
        (
            d_query_shift,
            d_value_shift,
            d_out_shift,
            d_gain_one,
            d_shift_one,
            d_down_shift,
            d_gain_two,
            d_shift_two,
        )
    ):
        small_grads = jnp.where(
            row_places == position, grad.reshape(1, model_width), small_grads
        )
    small_grads = lax.optimization_barrier(small_grads.astype(jnp.bfloat16))
    small_grads = jnp.moveaxis(small_grads.reshape(8, 32, part), 0, 1)
    inner_grads = d_up_shift.astype(jnp.bfloat16).reshape(32, 1, inner_part)
    small_grads = jnp.concatenate(
        [
            jnp.pad(small_grads, ((0, 0), (0, 0), (0, 256 - part))),
            jnp.pad(inner_grads, ((0, 0), (0, part - 9), (0, 256 - inner_part))),
        ],
        1,
    ).reshape(32 * part, 256)
    keep, send = attn_products(
        tokens_across,
        d_query_pre,
        d_key_low,
        d_value_low,
        context_across,
        d_attn,
        small_grads,
    )
    grads = core_fold_split(keep, send).reshape(2, 2, 4, part, keep.shape[-1])
    grads = jnp.concatenate(plane_fold(grads[..., :half], grads[..., half:]), 2)
    attn_terms = scatter_line(grads)
    ffn_total = line_total(ffn_terms)
    attn_total = line_total(attn_terms)
    d_up = ffn_total[:, :ff_width]
    d_down = jnp.concatenate(
        [
            ffn_total[:, ff_width + k * model_width : ff_width + (k + 1) * model_width]
            for k in range(stack_count)
        ]
    )
    own = attn_total[:, 4 * model_width : 4 * model_width + 128]
    vectors = [own[position, :part] for position in range(8)]
    return (
        layer_out,
        tokens_grad,
        attn_total[:, : 3 * model_width],
        vectors[0],
        vectors[1],
        attn_total[:, 3 * model_width : 4 * model_width],
        vectors[2],
        vectors[3],
        vectors[4],
        d_up,
        own[8, :inner_part],
        d_down,
        vectors[5],
        vectors[6],
        vectors[7],
    )


def contract_first(left, right):
    return lax.dot_general(
        left, right, (((0,), (0,)), ((), ())), preferred_element_type=jnp.float32
    )


def low_lanes(shape):
    return lax.broadcasted_iota(jnp.int32, shape, 1) < shape[1] // 2


def stack_heads(value):
    zero, low_half = jnp.zeros_like(value), low_lanes(value.shape)
    return jnp.concatenate(
        [jnp.where(low_half, value, zero), jnp.where(low_half, zero, value)], 0
    )


def join_heads(stacked):
    rows = stacked.shape[0] // 2
    return jnp.where(low_lanes((rows, stacked.shape[1])), stacked[:rows], stacked[rows:])


def length_bias(length, key_count):
    places = lax.broadcasted_iota(jnp.int32, (1, key_count), 1)
    return jnp.where(places < length, 0.0, NEG_FILL)


def pair_rows(ref, span):
    return ref[:, 0, :, span].reshape(-1, 128)


def attend_kernel(lengths, query_ref, key_ref, value_ref, context_ref, logsum_ref):
    bias = length_bias(lengths[pl.program_id(0)], key_ref.shape[0] * key_ref.shape[2])
    for pair in range(query_ref.shape[2] // 128):
        span = slice(pair * 128, (pair + 1) * 128)
        keys, values = pair_rows(key_ref, span), pair_rows(value_ref, span)
        scores = contract_last(stack_heads(query_ref[0, :, span]), keys) + bias
        row_max = jnp.max(scores, 1, keepdims=True)
        weights = jnp.exp(scores - row_max)
        total = jnp.sum(weights, 1, keepdims=True)
        logsum_ref[0, pair] = jnp.broadcast_to(
            row_max + jnp.log(total), logsum_ref.shape[2:]
        )
        summed = jnp.dot(
            weights.astype(jnp.bfloat16), values, preferred_element_type=jnp.float32
        )
        context_ref[0, :, span] = join_heads(summed * (1.0 / total)).astype(jnp.bfloat16)


def attend_back_kernel(
    lengths,
    query_ref,
    d_context_ref,
    key_ref,
    value_ref,
    logsum_ref,
    d_query_ref,
    d_key_keep,
    d_key_send,
    d_value_keep,
    d_value_send,
):
    core = lengths[pl.num_programs(0)]
    place_count, rows = key_ref.shape[0], key_ref.shape[2]
    bias = length_bias(lengths[pl.program_id(0)], place_count * rows)
    for pair in range(query_ref.shape[2] // 128):
        span = slice(pair * 128, (pair + 1) * 128)
        keys, values = pair_rows(key_ref, span), pair_rows(value_ref, span)
        query = stack_heads(query_ref[0, :, span])
        d_context = stack_heads(d_context_ref[0, :, span])
        scores = contract_last(query, keys) + bias
        probs = jnp.exp(scores - logsum_ref[0, pair][:, 0:1])
        d_probs = contract_last(d_context, values)
        prob_delta = jnp.sum(probs * d_probs, 1, keepdims=True)
        d_scores = (probs * (d_probs - prob_delta)).astype(jnp.bfloat16)
        d_query = join_heads(jnp.dot(d_scores, keys, preferred_element_type=jnp.float32))
        d_query_ref[0, :, span] = d_query.astype(jnp.bfloat16) * jnp.asarray(0.125, jnp.bfloat16)
        for total, keep_ref, send_ref in (
            (contract_first(d_scores, query), d_key_keep, d_key_send),
            (contract_first(probs.astype(jnp.bfloat16), d_context), d_value_keep, d_value_send),
        ):
            total = total.astype(jnp.bfloat16).reshape(place_count // 2, 2, rows, 128)
            keep_ref[:, 0, :, span] = jnp.where(core == 0, total[:, 0], total[:, 1])
            send_ref[:, 0, :, span] = jnp.where(core == 0, total[:, 1], total[:, 0])


def attention_call(kernel, slot_lengths, operands, backward):
    queries, keys = operands[0], operands[2 if backward else 1]
    slot_count, row_count, width = queries.shape
    place_count, lanes = keys.shape[0], 256
    pairs = width // lanes
    row_spec = pl.BlockSpec((1, row_count, lanes), lambda s, p, _: (s, 0, p))
    key_spec = pl.BlockSpec((place_count, 1, row_count, lanes), lambda s, p, _: (0, s, 0, p))
    stat_spec = pl.BlockSpec((1, 2, 2 * row_count, 128), lambda s, p, _: (s, p, 0, 0))
    low_rows = jax.ShapeDtypeStruct(queries.shape, jnp.bfloat16)
    half_keys = jax.ShapeDtypeStruct((place_count // 2,) + keys.shape[1:], jnp.bfloat16)
    half_spec = pl.BlockSpec((place_count // 2, 1, row_count, lanes), lambda s, p, _: (0, s, 0, p))
    stats = jax.ShapeDtypeStruct((slot_count, 2 * pairs, 2 * row_count, 128), jnp.float32)
    products = 5 if backward else 2
    scores = 4 * slot_count * pairs * row_count * place_count * row_count
    return pl.pallas_call(
        kernel,
        out_shape=(low_rows,) + (half_keys,) * 4 if backward else (low_rows, stats),
        grid_spec=pltpu.PrefetchScalarGridSpec(
            num_scalar_prefetch=1,
            grid=(slot_count, pairs),
            in_specs=(
                [row_spec, row_spec, key_spec, key_spec, stat_spec]
                if backward
                else [row_spec, key_spec, key_spec]
            ),
            out_specs=[row_spec] + [half_spec] * 4 if backward else [row_spec, stat_spec],
        ),
        cost_estimate=pl.CostEstimate(
            flops=products * 4 * scores * lanes,
            bytes_accessed=products * 2 * place_count * slot_count * row_count * width,
            transcendentals=scores,
        ),
    )(slot_lengths, *operands)


def products_kernel(core_ref, *refs):
    tokens_ref, query_ref, key_ref, value_ref, context_ref, attn_ref, small_ref, keep, send = refs
    core = core_ref[0]
    width = small_ref.shape[0]
    half = keep.shape[-1]
    columns = []
    for left, right in (
        (tokens_ref, query_ref),
        (tokens_ref, key_ref),
        (tokens_ref, value_ref),
        (context_ref, attn_ref),
        (None, small_ref),
    ):
        columns += [(left, right, start) for start in range(0, right.shape[1], 128)]
    per_step = half // 128

    def run(mine):
        place = 0
        while place < len(mine):
            left, right, start = mine[place]
            wide = place + 1 < len(mine) and mine[place + 1][1] is right
            lanes = 256 if wide else 128
            block = right[:, start : start + lanes]
            if left is not None:
                block = jnp.dot(left[...], block, preferred_element_type=jnp.float32)
                block = block.astype(jnp.bfloat16)
            block = block.reshape(4, 2, width // 8, lanes)
            span = slice(place * 128, place * 128 + lanes)
            keep[:, :, span] = jnp.where(core == 0, block[:, 0], block[:, 1])
            send[:, :, span] = jnp.where(core == 0, block[:, 1], block[:, 0])
            place += lanes // 128

    for step in range(2):
        pl.when(pl.program_id(0) == step)(
            lambda step=step: run(columns[step * per_step : (step + 1) * per_step])
        )


def attn_products(tokens, d_query, d_key, d_value, context, d_attn, small):
    width, rows = tokens.shape
    operands = (tokens, d_query, d_key, d_value, context, d_attn, small)
    total = 4 * width + small.shape[1]
    out_shape = jax.ShapeDtypeStruct((4, width // 8, total), jnp.bfloat16)
    out_spec = pl.BlockSpec((4, width // 8, total // 2), lambda i, _: (0, 0, i))
    return pl.pallas_call(
        products_kernel,
        out_shape=(out_shape, out_shape),
        grid_spec=pltpu.PrefetchScalarGridSpec(
            num_scalar_prefetch=1,
            grid=(2,),
            in_specs=[pl.BlockSpec(operand.shape, lambda i, _: (0, 0)) for operand in operands],
            out_specs=[out_spec, out_spec],
        ),
        cost_estimate=pl.CostEstimate(
            flops=8 * rows * width * width, bytes_accessed=16 * width * width, transcendentals=0
        ),
    )(places()[0].reshape(1), *operands)


def solution(mesh):
    fast = mesh.shape[SEQ] == 8 and mesh.shape[SLOT] == 4
    return jax.shard_map(
        body_fast if fast else body,
        mesh=mesh,
        in_specs=(
            P(SLOT, SEQ, None),
            P(ALL_AXES, None),
            P(ALL_AXES),
            P(ALL_AXES),
            P(ALL_AXES, None),
            P(ALL_AXES),
            P(ALL_AXES),
            P(ALL_AXES),
            P(ALL_AXES, None),
            P(ALL_AXES),
            P(ALL_AXES, None),
            P(ALL_AXES),
            P(ALL_AXES),
            P(ALL_AXES),
            P(SLOT),
            P(SLOT, SEQ, None),
        ),
        out_specs=(
            P(SLOT, SEQ, None),
            P(SLOT, SEQ, None),
            P(ALL_AXES, None),
            P(ALL_AXES),
            P(ALL_AXES),
            P(ALL_AXES, None),
            P(ALL_AXES),
            P(ALL_AXES),
            P(ALL_AXES),
            P(ALL_AXES, None),
            P(ALL_AXES),
            P(ALL_AXES, None),
            P(ALL_AXES),
            P(ALL_AXES),
            P(ALL_AXES),
        ),
        check_vma=False,
    )
```
